32 devices in a mesh: heads: 2 (over x), wide: 16 (over z, y, core).
Axes of the slice: x: 2, y: 2, z: 4, core: 2. Of those that a mesh axis runs over, the one named last changes fastest.
Arguments:
- tokens: bfloat16 [32, 1024, 768], P(('heads', 'wide')), may hold values from -36 to 36
- cotangent: bfloat16 [32, 1024, 768], P(('heads', 'wide')), may hold values from -11 to 11
- lengths: int32 [32], P(('heads', 'wide')), may hold values from 196 to 1024, as said below
- step_count: int32 [1], replicated, may hold values from 2 to 20
- attend_weights: float32 [3, 768, 768], P(None, 'wide', 'heads'), may hold values from -0.21875 to 0.21875
- output_weights: float32 [768, 768], P('heads', 'wide'), may hold values from -7 to 7
- expand_weights: float32 [768, 3072], P('wide', 'heads'), may hold values from -0.21875 to 0.21875
- reduce_weights: float32 [3072, 768], P('heads', 'wide'), may hold values from -1 to 1
- expand_bias: float32 [3072], P(('heads', 'wide')), may hold values from -3 to 3
- norm_gains: float32 [3, 768], P(None, ('heads', 'wide')), may hold values from 0.1 to 1.9
- first_attend: float32 [3, 768, 768], P(None, 'wide', 'heads'), may hold values from -1.25 to 1.25
- first_output: float32 [768, 768], P('heads', 'wide'), may hold values from -0.25 to 0.25
- first_expand: float32 [768, 3072], P('wide', 'heads'), may hold values from -0.875 to 0.875
- first_reduce: float32 [3072, 768], P('heads', 'wide'), may hold values from -2 to 2
- first_bias: float32 [3072], P(('heads', 'wide')), may hold values from -0.875 to 0.875
- first_gains: float32 [3, 768], P(None, ('heads', 'wide')), may hold values from -3 to 3
- second_attend: float32 [3, 768, 768], P(None, 'wide', 'heads'), may hold values from 0.1048576 to 1.703936
- second_output: float32 [768, 768], P('heads', 'wide'), may hold values from 0.0032768 to 0.0524288
- second_expand: float32 [768, 3072], P('wide', 'heads'), may hold values from 0.0458752 to 0.753664
- second_reduce: float32 [3072, 768], P('heads', 'wide'), may hold values from 0.2195456 to 3.60448
- second_bias: float32 [3072], P(('heads', 'wide')), may hold values from 0.0458752 to 0.753664
- second_gains: float32 [3, 768], P(None, ('heads', 'wide')), may hold values from 0.524288 to 8.192
- average_attend: float32 [3, 768, 768], P(None, 'wide', 'heads'), may hold values from -0.21875 to 0.21875
- average_output: float32 [768, 768], P('heads', 'wide'), may hold values from -1.75 to 1.75
- average_expand: float32 [768, 3072], P('wide', 'heads'), may hold values from -0.21875 to 0.21875
- average_reduce: float32 [3072, 768], P('heads', 'wide'), may hold values from -0.109375 to 0.109375
- average_bias: float32 [3072], P(('heads', 'wide')), may hold values from -3 to 3
- average_gains: float32 [3, 768], P(None, ('heads', 'wide')), may hold values from 0.1 to 1.9
Outputs:
- block_output: float32 [32, 1024, 768], P(('heads', 'wide'))
- token_gradient: float32 [32, 1024, 768], P(('heads', 'wide'))
- gradient_norm: float32 [1], replicated
- clip_attend: float32 [3, 768, 768], P(None, 'wide', 'heads')
- mean_attend: float32 [3, 768, 768], P(None, 'wide', 'heads')
- square_attend: float32 [3, 768, 768], P(None, 'wide', 'heads')
- weight_attend: float32 [3, 768, 768], P(None, 'wide', 'heads')
- smooth_attend: float32 [3, 768, 768], P(None, 'wide', 'heads')
- clip_output: float32 [768, 768], P('heads', 'wide')
- mean_output: float32 [768, 768], P('heads', 'wide')
- square_output: float32 [768, 768], P('heads', 'wide')
- weight_output: float32 [768, 768], P('heads', 'wide')
- smooth_output: float32 [768, 768], P('heads', 'wide')
- clip_expand: float32 [768, 3072], P('wide', 'heads')
- mean_expand: float32 [768, 3072], P('wide', 'heads')
- square_expand: float32 [768, 3072], P('wide', 'heads')
- weight_expand: float32 [768, 3072], P('wide', 'heads')
- smooth_expand: float32 [768, 3072], P('wide', 'heads')
- clip_reduce: float32 [3072, 768], P('heads', 'wide')
- mean_reduce: float32 [3072, 768], P('heads', 'wide')
- square_reduce: float32 [3072, 768], P('heads', 'wide')
- weight_reduce: float32 [3072, 768], P('heads', 'wide')
- smooth_reduce: float32 [3072, 768], P('heads', 'wide')
- clip_bias: float32 [3072], P(('heads', 'wide'))
- mean_bias: float32 [3072], P(('heads', 'wide'))
- square_bias: float32 [3072], P(('heads', 'wide'))
- weight_bias: float32 [3072], P(('heads', 'wide'))
- smooth_bias: float32 [3072], P(('heads', 'wide'))
- clip_gains: float32 [3, 768], P(None, ('heads', 'wide'))
- mean_gains: float32 [3, 768], P(None, ('heads', 'wide'))
- square_gains: float32 [3, 768], P(None, ('heads', 'wide'))
- weight_gains: float32 [3, 768], P(None, ('heads', 'wide'))
- smooth_gains: float32 [3, 768], P(None, ('heads', 'wide'))
The draws below stay inside these ranges and needn't reach their ends.
Inputs may be any that keep to these rules, and one draw needn't show every extreme that they name: `lengths`: each image has 1024 * 196 // 1024 (at least 1), 576 or 1024 valid tokens; image 0 has 1024, image 1 the fewest.
All inputs are finite; a program needn't handle non-finite values.
Results may differ from the reference program's by a relative error of at most 0.011.
Values may be sent and summed in bfloat16 or wider, within the bound.
A program may use at most 192 MiB of HBM per device.

```python
import math
import jax
import jax.numpy as jnp
from jax import lax

D = 768
HEADS = 12
HEAD_DIM = 64
FF = 3072
SEQ = 1024
IMAGES = 32
TOKENS = 32768


def rising(count):
    place = lax.broadcasted_iota(jnp.float32, (count,), 0) / count
    return jnp.power(3.0, place - 0.5)


def draw_tokens(key, part):
    keys = jax.random.split(key, 3)
    feature_scale = jnp.exp(jax.random.uniform(keys[0], (D,), jnp.float32, math.log(0.3), math.log(3.0)))
    row_scale = jnp.exp(jax.random.uniform(keys[1], (IMAGES, SEQ, 1), jnp.float32, math.log(0.5), math.log(2.0)))
    base_values = jnp.clip(jax.random.normal(keys[2], (IMAGES, SEQ, D), jnp.float32), -6.0, 6.0)
    return (base_values * feature_scale * row_scale).astype(jnp.bfloat16)


def draw_cotangent(key, part):
    base_values = jnp.clip(jax.random.normal(key, (IMAGES, SEQ, D), jnp.float32), -6.0, 6.0) * rising(D)
    return base_values.astype(jnp.bfloat16)


def ramped_weight(key, rows, columns, spread):
    base_values = jnp.clip(jax.random.normal(key, (rows, columns), jnp.float32), -4.0, 4.0) * rising(rows)[:, None]
    return base_values * spread


def draw_output_weights(key, part):
    return ramped_weight(key, HEADS * HEAD_DIM, D, max(1, D * 16 // SEQ) ** (-0.5))


def draw_reduce_weights(key, part):
    return ramped_weight(key, FF, D, FF ** (-0.5))


def draw_lengths(key, part):
    table = jnp.array([max(1, SEQ * 196 // 1024), max(1, SEQ * 576 // 1024), SEQ], jnp.int32)
    picks = jax.random.randint(key, (IMAGES,), 0, 3)
    chosen = jnp.sum(jnp.where(picks[:, None] == jnp.arange(3, dtype=jnp.int32)[None, :], table[None, :], 0), axis=1)
    chosen = chosen.at[0].set(SEQ).at[1].set(table[0])
    return chosen.astype(jnp.int32)


def steps_of(stream_key, dims, shards, least, top_value):
    def one(dim, blocks):
        draws = jax.random.uniform(jax.random.fold_in(jax.random.fold_in(stream_key, 6), dim), (blocks,), jnp.float32, least / len(shards), top_value / len(shards))
        return jnp.repeat(jnp.exp(draws), dims[dim] // blocks).reshape((-1,) + (1,) * (len(dims) - dim - 1))

    gain = one(*shards[0])
    for cut in shards[1:]:
        gain = gain * one(*cut)
    return gain


def noise(key, extent, scale, most, shards=(), kind=jnp.bfloat16):
    values = scale * jax.random.normal(key, extent, jnp.float32)
    if shards:
        values = values * steps_of(key, extent, shards, -0.22, 0.18)
    return jnp.clip(values, -most, most).astype(kind)


def setup_inputs(seed: int = 0) -> dict:
    key_of = jax.random.split(jax.random.key(seed), 29)
    return {
        "tokens": draw_tokens(jax.random.fold_in(key_of[28], 71), 0),
        "cotangent": draw_cotangent(jax.random.fold_in(key_of[28], 71), 0),
        "lengths": draw_lengths(jax.random.fold_in(key_of[28], 71), 0),
        "step_count": jax.random.randint(key_of[3], (1,), 2, 21).astype(jnp.int32),
        "attend_weights": noise(key_of[4], (3, D, HEADS * HEAD_DIM), D ** -0.5, 0.21875, ((1, 16), (2, 2)), jnp.float32),
        "output_weights": draw_output_weights(jax.random.fold_in(key_of[28], 71), 0),
        "expand_weights": noise(key_of[6], (D, FF), D ** -0.5, 0.21875, ((0, 16), (1, 2)), jnp.float32),
        "reduce_weights": draw_reduce_weights(jax.random.fold_in(key_of[28], 71), 0),
        "expand_bias": noise(key_of[8], (FF,), 0.5, 3.0, ((0, 32),), jnp.float32),
        "norm_gains": jnp.clip(1.0 + 0.18 * jax.random.normal(key_of[9], (3, D), jnp.float32), 0.1, 1.9),
        "first_attend": noise(key_of[10], (3, D, HEADS * HEAD_DIM), (0.00123 * TOKENS ** 0.5), 1.25, ((1, 16), (2, 2)), jnp.float32),
        "first_output": noise(key_of[11], (HEADS * HEAD_DIM, D), (0.00022 * TOKENS ** 0.5), 0.25, ((0, 2), (1, 16)), jnp.float32),
        "first_expand": noise(key_of[12], (D, FF), (0.00082 * TOKENS ** 0.5), 0.875, ((0, 16), (1, 2)), jnp.float32),
        "first_reduce": noise(key_of[13], (FF, D), (0.00178 * TOKENS ** 0.5), 2.0, ((0, 2), (1, 16)), jnp.float32),
        "first_bias": noise(key_of[14], (FF,), (0.00082 * TOKENS ** 0.5), 0.875, ((0, 32),), jnp.float32),
        "first_gains": noise(key_of[15], (3, D), (0.0027 * TOKENS ** 0.5), 3.0, ((1, 32),), jnp.float32),
        "second_attend": jnp.clip(jnp.exp(math.log(1.703936) - 2.7880929 * jax.random.uniform(key_of[16], (3, D, HEADS * HEAD_DIM), jnp.float32) ** steps_of(key_of[16], (3, D, HEADS * HEAD_DIM), ((1, 16), (2, 2)), -0.2, 0.2)), 0.1048576, 1.703936),
        "second_output": jnp.clip(jnp.exp(math.log(0.0524288) - 2.7725887 * jax.random.uniform(key_of[17], (HEADS * HEAD_DIM, D), jnp.float32) ** steps_of(key_of[17], (HEADS * HEAD_DIM, D), ((0, 2), (1, 16)), -0.2, 0.2)), 0.0032768, 0.0524288),
        "second_expand": jnp.clip(jnp.exp(math.log(0.753664) - 2.799022 * jax.random.uniform(key_of[18], (D, FF), jnp.float32) ** steps_of(key_of[18], (D, FF), ((0, 16), (1, 2)), -0.2, 0.2)), 0.0458752, 0.753664),
        "second_reduce": jnp.clip(jnp.exp(math.log(3.60448) - 2.7983728 * jax.random.uniform(key_of[19], (FF, D), jnp.float32) ** steps_of(key_of[19], (FF, D), ((0, 2), (1, 16)), -0.2, 0.2)), 0.2195456, 3.60448),
        "second_bias": jnp.clip(jnp.exp(math.log(0.753664) - 2.799022 * jax.random.uniform(key_of[20], (FF,), jnp.float32) ** steps_of(key_of[20], (FF,), ((0, 32),), -0.2, 0.2)), 0.0458752, 0.753664),
        "second_gains": jnp.clip(jnp.exp(math.log(8.192) - 2.7488722 * jax.random.uniform(key_of[21], (3, D), jnp.float32) ** steps_of(key_of[21], (3, D), ((1, 32),), -0.2, 0.2)), 0.524288, 8.192),
        "average_attend": noise(key_of[22], (3, D, HEADS * HEAD_DIM), D ** -0.5, 0.21875, ((1, 16), (2, 2)), jnp.float32),
        "average_output": noise(key_of[23], (HEADS * HEAD_DIM, D), (max(1, D * 16 // SEQ)) ** -0.5, 1.75, ((0, 2), (1, 16)), jnp.float32),
        "average_expand": noise(key_of[24], (D, FF), D ** -0.5, 0.21875, ((0, 16), (1, 2)), jnp.float32),
        "average_reduce": noise(key_of[25], (FF, D), FF ** -0.5, 0.109375, ((0, 2), (1, 16)), jnp.float32),
        "average_bias": noise(key_of[26], (FF,), 0.5, 3.0, ((0, 32),), jnp.float32),
        "average_gains": jnp.clip(1.0 + 0.18 * jax.random.normal(key_of[27], (3, D), jnp.float32), 0.1, 1.9),
    }


@jax.custom_vjp
def low(v):
    return lax.optimization_barrier(v.astype(jnp.bfloat16)).astype(jnp.float32)

@jax.custom_vjp
def low_back(v):
    return v

def low_keep(v):
    return (low(v), None)

def low_pass(kept, grad):
    return (grad,)

def back_keep(v):
    return (v, None)

def back_low(kept, grad):
    return (low(grad),)
low.defvjp(low_keep, low_pass)
low_back.defvjp(back_keep, back_low)
HIGHEST = lax.Precision.HIGHEST
NORM_EPS = 1e-06
MASKED = -1e+30
BETA_FIRST = 0.9
BETA_SECOND = 0.95
AVERAGE_CAP = 0.9999
ADAM_EPS = 1e-08
RATES = (0.03, 0.2, 0.03, 0.015, 0.3, 0.3)
DECAYS = (0.05, 0.05, 0.05, 0.05, 0.0, 0.0)

def layer_norm(values, gain_row):
    center = values - lax.optimization_barrier(jnp.mean(values, axis=-1, keepdims=True))
    return center * lax.rsqrt(lax.optimization_barrier(jnp.mean(center * center, axis=-1, keepdims=True)) + NORM_EPS) * gain_row

def head_norm(values, gain_row):
    shaped = values.reshape(values.shape[:-1] + (HEADS, HEAD_DIM))
    return layer_norm(shaped, gain_row.reshape(HEADS, HEAD_DIM)).reshape(values.shape)

def attend_image(block_parts):
    queries, key_rows, values, valid_keys = block_parts
    scores = jnp.einsum('qhd,khd->hqk', queries, key_rows, precision=HIGHEST) * HEAD_DIM ** (-0.5)
    scores = jnp.where(valid_keys[None, None, :] > 0, low_back(scores), MASKED)
    row_top = lax.optimization_barrier(jnp.max(scores, axis=-1, keepdims=True))
    expo_scores = jnp.exp(scores - row_top)
    probs = low(expo_scores / lax.optimization_barrier(jnp.sum(expo_scores, axis=-1, keepdims=True)))
    return jnp.einsum('hqk,khd->qhd', probs, values, precision=HIGHEST)

def forward(params, inputs, valid_mask):
    attend_w, output_w, expand_w, reduce_w, bias_row, gains = params
    image_count = inputs.shape[0]
    normed = low(layer_norm(inputs, gains[0]))
    projected = jnp.einsum('gsd,cde->cgse', normed, low(attend_w), precision=HIGHEST)
    queries = low(head_norm(low_back(projected[0]), gains[1]))
    key_rows = low(head_norm(low_back(projected[1]), gains[2]))
    values = low(low_back(projected[2]))
    split_shape = (image_count, SEQ, HEADS, HEAD_DIM)
    mixed_heads = lax.map(jax.checkpoint(attend_image), (queries.reshape(split_shape), key_rows.reshape(split_shape), values.reshape(split_shape), valid_mask))
    mixed_heads = low(low_back(mixed_heads.reshape(image_count, SEQ, HEADS * HEAD_DIM)))
    attended = jnp.einsum('gse,ed->gsd', mixed_heads, low(output_w), precision=HIGHEST)
    pre_act = low_back(jnp.einsum('gsd,df->gsf', normed, low(expand_w), precision=HIGHEST) + low(bias_row))
    hidden = low(jax.nn.gelu(pre_act, approximate=False))
    expanded = jnp.einsum('gsf,fd->gsd', hidden, low(reduce_w), precision=HIGHEST)
    return inputs + attended + expanded

def optimizer_update(weight, raw_grad, factor, first, second, average, rate, decay, first_fix, second_fix, keep):
    clipped = raw_grad * factor
    first_new = BETA_FIRST * first + (1.0 - BETA_FIRST) * clipped
    second_new = BETA_SECOND * second + (1.0 - BETA_SECOND) * clipped * clipped
    direction = first_new / first_fix / (jnp.sqrt(second_new / second_fix) + ADAM_EPS)
    weight_new = weight - rate * (direction + decay * weight)
    average_new = keep * average + (1.0 - keep) * weight_new
    return (clipped, first_new, second_new, weight_new, average_new)

def reference(tokens, cotangent, lengths, step_count, attend_weights, output_weights, expand_weights, reduce_weights, expand_bias, norm_gains, first_attend, first_output, first_expand, first_reduce, first_bias, first_gains, second_attend, second_output, second_expand, second_reduce, second_bias, second_gains, average_attend, average_output, average_expand, average_reduce, average_bias, average_gains):
    params = (attend_weights, output_weights, expand_weights, reduce_weights, expand_bias, norm_gains)
    group_size = 4
    group_total = IMAGES // group_size
    positions = lax.broadcasted_iota(jnp.int32, (IMAGES, SEQ), 1)
    valid_mask = (positions < lengths[:, None]).astype(jnp.float32)
    inputs = tokens.astype(jnp.float32).reshape(group_total, group_size, SEQ, D)
    upstream = (cotangent.astype(jnp.float32) * valid_mask[:, :, None]).reshape(group_total, group_size, SEQ, D)
    valid_groups = valid_mask.reshape(group_total, group_size, SEQ)

    def group_step(totals, pieces):
        group_inputs, group_upstream, group_valid = pieces
        outputs, pullback = jax.vjp(lambda weights, values: forward(weights, values, group_valid), params, group_inputs)
        weight_grads, input_grads = pullback(group_upstream)
        summed = tuple((left + right for left, right in zip(totals, weight_grads)))
        return (summed, (outputs, input_grads))
    zeros_start = tuple((jnp.zeros_like(entry) for entry in params))
    totals, (outputs, input_grads) = lax.scan(group_step, zeros_start, (inputs, upstream, valid_groups))
    block_output = outputs.reshape(IMAGES, SEQ, D)
    token_gradient = input_grads.reshape(IMAGES, SEQ, D)
    squares = jnp.sum(jnp.stack([jnp.sum(entry * entry) for entry in totals]))
    grad_norm = jnp.sqrt(squares)
    limit = 0.02 * math.sqrt(TOKENS * D * FF)
    factor = jnp.minimum(1.0, limit / grad_norm)
    step_float = step_count[0].astype(jnp.float32)
    first_fix = 1.0 - jnp.power(BETA_FIRST, step_float)
    second_fix = 1.0 - jnp.power(BETA_SECOND, step_float)
    keep = jnp.minimum(AVERAGE_CAP, (1.0 + step_float) / (10.0 + step_float))
    firsts = (first_attend, first_output, first_expand, first_reduce, first_bias, first_gains)
    seconds = (second_attend, second_output, second_expand, second_reduce, second_bias, second_gains)
    averages = (average_attend, average_output, average_expand, average_reduce, average_bias, average_gains)
    updated = [optimizer_update(params[index], totals[index], factor, firsts[index], seconds[index], averages[index], RATES[index], DECAYS[index], first_fix, second_fix, keep) for index in range(6)]
    attend_new, output_new, expand_new, reduce_new, bias_new, gains_new = updated
    return (block_output, token_gradient, grad_norm.reshape(1), attend_new[0], attend_new[1], attend_new[2], attend_new[3], attend_new[4], output_new[0], output_new[1], output_new[2], output_new[3], output_new[4], expand_new[0], expand_new[1], expand_new[2], expand_new[3], expand_new[4], reduce_new[0], reduce_new[1], reduce_new[2], reduce_new[3], reduce_new[4], bias_new[0], bias_new[1], bias_new[2], bias_new[3], bias_new[4], gains_new[0], gains_new[1], gains_new[2], gains_new[3], gains_new[4])
```

```python
from functools import partial
import math

import jax
import jax.numpy as jnp
from jax import lax
from jax.experimental import pallas as pl
from jax.experimental.pallas import tpu as pltpu
from jax.sharding import PartitionSpec as P

D = 768
HEADS = 12
HEAD_DIM = 64
FF = 3072
HALF_E = D // 2
HALF_F = FF // 2
PAIR = 128
PAIRS = HALF_E // PAIR
CHUNK = 512
CHUNKS = HALF_F // CHUNK
QUERY_ROWS = 512
BF = jnp.bfloat16
F32 = jnp.float32

NORM_EPS = 1e-06
MASKED = -1e30
BETA_FIRST = 0.9
BETA_SECOND = 0.95
AVERAGE_CAP = 0.9999
ADAM_EPS = 1e-08
RATES = (0.03, 0.2, 0.03, 0.015, 0.3, 0.3)
DECAYS = (0.05, 0.05, 0.05, 0.05, 0.0, 0.0)


def dot(left, right, left_dim, right_dim):
    return lax.dot_general(
        left, right, (((left_dim,), (right_dim,)), ((), ())), preferred_element_type=F32
    )


def row_norm(values):
    center = values - jnp.mean(values, axis=-1, keepdims=True)
    inverse = lax.rsqrt(jnp.mean(center * center, axis=-1, keepdims=True) + NORM_EPS)
    return center * inverse, inverse


def head_mean(values):
    width = values.shape[1]
    row = lax.broadcasted_iota(jnp.int32, (width, width), 0) // HEAD_DIM
    column = lax.broadcasted_iota(jnp.int32, (width, width), 1) // HEAD_DIM
    block = jnp.where(row == column, 1.0 / HEAD_DIM, 0.0).astype(BF)
    high = values.astype(BF)
    rest = (values - high.astype(F32)).astype(BF)
    return dot(high, block, 1, 0) + dot(rest, block, 1, 0)


def head_norm(values):
    center = values - head_mean(values)
    inverse = lax.rsqrt(head_mean(center * center) + NORM_EPS)
    return center * inverse, inverse


def head_norm_back(upstream, normal, inverse):
    return inverse * (upstream - head_mean(upstream) - normal * head_mean(upstream * normal))


def pair_attention(query, keyed, value, back_mixed, key_bias):
    rows = query.shape[0]
    lane = lax.broadcasted_iota(jnp.int32, (rows, PAIR), 1)
    low = lane < HEAD_DIM
    first = lane == 0
    zero = jnp.zeros((rows, PAIR), BF)
    one_lane = jnp.where(first, 1.0, 0.0).astype(BF)
    bias_lane = jnp.where(first, key_bias, 0.0).astype(BF)
    query_wide = jnp.concatenate([query, one_lane], axis=1)
    value_wide = jnp.concatenate([value, jnp.ones((rows, PAIR), BF)], axis=1)
    blocks = rows // QUERY_ROWS
    mixed = [[None] * blocks for _ in range(2)]
    back_query = [[None] * blocks for _ in range(2)]
    back_keyed = None
    back_value = None
    lane_q = lane[:QUERY_ROWS]
    low_q = low[:QUERY_ROWS]
    for head in range(2):
        mine = low if head == 0 else ~low
        mine_q = mine[:QUERY_ROWS]
        key_wide = jnp.concatenate([jnp.where(mine, keyed, zero), bias_lane], axis=1)
        query_mine = jnp.where(mine, query, zero)
        for block in range(blocks):
            cut = slice(block * QUERY_ROWS, (block + 1) * QUERY_ROWS)
            expo = jnp.exp(dot(query_wide[cut], key_wide, 1, 1))
            expo_low = expo.astype(BF)
            sums = dot(expo_low, value_wide, 1, 0)
            inverse = 1.0 / sums[:, PAIR:]
            rows_mixed = sums[:, :PAIR] * inverse
            scaled = jnp.where(mine_q, back_mixed[cut].astype(F32) * inverse, 0.0).astype(BF)
            inner = jnp.sum(rows_mixed * scaled.astype(F32), axis=1, keepdims=True)
            inner_high = inner.astype(BF).astype(F32)
            inner_lanes = jnp.where(
                lane_q == 0, -inner_high, jnp.where(lane_q == 1, inner_high - inner, 0.0)
            ).astype(BF)
            centered = dot(jnp.concatenate([scaled, inner_lanes], axis=1), value_wide, 1, 1)
            back_scores = (expo * centered).astype(BF)
            mixed[head][block] = rows_mixed
            back_query[head][block] = dot(back_scores, keyed, 1, 0)
            add_keyed = dot(query_mine[cut], back_scores, 0, 0)
            add_value = dot(scaled, expo_low, 0, 0)
            back_keyed = add_keyed if back_keyed is None else back_keyed + add_keyed
            back_value = add_value if back_value is None else back_value + add_value
    join = lambda parts: jnp.concatenate(
        [jnp.where(low_q, parts[0][block], parts[1][block]) for block in range(blocks)], axis=0
    )
    return join(mixed).astype(BF), join(back_query), back_keyed.T, back_value.T.astype(BF)


def attention_section(weights_first, weights_second, normed, upstream, query_gain, key_gain, key_bias):
    three = 3 * PAIR
    into = jnp.concatenate([weights_first[:, :three], weights_second[:, :three]], axis=1)
    out = jnp.concatenate([weights_first[:, three:], weights_second[:, three:]], axis=1)
    projected = dot(normed, into, 1, 0)
    back_mixed = dot(upstream, out, 1, 0).astype(BF)
    pick = lambda place: jnp.concatenate(
        [
            projected[:, place * PAIR : (place + 1) * PAIR],
            projected[:, three + place * PAIR : three + (place + 1) * PAIR],
        ],
        axis=1,
    )
    query_hat, query_inv = head_norm(pick(0))
    key_hat, key_inv = head_norm(pick(1))
    query = (query_hat * query_gain).astype(BF)
    keyed = (key_hat * key_gain).astype(BF)
    value = pick(2).astype(BF)
    query = (query.astype(F32) * HEAD_DIM ** (-0.5)).astype(BF)
    parts = [
        pair_attention(
            query[:, cut], keyed[:, cut], value[:, cut], back_mixed[:, cut], key_bias
        )
        for cut in (slice(0, PAIR), slice(PAIR, 2 * PAIR))
    ]
    mixed = jnp.concatenate([parts[0][0], parts[1][0]], axis=1)
    back_qn = jnp.concatenate([parts[0][1], parts[1][1]], axis=1) * HEAD_DIM ** (-0.5)
    back_kn = jnp.concatenate([parts[0][2], parts[1][2]], axis=1)
    query_gain_back = jnp.sum(back_qn * query_hat, axis=0, keepdims=True)
    key_gain_back = jnp.sum(back_kn * key_hat, axis=0, keepdims=True)
    back_query = head_norm_back(back_qn * query_gain, query_hat, query_inv).astype(BF)
    back_keyed = head_norm_back(back_kn * key_gain, key_hat, key_inv).astype(BF)
    back_into = jnp.concatenate(
        [
            back_query[:, :PAIR],
            back_keyed[:, :PAIR],
            parts[0][3],
            back_query[:, PAIR:],
            back_keyed[:, PAIR:],
            parts[1][3],
        ],
        axis=1,
    )
    add_out = dot(mixed, out, 1, 1)
    add_back = dot(back_into, into, 1, 1)
    grad_into = dot(normed, back_into, 0, 0)
    grad_out = dot(upstream, mixed, 0, 0)
    grads = [
        jnp.concatenate(
            [grad_into[:, half * three : (half + 1) * three], grad_out[:, half * PAIR : (half + 1) * PAIR]],
            axis=1,
        )
        for half in range(2)
    ]
    return add_out, add_back, grads, query_gain_back, key_gain_back


def mlp_section(weights, normed, upstream, bias):
    expand = weights[:, :CHUNK]
    reduce = weights[:, CHUNK:]
    pre = dot(normed, expand, 1, 0) + bias
    back_hidden = dot(upstream, reduce, 1, 0)
    phi = 0.5 * (1.0 + lax.erf(pre * math.sqrt(0.5)))
    density = jnp.exp(-0.5 * pre * pre) * (1.0 / math.sqrt(2.0 * math.pi))
    hidden = (pre * phi).astype(BF)
    back_pre = (back_hidden * (phi + pre * density)).astype(BF)
    add_out = dot(hidden, reduce, 1, 1)
    add_back = dot(back_pre, expand, 1, 1)
    grad = jnp.concatenate([dot(normed, back_pre, 0, 0), dot(upstream, hidden, 0, 0)], axis=1)
    return add_out, add_back, grad, jnp.sum(back_pre.astype(F32), axis=0, keepdims=True)


def start_input(
    length_ref, tokens_ref, cotangent_ref, gains_ref, normed_ref, upstream_ref, out_ref, back_ref
):
    place = lax.broadcasted_iota(jnp.int32, (tokens_ref.shape[0], 1), 0)
    inputs = tokens_ref[...].astype(F32)
    input_hat, _ = row_norm(inputs)
    normed_ref[...] = (input_hat * gains_ref[0:1, :]).astype(BF)
    upstream_ref[...] = jnp.where(place < length_ref[0], cotangent_ref[...].astype(F32), 0.0).astype(BF)
    out_ref[...] = inputs
    back_ref[...] = jnp.zeros_like(back_ref)


def finish_input(tokens_ref, gains_ref, upstream_ref, back_ref, gains_back_ref):
    input_hat, input_inv = row_norm(tokens_ref[...].astype(F32))
    back_normed = back_ref[...]
    gains_back_ref[0:1, :] = jnp.sum(back_normed * input_hat, axis=0, keepdims=True)
    scaled = back_normed * gains_ref[0:1, :]
    back_ref[...] = upstream_ref[...].astype(F32) + input_inv * (
        scaled
        - jnp.mean(scaled, axis=-1, keepdims=True)
        - input_hat * jnp.mean(scaled * input_hat, axis=-1, keepdims=True)
    )


def local_kernel(
    length_ref, tokens_ref, cotangent_ref, gains_ref, bias_ref, pair_ref, chunk_ref,
    out_ref, back_ref, grad_pair_ref, grad_chunk_ref, bias_back_ref, gains_back_ref,
    normed_ref, upstream_ref,
):
    index = pl.program_id(0)

    @pl.when(index == 0)
    def _():
        start_input(
            length_ref, tokens_ref, cotangent_ref, gains_ref, normed_ref, upstream_ref, out_ref, back_ref
        )

    is_pair = (index == 0) | (index > 2 * CHUNKS)

    @pl.when(is_pair)
    def _():
        unit = jnp.where(index == 0, 0, index - 2 * CHUNKS)
        starts = [pl.multiple_of(half * HALF_E + unit * PAIR, PAIR) for half in range(2)]
        gain_of = lambda row: jnp.concatenate(
            [gains_ref[row : row + 1, pl.ds(start, PAIR)] for start in starts], axis=1
        )
        place = lax.broadcasted_iota(jnp.int32, (tokens_ref.shape[0], 1), 0)
        add_out, add_back, grads, query_back, key_back = attention_section(
            pair_ref[0, 0], pair_ref[0, 1], normed_ref[...], upstream_ref[...],
            gain_of(1), gain_of(2), jnp.where(place < length_ref[0], 0.0, MASKED),
        )
        out_ref[...] += add_out
        back_ref[...] += add_back
        for half in range(2):
            grad_pair_ref[0, half] = grads[half].astype(BF)
            cut = slice(half * PAIR, (half + 1) * PAIR)
            gains_back_ref[1:2, pl.ds(starts[half], PAIR)] = query_back[:, cut]
            gains_back_ref[2:3, pl.ds(starts[half], PAIR)] = key_back[:, cut]

    @pl.when(~is_pair)
    def _():
        unit = (index - 1) // 2
        half = lax.rem(index - 1, 2)
        start = pl.multiple_of(half * HALF_F + unit * CHUNK, CHUNK)
        add_out, add_back, grad, bias_back = mlp_section(
            chunk_ref[0, 0], normed_ref[...], upstream_ref[...],
            bias_ref[0:1, pl.ds(start, CHUNK)],
        )
        out_ref[...] += add_out
        back_ref[...] += add_back
        grad_chunk_ref[0, 0] = grad.astype(BF)
        bias_back_ref[0:1, pl.ds(start, CHUNK)] = bias_back

    @pl.when(index == PAIRS + 2 * CHUNKS - 1)
    def _():
        finish_input(tokens_ref, gains_ref, upstream_ref, back_ref, gains_back_ref)


def local_block(length, tokens, cotangent, gains, bias, pair_weights, chunk_weights):
    slots = tokens.shape[0]
    steps = PAIRS + 2 * CHUNKS
    whole = lambda shape: pl.BlockSpec(shape, lambda index: (0,) * len(shape))
    pair_at = lambda index: (jnp.maximum(index - 2 * CHUNKS, 0), 0, 0, 0)

    def chunk_at(index):
        flat = jnp.clip(index - 1, 0, 2 * CHUNKS - 1)
        return (flat // 2, lax.rem(flat, 2), 0, 0)

    pair_spec = pl.BlockSpec((1, 2, D, 4 * PAIR), pair_at)
    chunk_spec = pl.BlockSpec((1, 1, D, 2 * CHUNK), chunk_at)
    return pl.pallas_call(
        local_kernel,
        grid=(steps,),
        in_specs=[
            pl.BlockSpec(memory_space=pltpu.SMEM),
            whole((slots, D)), whole((slots, D)), whole((3, D)), whole((1, FF)), pair_spec, chunk_spec,
        ],
        out_specs=[
            whole((slots, D)), whole((slots, D)), pair_spec, chunk_spec, whole((1, FF)), whole((3, D)),
        ],
        out_shape=[
            jax.ShapeDtypeStruct((slots, D), F32),
            jax.ShapeDtypeStruct((slots, D), F32),
            jax.ShapeDtypeStruct((PAIRS, 2, D, 4 * PAIR), BF),
            jax.ShapeDtypeStruct((CHUNKS, 2, D, 2 * CHUNK), BF),
            jax.ShapeDtypeStruct((1, FF), F32),
            jax.ShapeDtypeStruct((3, D), F32),
        ],
        scratch_shapes=[pltpu.VMEM((slots, D), BF), pltpu.VMEM((slots, D), BF)],
        compiler_params=pltpu.CompilerParams(vmem_limit_bytes=60 << 20),
        name="local_block",
    )(length, tokens, cotangent, gains, bias, pair_weights, chunk_weights)


def optimizer_update(
    weight, raw_grad, factor, first, second, average, rate, decay, first_fix, second_fix, keep
):
    clipped = raw_grad * factor
    first_new = BETA_FIRST * first + (1.0 - BETA_FIRST) * clipped
    second_new = BETA_SECOND * second + (1.0 - BETA_SECOND) * clipped * clipped
    direction = first_new / first_fix / (jnp.sqrt(second_new / second_fix) + ADAM_EPS)
    weight_new = weight - rate * (direction + decay * weight)
    average_new = keep * average + (1.0 - keep) * weight_new
    return (clipped, first_new, second_new, weight_new, average_new)


def pack_shards(attend_weights, output_weights, expand_weights, reduce_weights):
    rows = attend_weights.shape[1]
    attend = attend_weights.astype(BF).reshape(3, rows, PAIRS, PAIR)
    attend = jnp.transpose(attend, (2, 1, 0, 3)).reshape(PAIRS, rows, 3 * PAIR)
    output = jnp.transpose(
        output_weights.astype(BF).T.reshape(rows, PAIRS, PAIR), (1, 0, 2)
    )
    expand = jnp.transpose(expand_weights.astype(BF).reshape(rows, CHUNKS, CHUNK), (1, 0, 2))
    reduce = jnp.transpose(reduce_weights.astype(BF).T.reshape(rows, CHUNKS, CHUNK), (1, 0, 2))
    return jnp.concatenate([attend, output], axis=2), jnp.concatenate([expand, reduce], axis=2)


def unpack_shards(pair_grads, chunk_grads):
    rows = pair_grads.shape[1]
    attend = jnp.transpose(
        pair_grads[:, :, : 3 * PAIR].reshape(PAIRS, rows, 3, PAIR), (2, 1, 0, 3)
    ).reshape(3, rows, HALF_E)
    join = lambda part: jnp.transpose(part, (1, 0, 2)).reshape(rows, -1)
    return (
        attend,
        join(pair_grads[:, :, 3 * PAIR :]).T,
        join(chunk_grads[:, :, :CHUNK]),
        join(chunk_grads[:, :, CHUNK:]).T,
    )


def gathered_block(lengths, tokens, cotangent, norm_gains, expand_bias, pair_own, chunk_own):
    both = ("heads", "wide")
    gains = lax.all_gather(norm_gains, both, axis=1, tiled=True)
    bias = lax.all_gather(expand_bias.astype(BF), both, axis=0, tiled=True).astype(F32)
    whole = lambda own: lax.all_gather(
        lax.all_gather(own, "wide", axis=1, tiled=True), "heads", axis=1
    )
    block_output, token_gradient, pair_grads, chunk_grads, bias_back, gains_back = local_block(
        lengths, tokens, cotangent, gains, bias[None, :], whole(pair_own), whole(chunk_own)
    )
    scatter = lambda part: lax.psum_scatter(
        lax.psum_scatter(part, "heads", scatter_dimension=1),
        "wide", scatter_dimension=1, tiled=True,
    ).astype(F32)
    grads = unpack_shards(scatter(pair_grads), scatter(chunk_grads)) + (
        lax.psum_scatter(bias_back[0], both, scatter_dimension=0, tiled=True),
        lax.psum_scatter(gains_back, both, scatter_dimension=1, tiled=True),
    )
    squares = jnp.sum(jnp.stack([jnp.sum(entry * entry) for entry in grads]))
    return block_output, token_gradient, grads, lax.psum(squares, both)


def body(
    tokens, cotangent, lengths, step_count,
    attend_weights, output_weights, expand_weights, reduce_weights, expand_bias, norm_gains,
    *moments,
):
    masters = (
        attend_weights, output_weights, expand_weights, reduce_weights, expand_bias, norm_gains,
    )
    firsts, seconds, averages = moments[:6], moments[6:12], moments[12:]
    pair_own, chunk_own = pack_shards(*masters[:4])
    block_output, token_gradient, grads, total_squares = gathered_block(
        lengths, tokens[0], cotangent[0], norm_gains, expand_bias, pair_own, chunk_own
    )
    grad_norm = jnp.sqrt(total_squares)
    tokens_all = tokens.shape[1] * lax.axis_size("heads") * lax.axis_size("wide")
    limit = 0.02 * math.sqrt(tokens_all * D * FF)
    factor = jnp.minimum(1.0, limit / grad_norm)
    step_float = step_count[0].astype(F32)
    first_fix = 1.0 - jnp.power(BETA_FIRST, step_float)
    second_fix = 1.0 - jnp.power(BETA_SECOND, step_float)
    keep = jnp.minimum(AVERAGE_CAP, (1.0 + step_float) / (10.0 + step_float))
    results = [block_output[None], token_gradient[None], grad_norm.reshape(1)]
    for index in range(6):
        results.extend(
            optimizer_update(
                masters[index], grads[index], factor, firsts[index], seconds[index],
                averages[index], RATES[index], DECAYS[index], first_fix, second_fix, keep,
            )
        )
    return tuple(results)


def solution(mesh):
    both = ("heads", "wide")
    weight_specs = (
        P(None, "wide", "heads"), P("heads", "wide"), P("wide", "heads"), P("heads", "wide"),
        P(both), P(None, both),
    )
    image = P(both, None, None)
    return jax.shard_map(
        body,
        mesh=mesh,
        in_specs=(image, image, P(both), P()) + weight_specs * 4,
        out_specs=(image, image, P()) + tuple(spec for spec in weight_specs for _ in range(5)),
        check_vma=False,
    )
```

```python
from functools import partial
import math

import jax
import jax.numpy as jnp
from jax import lax
from jax.experimental import pallas as pl
from jax.experimental.pallas import tpu as pltpu
from jax.sharding import PartitionSpec as P

D = 768
HEADS = 12
HEAD_DIM = 64
FF = 3072
HALF_E = D // 2
HALF_F = FF // 2
PAIR = 128
PAIRS = HALF_E // PAIR
CHUNK = 512
CHUNKS = HALF_F // CHUNK
QUERY_ROWS = 512
ROWS = 256
BF = jnp.bfloat16
F32 = jnp.float32

NORM_EPS = 1e-06
MASKED = -1e30
BETA_FIRST = 0.9
BETA_SECOND = 0.95
AVERAGE_CAP = 0.9999
ADAM_EPS = 1e-08
RATES = (0.03, 0.2, 0.03, 0.015, 0.3, 0.3)
DECAYS = (0.05, 0.05, 0.05, 0.05, 0.0, 0.0)


def dot(left, right, left_dim, right_dim):
    return lax.dot_general(
        left, right, (((left_dim,), (right_dim,)), ((), ())), preferred_element_type=F32
    )


def row_norm(values):
    center = values - jnp.mean(values, axis=-1, keepdims=True)
    inverse = lax.rsqrt(jnp.mean(center * center, axis=-1, keepdims=True) + NORM_EPS)
    return center * inverse, inverse


def head_mean(values):
    width = values.shape[1]
    row = lax.broadcasted_iota(jnp.int32, (width, width), 0) // HEAD_DIM
    column = lax.broadcasted_iota(jnp.int32, (width, width), 1) // HEAD_DIM
    block = jnp.where(row == column, 1.0 / HEAD_DIM, 0.0).astype(BF)
    high = values.astype(BF)
    rest = (values - high.astype(F32)).astype(BF)
    return dot(high, block, 1, 0) + dot(rest, block, 1, 0)


def head_norm(values):
    center = values - head_mean(values)
    inverse = lax.rsqrt(head_mean(center * center) + NORM_EPS)
    return center * inverse, inverse


def head_norm_back(upstream, normal, inverse):
    return inverse * (upstream - head_mean(upstream) - normal * head_mean(upstream * normal))


def pair_attention(query, keyed, value, back_mixed, key_bias):
    rows = query.shape[0]
    lane = lax.broadcasted_iota(jnp.int32, (rows, PAIR), 1)
    low = lane < HEAD_DIM
    first = lane == 0
    zero = jnp.zeros((rows, PAIR), BF)
    one_lane = jnp.where(first, 1.0, 0.0).astype(BF)
    bias_lane = jnp.where(first, key_bias, 0.0).astype(BF)
    query_wide = jnp.concatenate([query, one_lane], axis=1)
    value_wide = jnp.concatenate([value, jnp.ones((rows, PAIR), BF)], axis=1)
    blocks = rows // QUERY_ROWS
    mixed = [[None] * blocks for _ in range(2)]
    back_query = [[None] * blocks for _ in range(2)]
    back_keyed = None
    back_value = None
    lane_q = lane[:QUERY_ROWS]
    low_q = low[:QUERY_ROWS]
    for head in range(2):
        mine = low if head == 0 else ~low
        mine_q = mine[:QUERY_ROWS]
        key_wide = jnp.concatenate([jnp.where(mine, keyed, zero), bias_lane], axis=1)
        query_mine = jnp.where(mine, query, zero)
        for block in range(blocks):
            cut = slice(block * QUERY_ROWS, (block + 1) * QUERY_ROWS)
            expo = jnp.exp(dot(query_wide[cut], key_wide, 1, 1))
            expo_low = expo.astype(BF)
            sums = dot(expo_low, value_wide, 1, 0)
            inverse = 1.0 / sums[:, PAIR:]
            rows_mixed = sums[:, :PAIR] * inverse
            scaled = jnp.where(mine_q, back_mixed[cut].astype(F32) * inverse, 0.0).astype(BF)
            inner = jnp.sum(rows_mixed * scaled.astype(F32), axis=1, keepdims=True)
            inner_high = inner.astype(BF).astype(F32)
            inner_lanes = jnp.where(
                lane_q == 0, -inner_high, jnp.where(lane_q == 1, inner_high - inner, 0.0)
            ).astype(BF)
            centered = dot(jnp.concatenate([scaled, inner_lanes], axis=1), value_wide, 1, 1)
            back_scores = (expo * centered).astype(BF)
            mixed[head][block] = rows_mixed
            back_query[head][block] = dot(back_scores, keyed, 1, 0)
            add_keyed = dot(query_mine[cut], back_scores, 0, 0)
            add_value = dot(scaled, expo_low, 0, 0)
            back_keyed = add_keyed if back_keyed is None else back_keyed + add_keyed
            back_value = add_value if back_value is None else back_value + add_value
    join = lambda parts: jnp.concatenate(
        [jnp.where(low_q, parts[0][block], parts[1][block]) for block in range(blocks)], axis=0
    )
    return join(mixed).astype(BF), join(back_query), back_keyed.T, back_value.T.astype(BF)


def attention_section(
    weights_first, weights_second, normed, upstream, query_gain, key_gain, key_bias, out_ref, back_ref,
    pause=lambda place: None,
):
    three = 3 * PAIR
    into = jnp.concatenate([weights_first[:, :three], weights_second[:, :three]], axis=1)
    out = jnp.concatenate([weights_first[:, three:], weights_second[:, three:]], axis=1)
    projected = dot(normed, into, 1, 0)
    back_mixed = dot(upstream, out, 1, 0).astype(BF)
    pick = lambda place: jnp.concatenate(
        [
            projected[:, place * PAIR : (place + 1) * PAIR],
            projected[:, three + place * PAIR : three + (place + 1) * PAIR],
        ],
        axis=1,
    )
    query_hat, query_inv = head_norm(pick(0))
    key_hat, key_inv = head_norm(pick(1))
    query = (query_hat * query_gain).astype(BF)
    keyed = (key_hat * key_gain).astype(BF)
    value = pick(2).astype(BF)
    query = (query.astype(F32) * HEAD_DIM ** (-0.5)).astype(BF)
    pause(0)
    parts = []
    for half in range(2):
        cut = slice(half * PAIR, (half + 1) * PAIR)
        parts.append(
            pair_attention(query[:, cut], keyed[:, cut], value[:, cut], back_mixed[:, cut], key_bias)
        )
        pause(1 + half)
    mixed = jnp.concatenate([parts[0][0], parts[1][0]], axis=1)
    back_qn = jnp.concatenate([parts[0][1], parts[1][1]], axis=1) * HEAD_DIM ** (-0.5)
    back_kn = jnp.concatenate([parts[0][2], parts[1][2]], axis=1)
    query_gain_back = jnp.sum(back_qn * query_hat, axis=0, keepdims=True)
    key_gain_back = jnp.sum(back_kn * key_hat, axis=0, keepdims=True)
    back_query = head_norm_back(back_qn * query_gain, query_hat, query_inv).astype(BF)
    back_keyed = head_norm_back(back_kn * key_gain, key_hat, key_inv).astype(BF)
    back_into = jnp.concatenate(
        [
            back_query[:, :PAIR],
            back_keyed[:, :PAIR],
            parts[0][3],
            back_query[:, PAIR:],
            back_keyed[:, PAIR:],
            parts[1][3],
        ],
        axis=1,
    )
    out_ref[...] += dot(mixed, out, 1, 1)
    back_ref[...] += dot(back_into, into, 1, 1)
    grad_into = dot(normed, back_into, 0, 0).astype(BF)
    grad_out = dot(upstream, mixed, 0, 0).astype(BF)
    grads = [
        jnp.concatenate(
            [grad_into[:, half * three : (half + 1) * three], grad_out[:, half * PAIR : (half + 1) * PAIR]],
            axis=1,
        )
        for half in range(2)
    ]
    return grads, query_gain_back, key_gain_back


def mlp_section(weights, normed, upstream, bias, out_ref, back_ref):
    expand = weights[:, :CHUNK]
    reduce = weights[:, CHUNK:]
    pre = dot(normed, expand, 1, 0) + bias
    back_hidden = dot(upstream, reduce, 1, 0)
    phi = 0.5 * (1.0 + lax.erf(pre * math.sqrt(0.5)))
    density = jnp.exp(-0.5 * pre * pre) * (1.0 / math.sqrt(2.0 * math.pi))
    hidden = (pre * phi).astype(BF)
    back_pre = (back_hidden * (phi + pre * density)).astype(BF)
    out_ref[...] += dot(hidden, reduce, 1, 1)
    back_ref[...] += dot(back_pre, expand, 1, 1)
    grads = [dot(normed, back_pre, 0, 0).astype(BF), dot(upstream, hidden, 0, 0).astype(BF)]
    return jnp.concatenate(grads, axis=1), jnp.sum(back_pre.astype(F32), axis=0, keepdims=True)


def over_rows(slots, act):
    def one(block, carry):
        act(pl.ds(pl.multiple_of(block * ROWS, ROWS), ROWS))
        return carry

    lax.fori_loop(0, slots // ROWS, one, 0)


def below(length_ref, rows):
    place = lax.broadcasted_iota(jnp.int32, (rows.size, 1), 0) + rows.start
    return place < length_ref[0]


def start_input(
    length_ref, tokens_ref, cotangent_ref, gains_ref, normed_ref, upstream_ref, out_ref, back_ref
):
    def one(rows):
        inputs = tokens_ref[rows, :].astype(F32)
        input_hat, _ = row_norm(inputs)
        normed_ref[rows, :] = (input_hat * gains_ref[0:1, :]).astype(BF)
        upstream_ref[rows, :] = jnp.where(
            below(length_ref, rows), cotangent_ref[rows, :].astype(F32), 0.0
        ).astype(BF)
        out_ref[rows, :] = inputs
        back_ref[rows, :] = jnp.zeros_like(inputs)

    over_rows(tokens_ref.shape[0], one)


def finish_input(tokens_ref, gains_ref, upstream_ref, back_ref, gains_back_ref):
    gains_back_ref[0:1, :] = jnp.zeros_like(gains_back_ref[0:1, :])

    def one(rows):
        input_hat, input_inv = row_norm(tokens_ref[rows, :].astype(F32))
        back_normed = back_ref[rows, :]
        gains_back_ref[0:1, :] += jnp.sum(back_normed * input_hat, axis=0, keepdims=True)
        scaled = back_normed * gains_ref[0:1, :]
        back_ref[rows, :] = upstream_ref[rows, :].astype(F32) + input_inv * (
            scaled
            - jnp.mean(scaled, axis=-1, keepdims=True)
            - input_hat * jnp.mean(scaled * input_hat, axis=-1, keepdims=True)
        )

    over_rows(tokens_ref.shape[0], one)


def local_kernel(
    length_ref, tokens_ref, cotangent_ref, gains_ref, bias_ref, pair_ref, chunk_ref,
    out_ref, back_ref, grad_pair_ref, grad_chunk_ref, bias_back_ref, gains_back_ref,
    normed_ref, upstream_ref,
):
    index = pl.program_id(0)

    @pl.when(index == 0)
    def _():
        start_input(
            length_ref, tokens_ref, cotangent_ref, gains_ref, normed_ref, upstream_ref, out_ref, back_ref
        )

    is_pair = (index == 0) | (index > 2 * CHUNKS)

    @pl.when(is_pair)
    def _():
        unit = jnp.where(index == 0, 0, index - 2 * CHUNKS)
        starts = [pl.multiple_of(half * HALF_E + unit * PAIR, PAIR) for half in range(2)]
        gain_of = lambda row: jnp.concatenate(
            [gains_ref[row : row + 1, pl.ds(start, PAIR)] for start in starts], axis=1
        )
        place = lax.broadcasted_iota(jnp.int32, (tokens_ref.shape[0], 1), 0)
        grads, query_back, key_back = attention_section(
            pair_ref[0, 0], pair_ref[0, 1], normed_ref[...], upstream_ref[...],
            gain_of(1), gain_of(2), jnp.where(place < length_ref[0], 0.0, MASKED), out_ref, back_ref,
        )
        for half in range(2):
            grad_pair_ref[0, half] = grads[half]
            cut = slice(half * PAIR, (half + 1) * PAIR)
            gains_back_ref[1:2, pl.ds(starts[half], PAIR)] = query_back[:, cut]
            gains_back_ref[2:3, pl.ds(starts[half], PAIR)] = key_back[:, cut]

    @pl.when(~is_pair)
    def _():
        unit = (index - 1) // 2
        half = lax.rem(index - 1, 2)
        start = pl.multiple_of(half * HALF_F + unit * CHUNK, CHUNK)
        grad, bias_back = mlp_section(
            chunk_ref[0, 0], normed_ref[...], upstream_ref[...],
            bias_ref[0:1, pl.ds(start, CHUNK)], out_ref, back_ref,
        )
        grad_chunk_ref[0, 0] = grad
        bias_back_ref[0:1, pl.ds(start, CHUNK)] = bias_back

    @pl.when(index == PAIRS + 2 * CHUNKS - 1)
    def _():
        finish_input(tokens_ref, gains_ref, upstream_ref, back_ref, gains_back_ref)


def local_block(length, tokens, cotangent, gains, bias, pair_weights, chunk_weights):
    slots = tokens.shape[0]
    steps = PAIRS + 2 * CHUNKS
    whole = lambda shape: pl.BlockSpec(shape, lambda index: (0,) * len(shape))
    pair_at = lambda index: (jnp.maximum(index - 2 * CHUNKS, 0), 0, 0, 0)

    def chunk_at(index):
        flat = jnp.clip(index - 1, 0, 2 * CHUNKS - 1)
        return (flat // 2, lax.rem(flat, 2), 0, 0)

    pair_spec = pl.BlockSpec((1, 2, D, 4 * PAIR), pair_at)
    chunk_spec = pl.BlockSpec((1, 1, D, 2 * CHUNK), chunk_at)
    return pl.pallas_call(
        local_kernel,
        grid=(steps,),
        in_specs=[
            pl.BlockSpec(memory_space=pltpu.SMEM),
            whole((slots, D)), whole((slots, D)), whole((3, D)), whole((1, FF)), pair_spec, chunk_spec,
        ],
        out_specs=[
            whole((slots, D)), whole((slots, D)), pair_spec, chunk_spec, whole((1, FF)), whole((3, D)),
        ],
        out_shape=[
            jax.ShapeDtypeStruct((slots, D), F32),
            jax.ShapeDtypeStruct((slots, D), F32),
            jax.ShapeDtypeStruct((PAIRS, 2, D, 4 * PAIR), BF),
            jax.ShapeDtypeStruct((CHUNKS, 2, D, 2 * CHUNK), BF),
            jax.ShapeDtypeStruct((1, FF), F32),
            jax.ShapeDtypeStruct((3, D), F32),
        ],
        scratch_shapes=[pltpu.VMEM((slots, D), BF), pltpu.VMEM((slots, D), BF)],
        compiler_params=pltpu.CompilerParams(vmem_limit_bytes=60 << 20),
        name="local_block",
    )(length, tokens, cotangent, gains, bias, pair_weights, chunk_weights)


PAIR_UNITS = (0, 1, 5)
CHUNK_UNITS = (2, 3, 4)
UNITS = 6
SECTIONS = PAIRS + 2 * CHUNKS
FIRST_CHUNK = 2
LAST_PAIR = SECTIONS - 1
GATHER_COPIES = 11
SCATTER_COPIES = 8
MESH = pl.DeviceIdType.MESH


class Traffic:
    def __init__(self, refs):
        self.__dict__.update(refs)
        self.deep = self.pair.shape[2]
        self.h = lax.axis_index("heads")
        wide = lax.axis_index("wide")
        self.c = lax.rem(wide, 2)
        self.b = lax.rem(wide // 2, 2)
        self.a = wide // 4

    def buffer(self, unit):
        if unit in PAIR_UNITS:
            return self.pair.at[PAIR_UNITS.index(unit)]
        return self.chunk.at[CHUNK_UNITS.index(unit)]

    def own(self, unit):
        if unit in PAIR_UNITS:
            return self.pair_own.at[PAIR_UNITS.index(unit)]
        return self.chunk_own.at[CHUNK_UNITS.index(unit)]

    def landing(self, unit, stage):
        if unit in PAIR_UNITS:
            return self.pair_landing[stage].at[PAIR_UNITS.index(unit)]
        return self.chunk_landing[stage].at[CHUNK_UNITS.index(unit)]

    def device(self, h=None, a=None, b=None, c=None):
        h = self.h if h is None else h
        a = self.a if a is None else a
        b = self.b if b is None else b
        c = self.c if c is None else c
        return (h, (a * 2 + b) * 2 + c)

    def beside(self, axis):
        if axis == "h":
            return self.device(h=1 - self.h)
        if axis == "b":
            return self.device(b=1 - self.b)
        return self.device(c=1 - self.c)

    def along(self, step):
        return self.device(a=lax.rem(self.a + step, self.deep))

    def copy(self, source, target, sems, unit, slot, device):
        send, recv = sems
        return pltpu.make_async_remote_copy(
            src_ref=source, dst_ref=target, send_sem=send.at[unit, slot], recv_sem=recv.at[unit, slot],
            device_id=device, device_id_type=MESH,
        )

    def gather_copy(self, unit, slot):
        buf, own, half = self.buffer(unit), self.own(unit), self.deep // 2
        h, a, b, c = self.h, self.a, self.b, self.c
        if slot < self.deep - 1:
            return self.copy(own, buf.at[h, a, b, c], self.gather_sems, unit, slot, self.along(slot + 1))
        slot -= self.deep - 1
        region, device = (
            (lambda r: r.at[h, :, b, c], self.beside("h")),
            (lambda r: r.at[h, :, b, c], self.beside("b")),
            (lambda r: r.at[1 - h, pl.ds(0, half), b, c], self.beside("b")),
            (lambda r: r.at[h, pl.ds(half, self.deep - half), 1 - b, c], self.beside("h")),
            (lambda r: r.at[h, :, b, c], self.beside("c")),
            (lambda r: r.at[1 - h, :, b, c], self.beside("c")),
            (lambda r: r.at[h, :, 1 - b, c], self.beside("c")),
            (lambda r: r.at[1 - h, :, 1 - b, c], self.beside("c")),
        )[slot]
        return self.copy(
            region(buf), region(buf), self.gather_sems, unit, slot + self.deep - 1, device
        )

    def gather_start(self, unit, slots):
        for slot in slots:
            self.gather_copy(unit, slot).start()

    def gather_wait(self, unit, slots):
        for slot in slots:
            self.gather_copy(unit, slot).wait_recv()

    def local_copy(self, unit):
        return pltpu.make_async_copy(
            self.own(unit), self.buffer(unit).at[self.h, self.a, self.b, self.c], self.local_sem.at[unit]
        )

    def gather_deep(self, unit):
        self.gather_start(unit, range(self.deep - 1))
        self.local_copy(unit).start()

    def gather_sides(self, unit):
        n = self.deep - 1
        self.local_copy(unit).wait()
        self.gather_wait(unit, range(n))
        self.gather_start(unit, (n, n + 1, n + 4))

    def gather_forward(self, unit):
        n = self.deep - 1
        self.gather_wait(unit, (n, n + 1))
        self.gather_start(unit, (n + 2, n + 3, n + 5, n + 6))

    def gather_core(self, unit):
        n = self.deep - 1
        self.gather_wait(unit, (n + 2, n + 3))
        self.gather_start(unit, (n + 7,))

    def gather_done(self, unit):
        n = self.deep - 1
        self.gather_wait(unit, range(n + 4, n + 8))
        for slot in range(n + 8):
            self.gather_copy(unit, slot).wait_send()

    def scatter_copy(self, unit, slot):
        buf, half = self.buffer(unit), self.deep // 2
        h, a, b, c = self.h, self.a, self.b, self.c
        land = lambda stage: self.landing(unit, stage)
        rest = self.deep - half
        if slot >= 5:
            step = slot - 4
            source = buf.at[h, lax.rem(a + step, self.deep), b, c]
            target, device = land(3).at[step - 1], self.along(step)
        else:
            source, target, device = (
                lambda: (buf.at[:, :, :, 1 - c], land(0), self.beside("c")),
                lambda: (buf.at[1 - h, pl.ds(0, half), 1 - b, c], land(1).at[pl.ds(0, half)], self.beside("b")),
                lambda: (buf.at[1 - h, pl.ds(half, rest), 1 - b, c], land(1).at[pl.ds(half, rest)], self.beside("h")),
                lambda: (buf.at[1 - h, :, b, c], land(2).at[0], self.beside("h")),
                lambda: (buf.at[h, :, 1 - b, c], land(2).at[1], self.beside("b")),
            )[slot]()
        return self.copy(source, target, self.scatter_sems, unit, slot, device)

    def scatter_start(self, unit, slots):
        for slot in slots:
            self.scatter_copy(unit, slot).start()

    def scatter_wait(self, unit, slots):
        for slot in slots:
            self.scatter_copy(unit, slot).wait_recv()

    def add(self, unit, where, *parts):
        buf = self.buffer(unit)
        total = buf[where].astype(F32)
        for part in parts:
            total = total + part.astype(F32)
        buf[where] = total.astype(BF)

    def scatter_core(self, unit):
        self.scatter_start(unit, (0,))

    def scatter_far(self, unit):
        h, b, c = self.h, self.b, self.c
        self.scatter_wait(unit, (0,))
        got = self.landing(unit, 0)
        far = (1 - h, slice(None), 1 - b)
        self.add(unit, far + (c,), got[far])
        self.scatter_start(unit, (1, 2))
        for near in ((1 - h, slice(None), b), (h, slice(None), 1 - b), (h, slice(None), b)):
            self.add(unit, near + (c,), got[near])

    def scatter_sides(self, unit):
        h, b, c, half = self.h, self.b, self.c, self.deep // 2
        self.scatter_wait(unit, (1, 2))
        got = self.landing(unit, 1)
        self.add(unit, (1 - h, slice(0, half), b, c), got[0:half])
        self.add(unit, (h, slice(half, self.deep), 1 - b, c), got[half : self.deep])
        self.scatter_start(unit, (3, 4))

    def scatter_deep(self, unit):
        self.scatter_wait(unit, (3, 4))
        got = self.landing(unit, 2)
        self.add(unit, (self.h, slice(None), self.b, self.c), got[0], got[1])
        self.scatter_start(unit, range(5, 4 + self.deep))

    def scatter_done(self, unit):
        self.scatter_wait(unit, range(5, 4 + self.deep))
        got = self.landing(unit, 3)
        total = self.buffer(unit)[self.h, self.a, self.b, self.c].astype(F32)
        for step in range(self.deep - 1):
            total = total + got[step].astype(F32)
        if unit in PAIR_UNITS:
            self.pair_sum[PAIR_UNITS.index(unit)] = total
        else:
            self.chunk_sum[CHUNK_UNITS.index(unit)] = total
        self.squares[...] += jnp.full(self.squares.shape, jnp.sum(total * total), F32)
        for slot in range(4 + self.deep):
            self.scatter_copy(unit, slot).wait_send()

    def everyone(self, act):
        wides = lax.axis_size("wide")
        count = wides * lax.axis_size("heads")
        me = self.h * wides + lax.axis_index("wide")

        def one(step, carry):
            flat = lax.rem(me + step, count)
            act(flat, (flat // wides, lax.rem(flat, wides)))
            return carry

        lax.fori_loop(1, count, one, 0)

    def small_copy(self, place, source, target, device):
        send, recv = self.small_sems
        return pltpu.make_async_remote_copy(
            src_ref=source, dst_ref=target, send_sem=send.at[place], recv_sem=recv.at[place],
            device_id=device, device_id_type=MESH,
        )

    def small_send(self, place, source_of, target):
        me = self.h * lax.axis_size("wide") + lax.axis_index("wide")
        self.everyone(
            lambda flat, device: self.small_copy(place, source_of(flat), target.at[me], device).start()
        )
        pltpu.make_async_copy(source_of(me), target.at[me], self.small_local.at[place]).start()

    def small_wait(self, place, source_of, target):
        me = self.h * lax.axis_size("wide") + lax.axis_index("wide")
        others = pl.ds(0, target.shape[0] - 1)
        whole = self.small_copy(place, target.at[others], target.at[others], self.beside("c"))
        whole.wait_recv()
        whole.wait_send()
        pltpu.make_async_copy(source_of(me), target.at[me], self.small_local.at[place]).wait()


def spread_matrix(lanes, width, period):
    lane = lax.broadcasted_iota(jnp.int32, (lanes, width), 0).astype(F32)
    column = lax.broadcasted_iota(jnp.int32, (lanes, width), 1).astype(F32)
    place = column - period * jnp.floor((column + 0.5) * (1.0 / period))
    return jnp.where(place == lane, 1.0, 0.0).astype(BF)


def owner_mask(count, width, period):
    owner = lax.broadcasted_iota(jnp.int32, (count, width), 0) * period
    column = lax.broadcasted_iota(jnp.int32, (count, width), 1)
    return (column >= owner) & (column < owner + period)


def split_dot(values, exact, right_dim):
    high = values.astype(BF)
    rest = values - high.astype(F32)
    middle = rest.astype(BF)
    last = (rest - middle.astype(F32)).astype(BF)
    return dot(high, exact, 1, right_dim) + dot(middle, exact, 1, right_dim) + dot(last, exact, 1, right_dim)


def step_kernel(
    length_ref, tokens_ref, cotangent_ref, small_ref, pair_own_ref, chunk_own_ref,
    block_ref, gradient_ref, pair_sum_ref, chunk_sum_ref, extra_ref, total_ref,
    pair_ref, chunk_ref, pair_land0, pair_land1, pair_land2, pair_land3,
    chunk_land0, chunk_land1, chunk_land2, chunk_land3,
    normed_ref, upstream_ref, out_ref, back_ref, gains_ref, bias_ref, gains_back_ref, bias_back_ref,
    smalls_ref, extra_send_ref, extras_ref, norm_ref, norms_ref, squares_ref,
    gather_send, gather_recv, scatter_send, scatter_recv, local_sem, small_send, small_recv, small_local,
    load_sem,
):
    t = Traffic(
        dict(
            pair=pair_ref, chunk=chunk_ref, pair_own=pair_own_ref, chunk_own=chunk_own_ref,
            pair_landing=(pair_land0, pair_land1, pair_land2, pair_land3),
            chunk_landing=(chunk_land0, chunk_land1, chunk_land2, chunk_land3),
            pair_sum=pair_sum_ref, chunk_sum=chunk_sum_ref, squares=squares_ref,
            gather_sems=(gather_send, gather_recv), scatter_sems=(scatter_send, scatter_recv),
            local_sem=local_sem, small_sems=(small_send, small_recv), small_local=small_local,
        )
    )
    slots = normed_ref.shape[0]
    devices = smalls_ref.shape[0]
    gain_width, bias_width = D // devices, FF // devices
    load_tokens = lambda: pltpu.make_async_copy(tokens_ref, normed_ref, load_sem.at[0])
    load_cotangent = lambda: pltpu.make_async_copy(cotangent_ref, upstream_ref, load_sem.at[1])
    load_tokens().start()
    load_cotangent().start()
    barrier = pltpu.get_barrier_semaphore()
    t.everyone(
        lambda flat, device: pl.semaphore_signal(barrier, inc=1, device_id=device, device_id_type=MESH)
    )
    pl.semaphore_wait(barrier, devices - 1)

    t.gather_deep(0)
    small_of = lambda flat: small_ref
    t.small_send(0, small_of, smalls_ref)
    squares_ref[...] = jnp.zeros_like(squares_ref)
    extra_send_ref[...] = jnp.zeros_like(extra_send_ref)
    load_cotangent().wait()
    load_tokens().wait()

    def prepare(rows):
        upstream_ref[rows, :] = jnp.where(
            below(length_ref, rows), upstream_ref[rows, :].astype(F32), 0.0
        ).astype(BF)
        inputs = normed_ref[rows, :].astype(F32)
        out_ref[rows, :] = inputs
        back_ref[rows, :], _ = row_norm(inputs)

    over_rows(slots, prepare)
    t.gather_sides(0)
    t.gather_deep(1)
    t.small_wait(0, small_of, smalls_ref)
    gain_spread = spread_matrix(128, D, gain_width)
    gain_owner = owner_mask(devices, D, gain_width)
    for row in range(3):
        spread = split_dot(smalls_ref[:, row, :], gain_spread, 0)
        gains_ref[row : row + 1, :] = jnp.sum(jnp.where(gain_owner, spread, 0.0), axis=0, keepdims=True)
    bias_spread = spread_matrix(128, FF, bias_width)
    bias_owner = owner_mask(devices, FF, bias_width)
    spread = dot(smalls_ref[:, 3, :].astype(BF), bias_spread, 1, 0)
    bias_ref[...] = jnp.sum(jnp.where(bias_owner, spread, 0.0), axis=0, keepdims=True)
    t.gather_forward(0)

    def scale(rows):
        normed_ref[rows, :] = (back_ref[rows, :] * gains_ref[0:1, :]).astype(BF)
        back_ref[rows, :] = jnp.zeros_like(back_ref[rows, :])

    over_rows(slots, scale)
    t.gather_core(0)
    t.gather_sides(1)
    t.gather_deep(2)
    t.gather_done(0)

    events = {
        (0, 0): [(t.gather_forward, 1)],
        (0, 1): [(t.gather_core, 1), (t.gather_sides, 2), (t.gather_deep, 3)],
        (0, 2): [(t.gather_forward, 2)],
        (1, -1): [(t.gather_done, 1), (t.scatter_core, 0)],
        (1, 0): [(t.gather_core, 2), (t.gather_sides, 3), (t.gather_deep, 4)],
        (1, 1): [(t.gather_forward, 3), (t.scatter_far, 0)],
        (1, 2): [(t.gather_core, 3), (t.gather_sides, 4), (t.gather_deep, 5), (t.scatter_sides, 0)],
        (2, -1): [(t.gather_done, 2), (t.scatter_core, 1), (t.gather_forward, 4)],
        (3, -1): [(t.scatter_deep, 0), (t.scatter_far, 1), (t.gather_core, 4), (t.gather_sides, 5)],
        (4, -1): [(t.gather_done, 3), (t.scatter_core, 2), (t.scatter_done, 0), (t.scatter_sides, 1), (t.gather_forward, 5)],
        (5, -1): [(t.scatter_far, 2), (t.scatter_deep, 1), (t.gather_core, 5)],
        (6, -1): [(t.gather_done, 4), (t.scatter_core, 3), (t.scatter_done, 1)],
        (7, -1): [(t.scatter_sides, 2), (t.scatter_far, 3)],
        (8, -1): [(t.gather_done, 5), (t.scatter_core, 4), (t.scatter_deep, 2), (t.scatter_sides, 3)],
        (8, 0): [(t.scatter_far, 4)],
        (8, 1): [(t.scatter_done, 2), (t.scatter_deep, 3), (t.scatter_sides, 4)],
        (8, 2): [(t.scatter_done, 3), (t.scatter_deep, 4)],
    }

    def run(index, place, sections):
        for section in sections:
            if (section, place) in events:

                @pl.when(index == section)
                def _():
                    for act, unit in events[section, place]:
                        act(unit)

    def step(index, carry):
        is_pair = (index < FIRST_CHUNK) | (index == LAST_PAIR)
        pair_sections = tuple(range(FIRST_CHUNK)) + (LAST_PAIR,)
        chunk_sections = range(FIRST_CHUNK, LAST_PAIR)

        @pl.when(is_pair)
        def _():
            run(index, -1, pair_sections)
            unit = jnp.where(index == LAST_PAIR, PAIRS - 1, index)
            starts = [pl.multiple_of(half * HALF_E + unit * PAIR, PAIR) for half in range(2)]
            gain_of = lambda row: jnp.concatenate(
                [gains_ref[row : row + 1, pl.ds(start, PAIR)] for start in starts], axis=1
            )
            grads, query_back, key_back = attention_section(
                pair_ref[unit, 0].reshape(D, 4 * PAIR), pair_ref[unit, 1].reshape(D, 4 * PAIR),
                normed_ref[...], upstream_ref[...], gain_of(1), gain_of(2),
                jnp.where(below(length_ref, pl.ds(0, slots)), 0.0, MASKED), out_ref, back_ref,
                lambda place: run(index, place, pair_sections),
            )
            for half in range(2):
                pair_ref[unit, half] = grads[half].reshape(pair_ref.shape[2:])
                cut = slice(half * PAIR, (half + 1) * PAIR)
                gains_back_ref[1:2, pl.ds(starts[half], PAIR)] = query_back[:, cut]
                gains_back_ref[2:3, pl.ds(starts[half], PAIR)] = key_back[:, cut]

        @pl.when(~is_pair)
        def _():
            run(index, -1, chunk_sections)
            unit = (index - FIRST_CHUNK) // 2
            half = lax.rem(index - FIRST_CHUNK, 2)
            start = pl.multiple_of(half * HALF_F + unit * CHUNK, CHUNK)
            grad, bias_back = mlp_section(
                chunk_ref[unit, half].reshape(D, 2 * CHUNK), normed_ref[...], upstream_ref[...],
                bias_ref[0:1, pl.ds(start, CHUNK)], out_ref, back_ref,
            )
            chunk_ref[unit, half] = grad.reshape(chunk_ref.shape[2:])
            bias_back_ref[0:1, pl.ds(start, CHUNK)] = bias_back

        return carry

    lax.fori_loop(0, SECTIONS, step, 0)
    t.scatter_core(5)
    load_tokens().start()
    store_block = pltpu.make_async_copy(out_ref, block_ref, load_sem.at[2])
    store_block.start()
    t.scatter_far(5)
    load_tokens().wait()
    finish_input(normed_ref, gains_ref, upstream_ref, back_ref, gains_back_ref)
    store_gradient = pltpu.make_async_copy(back_ref, gradient_ref, load_sem.at[3])
    store_gradient.start()
    t.scatter_sides(5)
    for row in range(3):
        rows = jnp.where(gain_owner, gains_back_ref[row : row + 1, :], 0.0)
        extra_send_ref[:, row, :] = split_dot(rows, gain_spread, 1)
    rows = jnp.where(bias_owner, bias_back_ref[...], 0.0)
    extra_send_ref[:, 3, :] = split_dot(rows, bias_spread, 1)
    extra_of = lambda flat: extra_send_ref.at[flat]
    t.small_send(1, extra_of, extras_ref)
    t.scatter_done(4)
    t.scatter_deep(5)
    t.small_wait(1, extra_of, extras_ref)
    extra = jnp.sum(extras_ref[...], axis=0)
    extra_ref[...] = extra
    t.scatter_done(5)
    norm_ref[...] = squares_ref[...] + jnp.full(squares_ref.shape, jnp.sum(extra * extra), F32)
    norm_of = lambda flat: norm_ref
    t.small_send(2, norm_of, norms_ref)
    store_block.wait()
    store_gradient.wait()
    t.small_wait(2, norm_of, norms_ref)
    total_ref[...] = jnp.sum(norms_ref[...], axis=0)


def exchanged_block(lengths, tokens, cotangent, norm_gains, expand_bias, pair_own, chunk_own):
    slots = tokens.shape[0]
    wides = lax.axis_size("wide")
    devices = wides * lax.axis_size("heads")
    deep = wides // 4
    rows = pair_own.shape[1]
    small = jnp.concatenate(
        [
            jnp.pad(norm_gains, ((0, 0), (0, 128 - norm_gains.shape[1]))),
            jnp.pad(expand_bias.astype(BF).astype(F32)[None], ((0, 4), (0, 128 - expand_bias.shape[0]))),
        ],
        axis=0,
    )
    vmem = pl.BlockSpec(memory_space=pltpu.VMEM)
    hbm = pl.BlockSpec(memory_space=pl.ANY)
    landings = lambda units, width: [
        pltpu.VMEM((units, 2, deep, 2, rows, width), BF),
        pltpu.VMEM((units, deep, rows, width), BF),
        pltpu.VMEM((units, 2, deep, rows, width), BF),
        pltpu.VMEM((units, deep - 1, rows, width), BF),
    ]
    tile = pltpu.VMEM((8, 128), F32)
    tiles = pltpu.VMEM((devices, 8, 128), F32)
    dma = pltpu.SemaphoreType.DMA
    gather_slots, scatter_slots = deep + 7, deep + 4
    block_output, token_gradient, pair_sum, chunk_sum, extra, total = pl.pallas_call(
        step_kernel,
        in_specs=[pl.BlockSpec(memory_space=pltpu.SMEM), hbm, hbm, vmem, hbm, hbm],
        out_specs=[hbm, hbm, vmem, vmem, vmem, vmem],
        out_shape=[
            jax.ShapeDtypeStruct((slots, D), F32),
            jax.ShapeDtypeStruct((slots, D), F32),
            jax.ShapeDtypeStruct((PAIRS, rows, 4 * PAIR), F32),
            jax.ShapeDtypeStruct((CHUNKS, rows, 2 * CHUNK), F32),
            jax.ShapeDtypeStruct((8, 128), F32),
            jax.ShapeDtypeStruct((8, 128), F32),
        ],
        scratch_shapes=[
            pltpu.VMEM((PAIRS, 2, deep, 2, 2, rows, 4 * PAIR), BF),
            pltpu.VMEM((CHUNKS, 2, deep, 2, 2, rows, 2 * CHUNK), BF),
        ]
        + landings(PAIRS, 4 * PAIR)
        + landings(CHUNKS, 2 * CHUNK)
        + [
            pltpu.VMEM((slots, D), BF), pltpu.VMEM((slots, D), BF),
            pltpu.VMEM((slots, D), F32), pltpu.VMEM((slots, D), F32),
            pltpu.VMEM((3, D), F32), pltpu.VMEM((1, FF), F32),
            pltpu.VMEM((3, D), F32), pltpu.VMEM((1, FF), F32),
            tiles, tiles, tiles, tile, tiles, tile,
            dma((UNITS, gather_slots)), dma((UNITS, gather_slots)),
            dma((UNITS, scatter_slots)), dma((UNITS, scatter_slots)),
            dma((UNITS,)), dma((3,)), dma((3,)), dma((3,)), dma((4,)),
        ],
        compiler_params=pltpu.CompilerParams(
            vmem_limit_bytes=67043328, collective_id=0, has_side_effects=True
        ),
        name="step_block",
    )(lengths, tokens, cotangent, small, pair_own, chunk_own)
    grads = unpack_shards(pair_sum, chunk_sum) + (
        extra[3, : expand_bias.shape[0]],
        extra[:3, : norm_gains.shape[1]],
    )
    return block_output, token_gradient, grads, total[0, 0]


def optimizer_update(
    weight, raw_grad, factor, first, second, average, rate, decay, first_fix, second_fix, keep
):
    clipped = raw_grad * factor
    first_new = BETA_FIRST * first + (1.0 - BETA_FIRST) * clipped
    second_new = BETA_SECOND * second + (1.0 - BETA_SECOND) * clipped * clipped
    direction = first_new / first_fix / (jnp.sqrt(second_new / second_fix) + ADAM_EPS)
    weight_new = weight - rate * (direction + decay * weight)
    average_new = keep * average + (1.0 - keep) * weight_new
    return (clipped, first_new, second_new, weight_new, average_new)


def pack_shards(attend_weights, output_weights, expand_weights, reduce_weights):
    rows = attend_weights.shape[1]
    attend = attend_weights.astype(BF).reshape(3, rows, PAIRS, PAIR)
    attend = jnp.transpose(attend, (2, 1, 0, 3)).reshape(PAIRS, rows, 3 * PAIR)
    output = jnp.transpose(
        output_weights.astype(BF).T.reshape(rows, PAIRS, PAIR), (1, 0, 2)
    )
    expand = jnp.transpose(expand_weights.astype(BF).reshape(rows, CHUNKS, CHUNK), (1, 0, 2))
    reduce = jnp.transpose(reduce_weights.astype(BF).T.reshape(rows, CHUNKS, CHUNK), (1, 0, 2))
    return jnp.concatenate([attend, output], axis=2), jnp.concatenate([expand, reduce], axis=2)


def unpack_shards(pair_grads, chunk_grads):
    rows = pair_grads.shape[1]
    attend = jnp.transpose(
        pair_grads[:, :, : 3 * PAIR].reshape(PAIRS, rows, 3, PAIR), (2, 1, 0, 3)
    ).reshape(3, rows, HALF_E)
    join = lambda part: jnp.transpose(part, (1, 0, 2)).reshape(rows, -1)
    return (
        attend,
        join(pair_grads[:, :, 3 * PAIR :]).T,
        join(chunk_grads[:, :, :CHUNK]),
        join(chunk_grads[:, :, CHUNK:]).T,
    )


def gathered_block(lengths, tokens, cotangent, norm_gains, expand_bias, pair_own, chunk_own):
    both = ("heads", "wide")
    gains = lax.all_gather(norm_gains, both, axis=1, tiled=True)
    bias = lax.all_gather(expand_bias.astype(BF), both, axis=0, tiled=True).astype(F32)
    whole = lambda own: lax.all_gather(
        lax.all_gather(own, "wide", axis=1, tiled=True), "heads", axis=1
    )
    block_output, token_gradient, pair_grads, chunk_grads, bias_back, gains_back = local_block(
        lengths, tokens, cotangent, gains, bias[None, :], whole(pair_own), whole(chunk_own)
    )
    scatter = lambda part: lax.psum_scatter(
        lax.psum_scatter(part, "heads", scatter_dimension=1),
        "wide", scatter_dimension=1, tiled=True,
    ).astype(F32)
    grads = unpack_shards(scatter(pair_grads), scatter(chunk_grads)) + (
        lax.psum_scatter(bias_back[0], both, scatter_dimension=0, tiled=True),
        lax.psum_scatter(gains_back, both, scatter_dimension=1, tiled=True),
    )
    squares = jnp.sum(jnp.stack([jnp.sum(entry * entry) for entry in grads]))
    return block_output, token_gradient, grads, lax.psum(squares, both)


def body(
    tokens, cotangent, lengths, step_count,
    attend_weights, output_weights, expand_weights, reduce_weights, expand_bias, norm_gains,
    *moments,
):
    masters = (
        attend_weights, output_weights, expand_weights, reduce_weights, expand_bias, norm_gains,
    )
    firsts, seconds, averages = moments[:6], moments[6:12], moments[12:]
    pair_own, chunk_own = pack_shards(*masters[:4])
    wides = lax.axis_size("wide")
    aligned = wides % 8 == 0 and pair_own.shape[1] % 16 == 0 and lax.axis_size("heads") == 2
    block_output, token_gradient, grads, total_squares = (exchanged_block if aligned else gathered_block)(
        lengths, tokens[0], cotangent[0], norm_gains, expand_bias, pair_own, chunk_own
    )
    grad_norm = jnp.sqrt(total_squares)
    tokens_all = tokens.shape[1] * lax.axis_size("heads") * lax.axis_size("wide")
    limit = 0.02 * math.sqrt(tokens_all * D * FF)
    factor = jnp.minimum(1.0, limit / grad_norm)
    step_float = step_count[0].astype(F32)
    first_fix = 1.0 - jnp.power(BETA_FIRST, step_float)
    second_fix = 1.0 - jnp.power(BETA_SECOND, step_float)
    keep = jnp.minimum(AVERAGE_CAP, (1.0 + step_float) / (10.0 + step_float))
    results = [block_output[None], token_gradient[None], grad_norm.reshape(1)]
    for index in range(6):
        results.extend(
            optimizer_update(
                masters[index], grads[index], factor, firsts[index], seconds[index],
                averages[index], RATES[index], DECAYS[index], first_fix, second_fix, keep,
            )
        )
    return tuple(results)


def solution(mesh):
    both = ("heads", "wide")
    weight_specs = (
        P(None, "wide", "heads"), P("heads", "wide"), P("wide", "heads"), P("heads", "wide"),
        P(both), P(None, both),
    )
    image = P(both, None, None)
    return jax.shard_map(
        body,
        mesh=mesh,
        in_specs=(image, image, P(both), P()) + weight_specs * 4,
        out_specs=(image, image, P()) + tuple(spec for spec in weight_specs for _ in range(5)),
        check_vma=False,
    )
```

```python
from functools import partial
import math

import jax
import jax.numpy as jnp
from jax import lax
from jax.experimental import pallas as pl
from jax.experimental.pallas import tpu as pltpu
from jax.sharding import PartitionSpec as P

D = 768
HEADS = 12
HEAD_DIM = 64
FF = 3072
HALF_E = D // 2
HALF_F = FF // 2
PAIR = 128
PAIRS = HALF_E // PAIR
CHUNK = 512
CHUNKS = HALF_F // CHUNK
QUERY_ROWS = 512
ROWS = 256
BF = jnp.bfloat16
F32 = jnp.float32

NORM_EPS = 1e-06
MASKED = -1e30
BETA_FIRST = 0.9
BETA_SECOND = 0.95
AVERAGE_CAP = 0.9999
ADAM_EPS = 1e-08
RATES = (0.03, 0.2, 0.03, 0.015, 0.3, 0.3)
DECAYS = (0.05, 0.05, 0.05, 0.05, 0.0, 0.0)


def dot(left, right, left_dim, right_dim):
    return lax.dot_general(
        left, right, (((left_dim,), (right_dim,)), ((), ())), preferred_element_type=F32
    )


def row_norm(values):
    center = values - jnp.mean(values, axis=-1, keepdims=True)
    inverse = lax.rsqrt(jnp.mean(center * center, axis=-1, keepdims=True) + NORM_EPS)
    return center * inverse, inverse


def head_mean(values):
    width = values.shape[1]
    row = lax.broadcasted_iota(jnp.int32, (width, width), 0) // HEAD_DIM
    column = lax.broadcasted_iota(jnp.int32, (width, width), 1) // HEAD_DIM
    block = jnp.where(row == column, 1.0 / HEAD_DIM, 0.0).astype(BF)
    high = values.astype(BF)
    rest = (values - high.astype(F32)).astype(BF)
    return dot(high, block, 1, 0) + dot(rest, block, 1, 0)


def head_norm(values):
    center = values - head_mean(values)
    inverse = lax.rsqrt(head_mean(center * center) + NORM_EPS)
    return center * inverse, inverse


def head_norm_back(upstream, normal, inverse):
    return inverse * (upstream - head_mean(upstream) - normal * head_mean(upstream * normal))


def pair_attention(query, keyed, value, back_mixed, key_bias):
    rows = query.shape[0]
    lane = lax.broadcasted_iota(jnp.int32, (rows, PAIR), 1)
    low = lane < HEAD_DIM
    first = lane == 0
    zero = jnp.zeros((rows, PAIR), BF)
    one_lane = jnp.where(first, 1.0, 0.0).astype(BF)
    bias_lane = jnp.where(first, key_bias, 0.0).astype(BF)
    query_wide = jnp.concatenate([query, one_lane], axis=1)
    value_wide = jnp.concatenate([value, jnp.ones((rows, PAIR), BF)], axis=1)
    blocks = rows // QUERY_ROWS
    mixed = [[None] * blocks for _ in range(2)]
    back_query = [[None] * blocks for _ in range(2)]
    back_keyed = None
    back_value = None
    lane_q = lane[:QUERY_ROWS]
    low_q = low[:QUERY_ROWS]
    for head in range(2):
        mine = low if head == 0 else ~low
        mine_q = mine[:QUERY_ROWS]
        key_wide = jnp.concatenate([jnp.where(mine, keyed, zero), bias_lane], axis=1)
        query_mine = jnp.where(mine, query, zero)
        for block in range(blocks):
            cut = slice(block * QUERY_ROWS, (block + 1) * QUERY_ROWS)
            expo = jnp.exp(dot(query_wide[cut], key_wide, 1, 1))
            expo_low = expo.astype(BF)
            sums = dot(expo_low, value_wide, 1, 0)
            inverse = 1.0 / sums[:, PAIR:]
            rows_mixed = sums[:, :PAIR] * inverse
            scaled = jnp.where(mine_q, back_mixed[cut].astype(F32) * inverse, 0.0).astype(BF)
            inner = jnp.sum(rows_mixed * scaled.astype(F32), axis=1, keepdims=True)
            inner_high = inner.astype(BF).astype(F32)
            inner_lanes = jnp.where(
                lane_q == 0, -inner_high, jnp.where(lane_q == 1, inner_high - inner, 0.0)
            ).astype(BF)
            centered = dot(jnp.concatenate([scaled, inner_lanes], axis=1), value_wide, 1, 1)
            back_scores = (expo * centered).astype(BF)
            mixed[head][block] = rows_mixed
            back_query[head][block] = dot(back_scores, keyed, 1, 0)
            add_keyed = dot(query_mine[cut], back_scores, 0, 0)
            add_value = dot(scaled, expo_low, 0, 0)
            back_keyed = add_keyed if back_keyed is None else back_keyed + add_keyed
            back_value = add_value if back_value is None else back_value + add_value
    join = lambda parts: jnp.concatenate(
        [jnp.where(low_q, parts[0][block], parts[1][block]) for block in range(blocks)], axis=0
    )
    return join(mixed).astype(BF), join(back_query), back_keyed, back_value


def attention_scratch(slots):
    rows = [pltpu.VMEM((2, slots, PAIR), BF)] * 4 + [pltpu.VMEM((2, slots, PAIR), F32)] * 5
    return rows + [pltpu.VMEM((2, PAIR, slots), F32)]


def attention_section(
    weights, normed, upstream, query_gain, key_gain, key_bias, out_ref, back_ref, work, store,
    pause=lambda place: None,
):
    (
        query_ref, key_ref, value_ref, back_mixed_ref,
        query_hat_ref, query_inv_ref, key_hat_ref, key_inv_ref, back_query_ref, back_keyed_ref,
    ) = work
    three = 3 * PAIR
    halves = (slice(0, PAIR), slice(PAIR, 2 * PAIR))
    both = [weights(half) for half in range(2)]
    into = jnp.concatenate([part[:, :three] for part in both], axis=1)
    out = jnp.concatenate([part[:, three:] for part in both], axis=1)
    projected = dot(normed, into, 1, 0)
    back_mixed = dot(upstream, out, 1, 0).astype(BF)
    pick = lambda place: jnp.concatenate(
        [
            projected[:, place * PAIR : (place + 1) * PAIR],
            projected[:, three + place * PAIR : three + (place + 1) * PAIR],
        ],
        axis=1,
    )
    query_hat, query_inv = head_norm(pick(0))
    key_hat, key_inv = head_norm(pick(1))
    query = (query_hat * query_gain).astype(BF)
    query = (query.astype(F32) * HEAD_DIM ** (-0.5)).astype(BF)
    keyed = (key_hat * key_gain).astype(BF)
    value = pick(2).astype(BF)
    for half, cut in enumerate(halves):
        for ref, rows in (
            (query_ref, query), (key_ref, keyed), (value_ref, value), (back_mixed_ref, back_mixed),
            (query_hat_ref, query_hat), (query_inv_ref, query_inv),
            (key_hat_ref, key_hat), (key_inv_ref, key_inv),
        ):
            ref[half] = rows[:, cut]

    def one_pair(half, carry):
        for place in range(2):
            pl.when(half == place)(partial(pause, place))
        mixed, back_query_ref[half], back_keyed_ref[half], back_value = pair_attention(
            query_ref[half], key_ref[half], value_ref[half], back_mixed_ref[half], key_bias
        )
        query_ref[half] = mixed
        value_ref[half] = back_value.T.astype(BF)
        return carry

    lax.fori_loop(0, 2, one_pair, 0)
    pause(2)
    whole = lambda ref: jnp.concatenate([ref[0], ref[1]], axis=1)
    both = [weights(half) for half in range(2)]
    into = jnp.concatenate([part[:, :three] for part in both], axis=1)
    out = jnp.concatenate([part[:, three:] for part in both], axis=1)
    mixed = whole(query_ref)
    query_hat, key_hat = whole(query_hat_ref), whole(key_hat_ref)
    back_qn = whole(back_query_ref) * HEAD_DIM ** (-0.5)
    back_kn = jnp.concatenate([back_keyed_ref[0].T, back_keyed_ref[1].T], axis=1)
    query_gain_back = jnp.sum(back_qn * query_hat, axis=0, keepdims=True)
    key_gain_back = jnp.sum(back_kn * key_hat, axis=0, keepdims=True)
    back_query = head_norm_back(back_qn * query_gain, query_hat, whole(query_inv_ref)).astype(BF)
    back_keyed = head_norm_back(back_kn * key_gain, key_hat, whole(key_inv_ref)).astype(BF)
    back_into = jnp.concatenate(
        [
            part
            for half, cut in enumerate(halves)
            for part in (back_query[:, cut], back_keyed[:, cut], value_ref[half])
        ],
        axis=1,
    )
    grad_into = dot(normed, back_into, 0, 0).astype(BF)
    grad_out = dot(upstream, mixed, 0, 0).astype(BF)
    grads = [
        jnp.concatenate([grad_into[:, half * three : (half + 1) * three], grad_out[:, cut]], axis=1)
        for half, cut in enumerate(halves)
    ]
    store(grads, query_gain_back, key_gain_back)
    pause(3)
    out_ref[...] += dot(mixed, out, 1, 1)
    back_ref[...] += dot(back_into, into, 1, 1)


def mlp_section(weights, normed, upstream, bias, out_ref, back_ref):
    expand = weights[:, :CHUNK]
    reduce = weights[:, CHUNK:]
    pre = dot(normed, expand, 1, 0) + bias
    back_hidden = dot(upstream, reduce, 1, 0)
    phi = 0.5 * (1.0 + lax.erf(pre * math.sqrt(0.5)))
    density = jnp.exp(-0.5 * pre * pre) * (1.0 / math.sqrt(2.0 * math.pi))
    hidden = (pre * phi).astype(BF)
    back_pre = (back_hidden * (phi + pre * density)).astype(BF)
    out_ref[...] += dot(hidden, reduce, 1, 1)
    back_ref[...] += dot(back_pre, expand, 1, 1)
    grads = [dot(normed, back_pre, 0, 0).astype(BF), dot(upstream, hidden, 0, 0).astype(BF)]
    return jnp.concatenate(grads, axis=1), jnp.sum(back_pre.astype(F32), axis=0, keepdims=True)


def over_rows(slots, act):
    def one(block, carry):
        act(pl.ds(pl.multiple_of(block * ROWS, ROWS), ROWS))
        return carry

    lax.fori_loop(0, slots // ROWS, one, 0)


def below(length_ref, rows):
    place = lax.broadcasted_iota(jnp.int32, (rows.size, 1), 0) + rows.start
    return place < length_ref[0]


def start_input(
    length_ref, tokens_ref, cotangent_ref, gains_ref, normed_ref, upstream_ref, out_ref, back_ref
):
    def one(rows):
        inputs = tokens_ref[rows, :].astype(F32)
        input_hat, _ = row_norm(inputs)
        normed_ref[rows, :] = (input_hat * gains_ref[0:1, :]).astype(BF)
        upstream_ref[rows, :] = jnp.where(
            below(length_ref, rows), cotangent_ref[rows, :].astype(F32), 0.0
        ).astype(BF)
        out_ref[rows, :] = inputs
        back_ref[rows, :] = jnp.zeros_like(inputs)

    over_rows(tokens_ref.shape[0], one)


def finish_input(tokens_ref, gains_ref, upstream_ref, back_ref, gains_back_ref):
    gains_back_ref[0:1, :] = jnp.zeros_like(gains_back_ref[0:1, :])

    def one(rows):
        input_hat, input_inv = row_norm(tokens_ref[rows, :].astype(F32))
        back_normed = back_ref[rows, :]
        gains_back_ref[0:1, :] += jnp.sum(back_normed * input_hat, axis=0, keepdims=True)
        scaled = back_normed * gains_ref[0:1, :]
        back_ref[rows, :] = upstream_ref[rows, :].astype(F32) + input_inv * (
            scaled
            - jnp.mean(scaled, axis=-1, keepdims=True)
            - input_hat * jnp.mean(scaled * input_hat, axis=-1, keepdims=True)
        )

    over_rows(tokens_ref.shape[0], one)


def local_kernel(
    length_ref, tokens_ref, cotangent_ref, gains_ref, bias_ref, pair_ref, chunk_ref,
    out_ref, back_ref, grad_pair_ref, grad_chunk_ref, bias_back_ref, gains_back_ref,
    normed_ref, upstream_ref, *work,
):
    index = pl.program_id(0)

    @pl.when(index == 0)
    def _():
        start_input(
            length_ref, tokens_ref, cotangent_ref, gains_ref, normed_ref, upstream_ref, out_ref, back_ref
        )

    is_pair = (index == 0) | (index > 2 * CHUNKS)

    @pl.when(is_pair)
    def _():
        unit = jnp.where(index == 0, 0, index - 2 * CHUNKS)
        starts = [pl.multiple_of(half * HALF_E + unit * PAIR, PAIR) for half in range(2)]
        gain_of = lambda row: jnp.concatenate(
            [gains_ref[row : row + 1, pl.ds(start, PAIR)] for start in starts], axis=1
        )
        place = lax.broadcasted_iota(jnp.int32, (tokens_ref.shape[0], 1), 0)

        def store(grads, query_back, key_back):
            for half in range(2):
                grad_pair_ref[0, half] = grads[half]
                cut = slice(half * PAIR, (half + 1) * PAIR)
                gains_back_ref[1:2, pl.ds(starts[half], PAIR)] = query_back[:, cut]
                gains_back_ref[2:3, pl.ds(starts[half], PAIR)] = key_back[:, cut]

        attention_section(
            lambda half: pair_ref[0, half], normed_ref[...], upstream_ref[...],
            gain_of(1), gain_of(2), jnp.where(place < length_ref[0], 0.0, MASKED), out_ref, back_ref, work,
            store,
        )

    @pl.when(~is_pair)
    def _():
        unit = (index - 1) // 2
        half = lax.rem(index - 1, 2)
        start = pl.multiple_of(half * HALF_F + unit * CHUNK, CHUNK)
        grad, bias_back = mlp_section(
            chunk_ref[0, 0], normed_ref[...], upstream_ref[...],
            bias_ref[0:1, pl.ds(start, CHUNK)], out_ref, back_ref,
        )
        grad_chunk_ref[0, 0] = grad
        bias_back_ref[0:1, pl.ds(start, CHUNK)] = bias_back

    @pl.when(index == PAIRS + 2 * CHUNKS - 1)
    def _():
        finish_input(tokens_ref, gains_ref, upstream_ref, back_ref, gains_back_ref)


def local_block(length, tokens, cotangent, gains, bias, pair_weights, chunk_weights):
    slots = tokens.shape[0]
    steps = PAIRS + 2 * CHUNKS
    whole = lambda shape: pl.BlockSpec(shape, lambda index: (0,) * len(shape))
    pair_at = lambda index: (jnp.maximum(index - 2 * CHUNKS, 0), 0, 0, 0)

    def chunk_at(index):
        flat = jnp.clip(index - 1, 0, 2 * CHUNKS - 1)
        return (flat // 2, lax.rem(flat, 2), 0, 0)

    pair_spec = pl.BlockSpec((1, 2, D, 4 * PAIR), pair_at)
    chunk_spec = pl.BlockSpec((1, 1, D, 2 * CHUNK), chunk_at)
    return pl.pallas_call(
        local_kernel,
        grid=(steps,),
        in_specs=[
            pl.BlockSpec(memory_space=pltpu.SMEM),
            whole((slots, D)), whole((slots, D)), whole((3, D)), whole((1, FF)), pair_spec, chunk_spec,
        ],
        out_specs=[
            whole((slots, D)), whole((slots, D)), pair_spec, chunk_spec, whole((1, FF)), whole((3, D)),
        ],
        out_shape=[
            jax.ShapeDtypeStruct((slots, D), F32),
            jax.ShapeDtypeStruct((slots, D), F32),
            jax.ShapeDtypeStruct((PAIRS, 2, D, 4 * PAIR), BF),
            jax.ShapeDtypeStruct((CHUNKS, 2, D, 2 * CHUNK), BF),
            jax.ShapeDtypeStruct((1, FF), F32),
            jax.ShapeDtypeStruct((3, D), F32),
        ],
        scratch_shapes=[pltpu.VMEM((slots, D), BF), pltpu.VMEM((slots, D), BF)]
        + attention_scratch(slots),
        compiler_params=pltpu.CompilerParams(vmem_limit_bytes=60 << 20),
        name="local_block",
    )(length, tokens, cotangent, gains, bias, pair_weights, chunk_weights)


PAIR_UNITS = (0, 1, 5)
CHUNK_UNITS = (2, 3, 4)
UNITS = 6
SECTIONS = PAIRS + 2 * CHUNKS
FIRST_CHUNK = 2
LAST_PAIR = SECTIONS - 1
GATHER_COPIES = 11
SCATTER_COPIES = 8
MESH = pl.DeviceIdType.MESH


class Traffic:
    def __init__(self, refs):
        self.__dict__.update(refs)
        self.deep = self.pair.shape[2]
        self.h = lax.axis_index("heads")
        wide = lax.axis_index("wide")
        self.c = lax.rem(wide, 2)
        self.b = lax.rem(wide // 2, 2)
        self.a = wide // 4

    def buffer(self, unit):
        if unit in PAIR_UNITS:
            return self.pair.at[PAIR_UNITS.index(unit)]
        return self.chunk.at[CHUNK_UNITS.index(unit)]

    def own(self, unit):
        if unit in PAIR_UNITS:
            return self.pair_own.at[PAIR_UNITS.index(unit)]
        return self.chunk_own.at[CHUNK_UNITS.index(unit)]

    def landing(self, unit, stage):
        pair = unit in PAIR_UNITS
        landing = (self.pair_landing if pair else self.chunk_landing)[stage]
        return landing.at[(PAIR_UNITS if pair else CHUNK_UNITS).index(unit) % landing.shape[0]]

    def device(self, h=None, a=None, b=None, c=None):
        h = self.h if h is None else h
        a = self.a if a is None else a
        b = self.b if b is None else b
        c = self.c if c is None else c
        return (h, (a * 2 + b) * 2 + c)

    def beside(self, axis):
        if axis == "h":
            return self.device(h=1 - self.h)
        if axis == "b":
            return self.device(b=1 - self.b)
        return self.device(c=1 - self.c)

    def along(self, step):
        return self.device(a=lax.rem(self.a + step, self.deep))

    def copy(self, source, target, sems, unit, slot, device):
        send, recv = sems
        return pltpu.make_async_remote_copy(
            src_ref=source, dst_ref=target, send_sem=send.at[unit, slot], recv_sem=recv.at[unit, slot],
            device_id=device, device_id_type=MESH,
        )

    def gather_copy(self, unit, slot):
        buf, own, half = self.buffer(unit), self.own(unit), self.deep // 2
        h, a, b, c = self.h, self.a, self.b, self.c
        if slot < self.deep - 1:
            return self.copy(own, buf.at[h, a, b, c], self.gather_sems, unit, slot, self.along(slot + 1))
        slot -= self.deep - 1
        region, device = (
            (lambda r: r.at[h, :, b, c], self.beside("h")),
            (lambda r: r.at[h, :, b, c], self.beside("b")),
            (lambda r: r.at[1 - h, pl.ds(0, half), b, c], self.beside("b")),
            (lambda r: r.at[h, pl.ds(half, self.deep - half), 1 - b, c], self.beside("h")),
            (lambda r: r.at[h, :, b, c], self.beside("c")),
            (lambda r: r.at[1 - h, :, b, c], self.beside("c")),
            (lambda r: r.at[h, :, 1 - b, c], self.beside("c")),
            (lambda r: r.at[1 - h, :, 1 - b, c], self.beside("c")),
        )[slot]
        return self.copy(
            region(buf), region(buf), self.gather_sems, unit, slot + self.deep - 1, device
        )

    def gather_start(self, unit, slots):
        for slot in slots:
            self.gather_copy(unit, slot).start()

    def gather_wait(self, unit, slots):
        for slot in slots:
            self.gather_copy(unit, slot).wait_recv()

    def local_copy(self, unit):
        return pltpu.make_async_copy(
            self.own(unit), self.buffer(unit).at[self.h, self.a, self.b, self.c], self.local_sem.at[unit]
        )

    def gather_deep(self, unit):
        self.gather_start(unit, range(self.deep - 1))
        self.local_copy(unit).start()

    def gather_sides(self, unit):
        n = self.deep - 1
        self.local_copy(unit).wait()
        self.gather_wait(unit, range(n))
        self.gather_start(unit, (n, n + 1, n + 4))

    def gather_forward(self, unit):
        n = self.deep - 1
        self.gather_wait(unit, (n, n + 1))
        self.gather_start(unit, (n + 2, n + 3, n + 5, n + 6))

    def gather_core(self, unit):
        n = self.deep - 1
        self.gather_wait(unit, (n + 2, n + 3))
        self.gather_start(unit, (n + 7,))

    def gather_done(self, unit):
        n = self.deep - 1
        self.gather_wait(unit, range(n + 4, n + 8))
        for slot in range(n + 8):
            self.gather_copy(unit, slot).wait_send()

    def scatter_copy(self, unit, slot):
        buf, half = self.buffer(unit), self.deep // 2
        h, a, b, c = self.h, self.a, self.b, self.c
        land = lambda stage: self.landing(unit, stage)
        rest = self.deep - half
        if slot >= 5:
            step = slot - 4
            source = buf.at[h, lax.rem(a + step, self.deep), b, c]
            target, device = land(3).at[step - 1], self.along(step)
        else:
            source, target, device = (
                lambda: (buf.at[:, :, :, 1 - c], land(0), self.beside("c")),
                lambda: (buf.at[1 - h, pl.ds(0, half), 1 - b, c], land(1).at[pl.ds(0, half)], self.beside("b")),
                lambda: (buf.at[1 - h, pl.ds(half, rest), 1 - b, c], land(1).at[pl.ds(half, rest)], self.beside("h")),
                lambda: (buf.at[1 - h, :, b, c], land(2).at[0], self.beside("h")),
                lambda: (buf.at[h, :, 1 - b, c], land(2).at[1], self.beside("b")),
            )[slot]()
        return self.copy(source, target, self.scatter_sems, unit, slot, device)

    def scatter_start(self, unit, slots):
        for slot in slots:
            self.scatter_copy(unit, slot).start()

    def scatter_wait(self, unit, slots):
        for slot in slots:
            self.scatter_copy(unit, slot).wait_recv()

    def add(self, unit, where, *parts):
        buf = self.buffer(unit)
        total = buf[where].astype(F32)
        for part in parts:
            total = total + part.astype(F32)
        buf[where] = total.astype(BF)

    def scatter_core(self, unit):
        self.scatter_start(unit, (0,))

    def scatter_far(self, unit):
        h, b, c = self.h, self.b, self.c
        self.scatter_wait(unit, (0,))
        got = self.landing(unit, 0)
        far = (1 - h, slice(None), 1 - b)
        self.add(unit, far + (c,), got[far])
        self.scatter_start(unit, (1, 2))
        for near in ((1 - h, slice(None), b), (h, slice(None), 1 - b), (h, slice(None), b)):
            self.add(unit, near + (c,), got[near])

    def scatter_sides(self, unit):
        h, b, c, half = self.h, self.b, self.c, self.deep // 2
        self.scatter_wait(unit, (1, 2))
        got = self.landing(unit, 1)
        self.add(unit, (1 - h, slice(0, half), b, c), got[0:half])
        self.add(unit, (h, slice(half, self.deep), 1 - b, c), got[half : self.deep])
        self.scatter_start(unit, (3, 4))

    def scatter_deep(self, unit):
        self.scatter_wait(unit, (3, 4))
        got = self.landing(unit, 2)
        self.add(unit, (self.h, slice(None), self.b, self.c), got[0], got[1])
        self.scatter_start(unit, range(5, 4 + self.deep))

    def scatter_done(self, unit):
        self.scatter_wait(unit, range(5, 4 + self.deep))
        got = self.landing(unit, 3)
        total = self.buffer(unit)[self.h, self.a, self.b, self.c].astype(F32)
        for step in range(self.deep - 1):
            total = total + got[step].astype(F32)
        if unit in PAIR_UNITS:
            self.pair_sum[PAIR_UNITS.index(unit)] = total
        else:
            self.chunk_sum[CHUNK_UNITS.index(unit)] = total
        self.squares[...] += jnp.full(self.squares.shape, jnp.sum(total * total), F32)
        for slot in range(4 + self.deep):
            self.scatter_copy(unit, slot).wait_send()

    def everyone(self, act):
        wides = lax.axis_size("wide")
        count = wides * lax.axis_size("heads")
        me = self.h * wides + lax.axis_index("wide")

        def one(step, carry):
            flat = lax.rem(me + step, count)
            act(flat, (flat // wides, lax.rem(flat, wides)))
            return carry

        lax.fori_loop(1, count, one, 0)

    def small_copy(self, place, source, target, device):
        send, recv = self.small_sems
        return pltpu.make_async_remote_copy(
            src_ref=source, dst_ref=target, send_sem=send.at[place], recv_sem=recv.at[place],
            device_id=device, device_id_type=MESH,
        )

    def small_send(self, place, source_of, target):
        me = self.h * lax.axis_size("wide") + lax.axis_index("wide")
        self.everyone(
            lambda flat, device: self.small_copy(place, source_of(flat), target.at[me], device).start()
        )
        pltpu.make_async_copy(source_of(me), target.at[me], self.small_local.at[place]).start()

    def small_wait(self, place, source_of, target):
        me = self.h * lax.axis_size("wide") + lax.axis_index("wide")
        others = pl.ds(0, target.shape[0] - 1)
        whole = self.small_copy(place, target.at[others], target.at[others], self.beside("c"))
        whole.wait_recv()
        whole.wait_send()
        pltpu.make_async_copy(source_of(me), target.at[me], self.small_local.at[place]).wait()


def spread_matrix(lanes, width, period):
    lane = lax.broadcasted_iota(jnp.int32, (lanes, width), 0).astype(F32)
    column = lax.broadcasted_iota(jnp.int32, (lanes, width), 1).astype(F32)
    place = column - period * jnp.floor((column + 0.5) * (1.0 / period))
    return jnp.where(place == lane, 1.0, 0.0).astype(BF)


def owner_mask(count, width, period):
    owner = lax.broadcasted_iota(jnp.int32, (count, width), 0) * period
    column = lax.broadcasted_iota(jnp.int32, (count, width), 1)
    return (column >= owner) & (column < owner + period)


def split_dot(values, exact, right_dim):
    high = values.astype(BF)
    rest = values - high.astype(F32)
    middle = rest.astype(BF)
    last = (rest - middle.astype(F32)).astype(BF)
    return dot(high, exact, 1, right_dim) + dot(middle, exact, 1, right_dim) + dot(last, exact, 1, right_dim)


def step_kernel(
    length_ref, tokens_ref, cotangent_ref, small_ref, pair_own_ref, chunk_own_ref,
    block_ref, gradient_ref, pair_sum_ref, chunk_sum_ref, extra_ref, total_ref,
    pair_ref, chunk_ref, pair_land0, pair_land1, pair_land2, pair_land3,
    chunk_land0, chunk_land1, chunk_land2, chunk_land3,
    normed_ref, upstream_ref, out_ref, back_ref, gains_ref, bias_ref, gains_back_ref, bias_back_ref,
    smalls_ref, extra_send_ref, extras_ref, norm_ref, squares_ref,
    gather_send, gather_recv, scatter_send, scatter_recv, local_sem, small_send, small_recv, small_local,
    load_sem, *work,
):
    t = Traffic(
        dict(
            pair=pair_ref, chunk=chunk_ref, pair_own=pair_own_ref, chunk_own=chunk_own_ref,
            pair_landing=(pair_land0, pair_land1, pair_land2, pair_land3),
            chunk_landing=(chunk_land0, chunk_land1, chunk_land2, chunk_land3),
            pair_sum=pair_sum_ref, chunk_sum=chunk_sum_ref, squares=squares_ref,
            gather_sems=(gather_send, gather_recv), scatter_sems=(scatter_send, scatter_recv),
            local_sem=local_sem, small_sems=(small_send, small_recv), small_local=small_local,
        )
    )
    slots = normed_ref.shape[0]
    devices = smalls_ref.shape[0]
    gain_width, bias_width = D // devices, FF // devices
    load_tokens = lambda: pltpu.make_async_copy(tokens_ref, normed_ref, load_sem.at[0])
    load_cotangent = lambda: pltpu.make_async_copy(cotangent_ref, upstream_ref, load_sem.at[1])
    load_tokens().start()
    load_cotangent().start()
    barrier = pltpu.get_barrier_semaphore()
    t.everyone(
        lambda flat, device: pl.semaphore_signal(barrier, inc=1, device_id=device, device_id_type=MESH)
    )
    pl.semaphore_wait(barrier, devices - 1)

    t.gather_deep(0)
    small_of = lambda flat: small_ref
    t.small_send(0, small_of, smalls_ref)
    squares_ref[...] = jnp.zeros_like(squares_ref)
    extra_send_ref[...] = jnp.zeros_like(extra_send_ref)
    load_cotangent().wait()
    load_tokens().wait()

    def prepare(rows):
        upstream_ref[rows, :] = jnp.where(
            below(length_ref, rows), upstream_ref[rows, :].astype(F32), 0.0
        ).astype(BF)
        inputs = normed_ref[rows, :].astype(F32)
        out_ref[rows, :] = inputs
        back_ref[rows, :], _ = row_norm(inputs)

    over_rows(slots, prepare)
    t.gather_sides(0)
    t.gather_deep(1)
    t.small_wait(0, small_of, smalls_ref)
    gain_spread = spread_matrix(128, D, gain_width)
    gain_owner = owner_mask(devices, D, gain_width)
    for row in range(3):
        spread = split_dot(smalls_ref[:, row, :], gain_spread, 0)
        gains_ref[row : row + 1, :] = jnp.sum(jnp.where(gain_owner, spread, 0.0), axis=0, keepdims=True)
    bias_spread = spread_matrix(128, FF, bias_width)
    bias_owner = owner_mask(devices, FF, bias_width)
    spread = dot(smalls_ref[:, 3, :].astype(BF), bias_spread, 1, 0)
    bias_ref[...] = jnp.sum(jnp.where(bias_owner, spread, 0.0), axis=0, keepdims=True)
    t.gather_forward(0)

    def scale(rows):
        normed_ref[rows, :] = (back_ref[rows, :] * gains_ref[0:1, :]).astype(BF)
        back_ref[rows, :] = jnp.zeros_like(back_ref[rows, :])

    over_rows(slots, scale)
    t.gather_core(0)
    t.gather_sides(1)
    t.gather_deep(2)
    t.gather_done(0)

    events = {
        (0, -1): [(t.gather_deep, 3)],
        (0, 1): [(t.gather_forward, 1), (t.gather_sides, 2), (t.gather_deep, 4), (t.gather_deep, 5)],
        (0, 2): [(t.gather_core, 1)],
        (0, 3): [(t.gather_done, 1), (t.gather_sides, 3)],
        (1, 0): [(t.gather_forward, 2)],
        (1, 1): [(t.gather_forward, 3), (t.gather_sides, 4)],
        (1, 2): [(t.gather_core, 2)],
        (1, 3): [(t.gather_done, 2), (t.scatter_core, 1), (t.gather_core, 3)],
        (2, -1): [(t.gather_sides, 5), (t.scatter_core, 0)],
        (3, -1): [(t.scatter_far, 1), (t.gather_forward, 4), (t.scatter_far, 0)],
        (4, -1): [(t.gather_done, 3), (t.scatter_core, 2), (t.scatter_sides, 1)],
        (5, -1): [(t.gather_core, 4), (t.scatter_far, 2), (t.gather_forward, 5), (t.scatter_sides, 0)],
        (6, -1): [(t.scatter_core, 3), (t.gather_done, 4)],
        (7, -1): [(t.gather_core, 5), (t.scatter_far, 3), (t.scatter_sides, 2), (t.gather_done, 5)],
        (8, -1): [(t.scatter_core, 4), (t.scatter_deep, 1), (t.scatter_deep, 0)],
        (8, 0): [(t.scatter_far, 4), (t.scatter_sides, 3)],
        (8, 1): [(t.scatter_deep, 2), (t.scatter_sides, 4)],
        (8, 2): [(t.scatter_deep, 3)],
        (8, 3): [(t.scatter_core, 5)],
        ("end", 0): [(t.scatter_far, 5)],
        ("end", 1): [(t.scatter_deep, 4), (t.scatter_sides, 5)],
        ("end", 2): [(t.scatter_done, 1)],
        ("end", 3): [
            (t.scatter_deep, 5), (t.scatter_done, 3), (t.scatter_done, 2), (t.scatter_done, 0),
            (t.scatter_done, 4),
        ],
    }

    def finish(place):
        for act, unit in events["end", place]:
            act(unit)

    def run(index, place, sections):
        for section in sections:
            if (section, place) in events:

                @pl.when(index == section)
                def _():
                    for act, unit in events[section, place]:
                        act(unit)

    def step(index, carry):
        is_pair = (index < FIRST_CHUNK) | (index == LAST_PAIR)
        pair_sections = tuple(range(FIRST_CHUNK)) + (LAST_PAIR,)
        chunk_sections = range(FIRST_CHUNK, LAST_PAIR)

        @pl.when(is_pair)
        def _():
            run(index, -1, pair_sections)
            unit = jnp.where(index == LAST_PAIR, PAIRS - 1, index)
            starts = [pl.multiple_of(half * HALF_E + unit * PAIR, PAIR) for half in range(2)]
            gain_of = lambda row: jnp.concatenate(
                [gains_ref[row : row + 1, pl.ds(start, PAIR)] for start in starts], axis=1
            )

            def store(grads, query_back, key_back):
                for half in range(2):
                    pair_ref[unit, half] = grads[half].reshape(pair_ref.shape[2:])
                    cut = slice(half * PAIR, (half + 1) * PAIR)
                    gains_back_ref[1:2, pl.ds(starts[half], PAIR)] = query_back[:, cut]
                    gains_back_ref[2:3, pl.ds(starts[half], PAIR)] = key_back[:, cut]

            attention_section(
                lambda half: pair_ref[unit, half].reshape(D, 4 * PAIR), normed_ref[...], upstream_ref[...],
                gain_of(1), gain_of(2), jnp.where(below(length_ref, pl.ds(0, slots)), 0.0, MASKED),
                out_ref, back_ref, work, store, lambda place: run(index, place, pair_sections),
            )

        @pl.when(~is_pair)
        def _():
            run(index, -1, chunk_sections)
            unit = (index - FIRST_CHUNK) // 2
            half = lax.rem(index - FIRST_CHUNK, 2)
            start = pl.multiple_of(half * HALF_F + unit * CHUNK, CHUNK)
            grad, bias_back = mlp_section(
                chunk_ref[unit, half].reshape(D, 2 * CHUNK), normed_ref[...], upstream_ref[...],
                bias_ref[0:1, pl.ds(start, CHUNK)], out_ref, back_ref,
            )
            chunk_ref[unit, half] = grad.reshape(chunk_ref.shape[2:])
            bias_back_ref[0:1, pl.ds(start, CHUNK)] = bias_back

        return carry

    lax.fori_loop(0, SECTIONS, step, 0)
    load_tokens().start()
    store_block = pltpu.make_async_copy(out_ref, block_ref, load_sem.at[2])
    store_block.start()
    finish(0)
    load_tokens().wait()
    finish_input(normed_ref, gains_ref, upstream_ref, back_ref, gains_back_ref)
    store_gradient = pltpu.make_async_copy(back_ref, gradient_ref, load_sem.at[3])
    store_gradient.start()
    finish(1)
    for row in range(3):
        rows = jnp.where(gain_owner, gains_back_ref[row : row + 1, :], 0.0)
        extra_send_ref[:, row, :] = split_dot(rows, gain_spread, 1)
    rows = jnp.where(bias_owner, bias_back_ref[...], 0.0)
    extra_send_ref[:, 3, :] = split_dot(rows, bias_spread, 1)
    extra_of = lambda flat: extra_send_ref.at[flat]
    t.small_send(1, extra_of, extras_ref)
    finish(2)
    finish(3)
    t.small_wait(1, extra_of, extras_ref)
    extra = jnp.sum(extras_ref[...], axis=0)
    extra_ref[...] = extra
    t.scatter_done(5)
    norm_ref[...] = squares_ref[...] + jnp.full(squares_ref.shape, jnp.sum(extra * extra), F32)
    norm_of = lambda flat: norm_ref
    t.small_send(2, norm_of, smalls_ref)
    store_block.wait()
    store_gradient.wait()
    t.small_wait(2, norm_of, smalls_ref)
    total_ref[...] = jnp.sum(smalls_ref[...], axis=0)


def exchanged_block(lengths, tokens, cotangent, norm_gains, expand_bias, pair_own, chunk_own):
    slots = tokens.shape[0]
    wides = lax.axis_size("wide")
    devices = wides * lax.axis_size("heads")
    deep = wides // 4
    rows = pair_own.shape[1]
    small = jnp.concatenate(
        [
            jnp.pad(norm_gains, ((0, 0), (0, 128 - norm_gains.shape[1]))),
            jnp.pad(expand_bias.astype(BF).astype(F32)[None], ((0, 4), (0, 128 - expand_bias.shape[0]))),
        ],
        axis=0,
    )
    vmem = pl.BlockSpec(memory_space=pltpu.VMEM)
    hbm = pl.BlockSpec(memory_space=pl.ANY)
    landings = lambda units, pairs, width: [
        pltpu.VMEM((2, 2, deep, 2, rows, width), BF),
        pltpu.VMEM((units, deep, rows, width), BF),
        pltpu.VMEM((pairs, 2, deep, rows, width), BF),
        pltpu.VMEM((units, deep - 1, rows, width), BF),
    ]
    tile = pltpu.VMEM((8, 128), F32)
    tiles = pltpu.VMEM((devices, 8, 128), F32)
    dma = pltpu.SemaphoreType.DMA
    gather_slots, scatter_slots = deep + 7, deep + 4
    block_output, token_gradient, pair_sum, chunk_sum, extra, total = pl.pallas_call(
        step_kernel,
        in_specs=[pl.BlockSpec(memory_space=pltpu.SMEM), hbm, hbm, vmem, hbm, hbm],
        out_specs=[hbm, hbm, vmem, vmem, vmem, vmem],
        out_shape=[
            jax.ShapeDtypeStruct((slots, D), F32),
            jax.ShapeDtypeStruct((slots, D), F32),
            jax.ShapeDtypeStruct((PAIRS, rows, 4 * PAIR), F32),
            jax.ShapeDtypeStruct((CHUNKS, rows, 2 * CHUNK), F32),
            jax.ShapeDtypeStruct((8, 128), F32),
            jax.ShapeDtypeStruct((8, 128), F32),
        ],
        scratch_shapes=[
            pltpu.VMEM((PAIRS, 2, deep, 2, 2, rows, 4 * PAIR), BF),
            pltpu.VMEM((CHUNKS, 2, deep, 2, 2, rows, 2 * CHUNK), BF),
        ]
        + landings(PAIRS, 2, 4 * PAIR)
        + landings(CHUNKS, CHUNKS, 2 * CHUNK)
        + [
            pltpu.VMEM((slots, D), BF), pltpu.VMEM((slots, D), BF),
            pltpu.VMEM((slots, D), F32), pltpu.VMEM((slots, D), F32),
            pltpu.VMEM((3, D), F32), pltpu.VMEM((1, FF), F32),
            pltpu.VMEM((3, D), F32), pltpu.VMEM((1, FF), F32),
            tiles, tiles, tiles, tile, tile,
            dma((UNITS, gather_slots)), dma((UNITS, gather_slots)),
            dma((UNITS, scatter_slots)), dma((UNITS, scatter_slots)),
            dma((UNITS,)), dma((3,)), dma((3,)), dma((3,)), dma((4,)),
        ]
        + attention_scratch(slots),
        compiler_params=pltpu.CompilerParams(
            vmem_limit_bytes=67043328, collective_id=0, has_side_effects=True
        ),
        name="step_block",
    )(lengths, tokens, cotangent, small, pair_own, chunk_own)
    grads = unpack_shards(pair_sum, chunk_sum) + (
        extra[3, : expand_bias.shape[0]],
        extra[:3, : norm_gains.shape[1]],
    )
    return block_output, token_gradient, grads, total[0, 0]


def optimizer_update(
    weight, raw_grad, factor, first, second, average, rate, decay, first_fix, second_fix, keep
):
    clipped = raw_grad * factor
    first_new = BETA_FIRST * first + (1.0 - BETA_FIRST) * clipped
    second_new = BETA_SECOND * second + (1.0 - BETA_SECOND) * clipped * clipped
    direction = first_new / first_fix / (jnp.sqrt(second_new / second_fix) + ADAM_EPS)
    weight_new = weight - rate * (direction + decay * weight)
    average_new = keep * average + (1.0 - keep) * weight_new
    return (clipped, first_new, second_new, weight_new, average_new)


def pack_shards(attend_weights, output_weights, expand_weights, reduce_weights):
    rows = attend_weights.shape[1]
    attend = attend_weights.astype(BF).reshape(3, rows, PAIRS, PAIR)
    attend = jnp.transpose(attend, (2, 1, 0, 3)).reshape(PAIRS, rows, 3 * PAIR)
    output = jnp.transpose(
        output_weights.astype(BF).T.reshape(rows, PAIRS, PAIR), (1, 0, 2)
    )
    expand = jnp.transpose(expand_weights.astype(BF).reshape(rows, CHUNKS, CHUNK), (1, 0, 2))
    reduce = jnp.transpose(reduce_weights.astype(BF).T.reshape(rows, CHUNKS, CHUNK), (1, 0, 2))
    return jnp.concatenate([attend, output], axis=2), jnp.concatenate([expand, reduce], axis=2)


def unpack_shards(pair_grads, chunk_grads):
    rows = pair_grads.shape[1]
    attend = jnp.transpose(
        pair_grads[:, :, : 3 * PAIR].reshape(PAIRS, rows, 3, PAIR), (2, 1, 0, 3)
    ).reshape(3, rows, HALF_E)
    join = lambda part: jnp.transpose(part, (1, 0, 2)).reshape(rows, -1)
    return (
        attend,
        join(pair_grads[:, :, 3 * PAIR :]).T,
        join(chunk_grads[:, :, :CHUNK]),
        join(chunk_grads[:, :, CHUNK:]).T,
    )


def gathered_block(lengths, tokens, cotangent, norm_gains, expand_bias, pair_own, chunk_own):
    both = ("heads", "wide")
    gains = lax.all_gather(norm_gains, both, axis=1, tiled=True)
    bias = lax.all_gather(expand_bias.astype(BF), both, axis=0, tiled=True).astype(F32)
    whole = lambda own: lax.all_gather(
        lax.all_gather(own, "wide", axis=1, tiled=True), "heads", axis=1
    )
    block_output, token_gradient, pair_grads, chunk_grads, bias_back, gains_back = local_block(
        lengths, tokens, cotangent, gains, bias[None, :], whole(pair_own), whole(chunk_own)
    )
    scatter = lambda part: lax.psum_scatter(
        lax.psum_scatter(part, "heads", scatter_dimension=1),
        "wide", scatter_dimension=1, tiled=True,
    ).astype(F32)
    grads = unpack_shards(scatter(pair_grads), scatter(chunk_grads)) + (
        lax.psum_scatter(bias_back[0], both, scatter_dimension=0, tiled=True),
        lax.psum_scatter(gains_back, both, scatter_dimension=1, tiled=True),
    )
    squares = jnp.sum(jnp.stack([jnp.sum(entry * entry) for entry in grads]))
    return block_output, token_gradient, grads, lax.psum(squares, both)


def body(
    tokens, cotangent, lengths, step_count,
    attend_weights, output_weights, expand_weights, reduce_weights, expand_bias, norm_gains,
    *moments,
):
    masters = (
        attend_weights, output_weights, expand_weights, reduce_weights, expand_bias, norm_gains,
    )
    firsts, seconds, averages = moments[:6], moments[6:12], moments[12:]
    pair_own, chunk_own = pack_shards(*masters[:4])
    wides = lax.axis_size("wide")
    aligned = wides % 8 == 0 and pair_own.shape[1] % 16 == 0 and lax.axis_size("heads") == 2
    block_output, token_gradient, grads, total_squares = (exchanged_block if aligned else gathered_block)(
        lengths, tokens[0], cotangent[0], norm_gains, expand_bias, pair_own, chunk_own
    )
    grad_norm = jnp.sqrt(total_squares)
    tokens_all = tokens.shape[1] * lax.axis_size("heads") * lax.axis_size("wide")
    limit = 0.02 * math.sqrt(tokens_all * D * FF)
    factor = jnp.minimum(1.0, limit / grad_norm)
    step_float = step_count[0].astype(F32)
    first_fix = 1.0 - jnp.power(BETA_FIRST, step_float)
    second_fix = 1.0 - jnp.power(BETA_SECOND, step_float)
    keep = jnp.minimum(AVERAGE_CAP, (1.0 + step_float) / (10.0 + step_float))
    results = [block_output[None], token_gradient[None], grad_norm.reshape(1)]
    for index in range(6):
        results.extend(
            optimizer_update(
                masters[index], grads[index], factor, firsts[index], seconds[index],
                averages[index], RATES[index], DECAYS[index], first_fix, second_fix, keep,
            )
        )
    return tuple(results)


def solution(mesh):
    both = ("heads", "wide")
    weight_specs = (
        P(None, "wide", "heads"), P("heads", "wide"), P("wide", "heads"), P("heads", "wide"),
        P(both), P(None, both),
    )
    image = P(both, None, None)
    return jax.shard_map(
        body,
        mesh=mesh,
        in_specs=(image, image, P(both), P()) + weight_specs * 4,
        out_specs=(image, image, P()) + tuple(spec for spec in weight_specs for _ in range(5)),
        check_vma=False,
    )
```

```python
from functools import partial
import math

import jax
import jax.numpy as jnp
from jax import lax
from jax.experimental import pallas as pl
from jax.experimental.pallas import tpu as pltpu
from jax.sharding import PartitionSpec as P

D = 768
HEADS = 12
HEAD_DIM = 64
FF = 3072
HALF_E = D // 2
HALF_F = FF // 2
PAIR = 128
PAIRS = HALF_E // PAIR
CHUNK = 512
CHUNKS = HALF_F // CHUNK
QUERY_ROWS = 512
ROWS = 256
BF = jnp.bfloat16
F32 = jnp.float32

NORM_EPS = 1e-06
MASKED = -1e30
BETA_FIRST = 0.9
BETA_SECOND = 0.95
AVERAGE_CAP = 0.9999
ADAM_EPS = 1e-08
RATES = (0.03, 0.2, 0.03, 0.015, 0.3, 0.3)
DECAYS = (0.05, 0.05, 0.05, 0.05, 0.0, 0.0)


def dot(left, right, left_dim, right_dim):
    return lax.dot_general(
        left, right, (((left_dim,), (right_dim,)), ((), ())), preferred_element_type=F32
    )


def row_norm(values):
    center = values - jnp.mean(values, axis=-1, keepdims=True)
    inverse = lax.rsqrt(jnp.mean(center * center, axis=-1, keepdims=True) + NORM_EPS)
    return center * inverse, inverse


def head_mean(values, exact=False):
    width = values.shape[1]
    row = lax.broadcasted_iota(jnp.int32, (width, width), 0) // HEAD_DIM
    column = lax.broadcasted_iota(jnp.int32, (width, width), 1) // HEAD_DIM
    block = jnp.where(row == column, 1.0 / HEAD_DIM, 0.0).astype(BF)
    high = values.astype(BF)
    mean = dot(high, block, 1, 0)
    if not exact:
        return mean
    return mean + dot((values - high.astype(F32)).astype(BF), block, 1, 0)


def head_norm(values):
    center = values - head_mean(values, True)
    inverse = lax.rsqrt(head_mean(center * center) + NORM_EPS)
    return center * inverse, inverse


def head_norm_back(upstream, normal, inverse):
    return inverse * (upstream - head_mean(upstream) - normal * head_mean(upstream * normal))


def pair_attention(query, keyed, value, back_mixed, key_bias):
    rows = query.shape[0]
    lane = lax.broadcasted_iota(jnp.int32, (rows, PAIR), 1)
    low = lane < HEAD_DIM
    first = lane == 0
    zero = jnp.zeros((rows, PAIR), BF)
    one_lane = jnp.where(first, 1.0, 0.0).astype(BF)
    bias_lane = jnp.where(first, key_bias, 0.0).astype(BF)
    query_wide = jnp.concatenate([query, one_lane], axis=1)
    value_wide = jnp.concatenate([value, jnp.ones((rows, PAIR), BF)], axis=1)
    blocks = rows // QUERY_ROWS
    mixed = [[None] * blocks for _ in range(2)]
    back_query = [[None] * blocks for _ in range(2)]
    back_keyed = None
    back_value = None
    lane_q = lane[:QUERY_ROWS]
    low_q = low[:QUERY_ROWS]
    for head in range(2):
        mine = low if head == 0 else ~low
        mine_q = mine[:QUERY_ROWS]
        key_wide = jnp.concatenate([jnp.where(mine, keyed, zero), bias_lane], axis=1)
        query_mine = jnp.where(mine, query, zero)
        for block in range(blocks):
            cut = slice(block * QUERY_ROWS, (block + 1) * QUERY_ROWS)
            expo = jnp.exp(dot(query_wide[cut], key_wide, 1, 1))
            expo_low = expo.astype(BF)
            sums = dot(expo_low, value_wide, 1, 0)
            inverse = 1.0 / sums[:, PAIR:]
            rows_mixed = sums[:, :PAIR] * inverse
            scaled = jnp.where(mine_q, back_mixed[cut].astype(F32) * inverse, 0.0).astype(BF)
            inner = jnp.sum(rows_mixed * scaled.astype(F32), axis=1, keepdims=True)
            inner_high = inner.astype(BF).astype(F32)
            inner_lanes = jnp.where(
                lane_q == 0, -inner_high, jnp.where(lane_q == 1, inner_high - inner, 0.0)
            ).astype(BF)
            centered = dot(jnp.concatenate([scaled, inner_lanes], axis=1), value_wide, 1, 1)
            back_scores = (expo * centered).astype(BF)
            mixed[head][block] = rows_mixed
            back_query[head][block] = dot(back_scores, keyed, 1, 0)
            add_keyed = dot(query_mine[cut], back_scores, 0, 0)
            add_value = dot(scaled, expo_low, 0, 0)
            back_keyed = add_keyed if back_keyed is None else back_keyed + add_keyed
            back_value = add_value if back_value is None else back_value + add_value
    join = lambda parts: jnp.concatenate(
        [jnp.where(low_q, parts[0][block], parts[1][block]) for block in range(blocks)], axis=0
    )
    return join(mixed).astype(BF), join(back_query), back_keyed, back_value


def attention_scratch(slots):
    rows = [pltpu.VMEM((2, slots, PAIR), BF)] * 4 + [pltpu.VMEM((2, slots, PAIR), F32)] * 5
    return rows + [pltpu.VMEM((2, PAIR, slots), F32)]


def attention_section(
    weights, normed, upstream, query_gain, key_gain, key_bias, out_ref, back_ref, work, store,
    pause=lambda place: None,
):
    (
        query_ref, key_ref, value_ref, back_mixed_ref,
        query_hat_ref, query_inv_ref, key_hat_ref, key_inv_ref, back_query_ref, back_keyed_ref,
    ) = work
    three = 3 * PAIR
    halves = (slice(0, PAIR), slice(PAIR, 2 * PAIR))
    both = [weights(half) for half in range(2)]
    into = jnp.concatenate([part[:, :three] for part in both], axis=1)
    out = jnp.concatenate([part[:, three:] for part in both], axis=1)
    projected = dot(normed, into, 1, 0)
    back_mixed = dot(upstream, out, 1, 0).astype(BF)
    pick = lambda place: jnp.concatenate(
        [
            projected[:, place * PAIR : (place + 1) * PAIR],
            projected[:, three + place * PAIR : three + (place + 1) * PAIR],
        ],
        axis=1,
    )
    query_hat, query_inv = head_norm(pick(0))
    key_hat, key_inv = head_norm(pick(1))
    query = (query_hat * query_gain).astype(BF)
    query = (query.astype(F32) * HEAD_DIM ** (-0.5)).astype(BF)
    keyed = (key_hat * key_gain).astype(BF)
    value = pick(2).astype(BF)
    for half, cut in enumerate(halves):
        for ref, rows in (
            (query_ref, query), (key_ref, keyed), (value_ref, value), (back_mixed_ref, back_mixed),
            (query_hat_ref, query_hat), (query_inv_ref, query_inv),
            (key_hat_ref, key_hat), (key_inv_ref, key_inv),
        ):
            ref[half] = rows[:, cut]

    def one_pair(half, carry):
        for place in range(2):
            pl.when(half == place)(partial(pause, place))
        mixed, back_query_ref[half], back_keyed_ref[half], back_value = pair_attention(
            query_ref[half], key_ref[half], value_ref[half], back_mixed_ref[half], key_bias
        )
        query_ref[half] = mixed
        value_ref[half] = back_value.T.astype(BF)
        return carry

    lax.fori_loop(0, 2, one_pair, 0)
    pause(2)
    whole = lambda ref: jnp.concatenate([ref[0], ref[1]], axis=1)
    both = [weights(half) for half in range(2)]
    into = jnp.concatenate([part[:, :three] for part in both], axis=1)
    out = jnp.concatenate([part[:, three:] for part in both], axis=1)
    mixed = whole(query_ref)
    query_hat, key_hat = whole(query_hat_ref), whole(key_hat_ref)
    back_qn = whole(back_query_ref) * HEAD_DIM ** (-0.5)
    back_kn = jnp.concatenate([back_keyed_ref[0].T, back_keyed_ref[1].T], axis=1)
    query_gain_back = jnp.sum(back_qn * query_hat, axis=0, keepdims=True)
    key_gain_back = jnp.sum(back_kn * key_hat, axis=0, keepdims=True)
    back_query = head_norm_back(back_qn * query_gain, query_hat, whole(query_inv_ref)).astype(BF)
    back_keyed = head_norm_back(back_kn * key_gain, key_hat, whole(key_inv_ref)).astype(BF)
    back_into = jnp.concatenate(
        [
            part
            for half, cut in enumerate(halves)
            for part in (back_query[:, cut], back_keyed[:, cut], value_ref[half])
        ],
        axis=1,
    )
    grad_into = dot(normed, back_into, 0, 0).astype(BF)
    grad_out = dot(upstream, mixed, 0, 0).astype(BF)
    grads = [
        jnp.concatenate([grad_into[:, half * three : (half + 1) * three], grad_out[:, cut]], axis=1)
        for half, cut in enumerate(halves)
    ]
    store(grads, query_gain_back, key_gain_back)
    pause(3)
    out_ref[...] += dot(mixed, out, 1, 1)
    back_ref[...] += dot(back_into, into, 1, 1)


def mlp_section(weights, normed, upstream, bias, out_ref, back_ref):
    expand = weights[:, :CHUNK]
    reduce = weights[:, CHUNK:]
    pre = dot(normed, expand, 1, 0) + bias
    back_hidden = dot(upstream, reduce, 1, 0)
    phi = 0.5 * (1.0 + lax.erf(pre * math.sqrt(0.5)))
    density = jnp.exp(-0.5 * pre * pre) * (1.0 / math.sqrt(2.0 * math.pi))
    hidden = (pre * phi).astype(BF)
    back_pre = (back_hidden * (phi + pre * density)).astype(BF)
    out_ref[...] += dot(hidden, reduce, 1, 1)
    back_ref[...] += dot(back_pre, expand, 1, 1)
    grads = [dot(normed, back_pre, 0, 0).astype(BF), dot(upstream, hidden, 0, 0).astype(BF)]
    return jnp.concatenate(grads, axis=1), jnp.sum(back_pre.astype(F32), axis=0, keepdims=True)


def over_rows(slots, act):
    def one(block, carry):
        act(pl.ds(pl.multiple_of(block * ROWS, ROWS), ROWS))
        return carry

    lax.fori_loop(0, slots // ROWS, one, 0)


def below(length_ref, rows):
    place = lax.broadcasted_iota(jnp.int32, (rows.size, 1), 0) + rows.start
    return place < length_ref[0]


def start_input(
    length_ref, tokens_ref, cotangent_ref, gains_ref, normed_ref, upstream_ref, out_ref, back_ref
):
    def one(rows):
        inputs = tokens_ref[rows, :].astype(F32)
        input_hat, _ = row_norm(inputs)
        normed_ref[rows, :] = (input_hat * gains_ref[0:1, :]).astype(BF)
        upstream_ref[rows, :] = jnp.where(
            below(length_ref, rows), cotangent_ref[rows, :].astype(F32), 0.0
        ).astype(BF)
        out_ref[rows, :] = inputs
        back_ref[rows, :] = jnp.zeros_like(inputs)

    over_rows(tokens_ref.shape[0], one)


def finish_input(tokens_ref, gains_ref, upstream_ref, back_ref, gains_back_ref):
    gains_back_ref[0:1, :] = jnp.zeros_like(gains_back_ref[0:1, :])

    def one(rows):
        input_hat, input_inv = row_norm(tokens_ref[rows, :].astype(F32))
        back_normed = back_ref[rows, :]
        gains_back_ref[0:1, :] += jnp.sum(back_normed * input_hat, axis=0, keepdims=True)
        scaled = back_normed * gains_ref[0:1, :]
        back_ref[rows, :] = upstream_ref[rows, :].astype(F32) + input_inv * (
            scaled
            - jnp.mean(scaled, axis=-1, keepdims=True)
            - input_hat * jnp.mean(scaled * input_hat, axis=-1, keepdims=True)
        )

    over_rows(tokens_ref.shape[0], one)


def local_kernel(
    length_ref, tokens_ref, cotangent_ref, gains_ref, bias_ref, pair_ref, chunk_ref,
    out_ref, back_ref, grad_pair_ref, grad_chunk_ref, bias_back_ref, gains_back_ref,
    normed_ref, upstream_ref, *work,
):
    index = pl.program_id(0)

    @pl.when(index == 0)
    def _():
        start_input(
            length_ref, tokens_ref, cotangent_ref, gains_ref, normed_ref, upstream_ref, out_ref, back_ref
        )

    is_pair = (index == 0) | (index > 2 * CHUNKS)

    @pl.when(is_pair)
    def _():
        unit = jnp.where(index == 0, 0, index - 2 * CHUNKS)
        starts = [pl.multiple_of(half * HALF_E + unit * PAIR, PAIR) for half in range(2)]
        gain_of = lambda row: jnp.concatenate(
            [gains_ref[row : row + 1, pl.ds(start, PAIR)] for start in starts], axis=1
        )
        place = lax.broadcasted_iota(jnp.int32, (tokens_ref.shape[0], 1), 0)

        def store(grads, query_back, key_back):
            for half in range(2):
                grad_pair_ref[0, half] = grads[half]
                cut = slice(half * PAIR, (half + 1) * PAIR)
                gains_back_ref[1:2, pl.ds(starts[half], PAIR)] = query_back[:, cut]
                gains_back_ref[2:3, pl.ds(starts[half], PAIR)] = key_back[:, cut]

        attention_section(
            lambda half: pair_ref[0, half], normed_ref[...], upstream_ref[...],
            gain_of(1), gain_of(2), jnp.where(place < length_ref[0], 0.0, MASKED), out_ref, back_ref, work,
            store,
        )

    @pl.when(~is_pair)
    def _():
        unit = (index - 1) // 2
        half = lax.rem(index - 1, 2)
        start = pl.multiple_of(half * HALF_F + unit * CHUNK, CHUNK)
        grad, bias_back = mlp_section(
            chunk_ref[0, 0], normed_ref[...], upstream_ref[...],
            bias_ref[0:1, pl.ds(start, CHUNK)], out_ref, back_ref,
        )
        grad_chunk_ref[0, 0] = grad
        bias_back_ref[0:1, pl.ds(start, CHUNK)] = bias_back

    @pl.when(index == PAIRS + 2 * CHUNKS - 1)
    def _():
        finish_input(tokens_ref, gains_ref, upstream_ref, back_ref, gains_back_ref)


def local_block(length, tokens, cotangent, gains, bias, pair_weights, chunk_weights):
    slots = tokens.shape[0]
    steps = PAIRS + 2 * CHUNKS
    whole = lambda shape: pl.BlockSpec(shape, lambda index: (0,) * len(shape))
    pair_at = lambda index: (jnp.maximum(index - 2 * CHUNKS, 0), 0, 0, 0)

    def chunk_at(index):
        flat = jnp.clip(index - 1, 0, 2 * CHUNKS - 1)
        return (flat // 2, lax.rem(flat, 2), 0, 0)

    pair_spec = pl.BlockSpec((1, 2, D, 4 * PAIR), pair_at)
    chunk_spec = pl.BlockSpec((1, 1, D, 2 * CHUNK), chunk_at)
    return pl.pallas_call(
        local_kernel,
        grid=(steps,),
        in_specs=[
            pl.BlockSpec(memory_space=pltpu.SMEM),
            whole((slots, D)), whole((slots, D)), whole((3, D)), whole((1, FF)), pair_spec, chunk_spec,
        ],
        out_specs=[
            whole((slots, D)), whole((slots, D)), pair_spec, chunk_spec, whole((1, FF)), whole((3, D)),
        ],
        out_shape=[
            jax.ShapeDtypeStruct((slots, D), F32),
            jax.ShapeDtypeStruct((slots, D), F32),
            jax.ShapeDtypeStruct((PAIRS, 2, D, 4 * PAIR), BF),
            jax.ShapeDtypeStruct((CHUNKS, 2, D, 2 * CHUNK), BF),
            jax.ShapeDtypeStruct((1, FF), F32),
            jax.ShapeDtypeStruct((3, D), F32),
        ],
        scratch_shapes=[pltpu.VMEM((slots, D), BF), pltpu.VMEM((slots, D), BF)]
        + attention_scratch(slots),
        compiler_params=pltpu.CompilerParams(vmem_limit_bytes=60 << 20),
        name="local_block",
    )(length, tokens, cotangent, gains, bias, pair_weights, chunk_weights)


PAIR_UNITS = (0, 1, 5)
CHUNK_UNITS = (2, 3, 4)
UNITS = 6
SECTIONS = PAIRS + 2 * CHUNKS
FIRST_CHUNK = 2
LAST_PAIR = SECTIONS - 1
GATHER_COPIES = 11
SCATTER_COPIES = 8
MESH = pl.DeviceIdType.MESH


class Traffic:
    def __init__(self, refs):
        self.__dict__.update(refs)
        self.deep = self.pair.shape[2]
        self.h = lax.axis_index("heads")
        wide = lax.axis_index("wide")
        self.c = lax.rem(wide, 2)
        self.b = lax.rem(wide // 2, 2)
        self.a = wide // 4

    def buffer(self, unit):
        if unit in PAIR_UNITS:
            return self.pair.at[PAIR_UNITS.index(unit)]
        return self.chunk.at[CHUNK_UNITS.index(unit)]

    def landing(self, unit, stage):
        pair = unit in PAIR_UNITS
        landing = (self.pair_landing if pair else self.chunk_landing)[stage]
        return landing.at[(PAIR_UNITS if pair else CHUNK_UNITS).index(unit) % landing.shape[0]]

    def device(self, h=None, a=None, b=None, c=None):
        h = self.h if h is None else h
        a = self.a if a is None else a
        b = self.b if b is None else b
        c = self.c if c is None else c
        return (h, (a * 2 + b) * 2 + c)

    def beside(self, axis):
        if axis == "h":
            return self.device(h=1 - self.h)
        if axis == "b":
            return self.device(b=1 - self.b)
        return self.device(c=1 - self.c)

    def along(self, step):
        return self.device(a=lax.rem(self.a + step, self.deep))

    def copy(self, source, target, sems, unit, slot, device):
        send, recv = sems
        return pltpu.make_async_remote_copy(
            src_ref=source, dst_ref=target, send_sem=send.at[unit, slot], recv_sem=recv.at[unit, slot],
            device_id=device, device_id_type=MESH,
        )

    def gather_copy(self, unit, slot):
        buf, half = self.buffer(unit), self.deep // 2
        h, a, b, c = self.h, self.a, self.b, self.c
        if slot < self.deep - 1:
            return self.copy(buf.at[h, a, b, c], buf.at[h, a, b, c], self.gather_sems, unit, slot, self.along(slot + 1))
        slot -= self.deep - 1
        region, device = (
            (lambda r: r.at[h, :, b, c], self.beside("h")),
            (lambda r: r.at[h, :, b, c], self.beside("b")),
            (lambda r: r.at[1 - h, pl.ds(0, half), b, c], self.beside("b")),
            (lambda r: r.at[h, pl.ds(half, self.deep - half), 1 - b, c], self.beside("h")),
            (lambda r: r.at[h, :, b, c], self.beside("c")),
            (lambda r: r.at[1 - h, :, b, c], self.beside("c")),
            (lambda r: r.at[h, :, 1 - b, c], self.beside("c")),
            (lambda r: r.at[1 - h, :, 1 - b, c], self.beside("c")),
        )[slot]
        return self.copy(
            region(buf), region(buf), self.gather_sems, unit, slot + self.deep - 1, device
        )

    def gather_start(self, unit, slots):
        for slot in slots:
            self.gather_copy(unit, slot).start()

    def gather_wait(self, unit, slots):
        for slot in slots:
            self.gather_copy(unit, slot).wait_recv()

    def pieces(self, unit):
        cut = lambda place: pl.ds(place * PAIR, PAIR)
        attend, output, expand, reduce = self.shards
        if unit in PAIR_UNITS:
            place = PAIR_UNITS.index(unit)
            return [attend.at[part, :, cut(place)] for part in range(3)] + [output.at[:, cut(place)]]
        first = CHUNK_UNITS.index(unit) * (CHUNK // PAIR)
        return [ref.at[:, cut(first + place)] for ref in (expand, reduce) for place in range(CHUNK // PAIR)]

    def staged(self, unit):
        rows, count = self.pair.shape[5], len(self.pieces(unit))
        half, first = ((0, 0), (0, 4), (0, 8), (1, 0), (1, 8), (0, 16))[unit]
        return self.stage.at[half, pl.ds(first * rows, count * rows), :]

    def load(self, unit):
        rows = self.pair.shape[5]
        for place, piece in enumerate(self.pieces(unit)):
            pltpu.make_async_copy(
                piece, self.staged(unit).at[pl.ds(place * rows, rows), :], self.local_sem.at[unit]
            ).start()

    def pack(self, unit):
        rows, staged, buf = self.pair.shape[5], self.staged(unit), self.buffer(unit)
        pltpu.make_async_copy(staged, staged, self.local_sem.at[unit]).wait()
        for place in range(len(self.pieces(unit))):
            buf[self.h, self.a, self.b, self.c, :, place * PAIR : (place + 1) * PAIR] = staged[
                place * rows : (place + 1) * rows, :
            ].astype(BF)

    def gather_deep(self, unit):
        self.gather_start(unit, range(self.deep - 1))

    def gather_sides(self, unit):
        n = self.deep - 1
        self.gather_wait(unit, range(n))
        self.gather_start(unit, (n, n + 1, n + 4))

    def gather_forward(self, unit):
        n = self.deep - 1
        self.gather_wait(unit, (n, n + 1))
        self.gather_start(unit, (n + 2, n + 3, n + 5, n + 6))

    def gather_core(self, unit):
        n = self.deep - 1
        self.gather_wait(unit, (n + 2, n + 3))
        self.gather_start(unit, (n + 7,))

    def gather_done(self, unit):
        n = self.deep - 1
        self.gather_wait(unit, range(n + 4, n + 8))
        for slot in range(n + 8):
            self.gather_copy(unit, slot).wait_send()

    def scatter_copy(self, unit, slot):
        buf, half = self.buffer(unit), self.deep // 2
        h, a, b, c = self.h, self.a, self.b, self.c
        land = lambda stage: self.landing(unit, stage)
        rest = self.deep - half
        if slot >= 5:
            step = slot - 4
            source = buf.at[h, lax.rem(a + step, self.deep), b, c]
            target, device = land(3).at[step - 1], self.along(step)
        else:
            source, target, device = (
                lambda: (buf.at[:, :, :, 1 - c], land(0), self.beside("c")),
                lambda: (buf.at[1 - h, pl.ds(0, half), 1 - b, c], land(1).at[pl.ds(0, half)], self.beside("b")),
                lambda: (buf.at[1 - h, pl.ds(half, rest), 1 - b, c], land(1).at[pl.ds(half, rest)], self.beside("h")),
                lambda: (buf.at[1 - h, :, b, c], land(2).at[0], self.beside("h")),
                lambda: (buf.at[h, :, 1 - b, c], land(2).at[1], self.beside("b")),
            )[slot]()
        return self.copy(source, target, self.scatter_sems, unit, slot, device)

    def scatter_start(self, unit, slots):
        for slot in slots:
            self.scatter_copy(unit, slot).start()

    def scatter_wait(self, unit, slots):
        for slot in slots:
            self.scatter_copy(unit, slot).wait_recv()

    def add(self, unit, where, *parts):
        buf = self.buffer(unit)
        total = buf[where].astype(F32)
        for part in parts:
            total = total + part.astype(F32)
        buf[where] = total.astype(BF)

    def scatter_core(self, unit):
        self.scatter_start(unit, (0,))

    def scatter_far(self, unit):
        h, b, c = self.h, self.b, self.c
        self.scatter_wait(unit, (0,))
        got = self.landing(unit, 0)
        far = (1 - h, slice(None), 1 - b)
        self.add(unit, far + (c,), got[far])
        self.scatter_start(unit, (1, 2))
        for near in ((1 - h, slice(None), b), (h, slice(None), 1 - b), (h, slice(None), b)):
            self.add(unit, near + (c,), got[near])

    def scatter_sides(self, unit):
        h, b, c, half = self.h, self.b, self.c, self.deep // 2
        self.scatter_wait(unit, (1, 2))
        got = self.landing(unit, 1)
        self.add(unit, (1 - h, slice(0, half), b, c), got[0:half])
        self.add(unit, (h, slice(half, self.deep), 1 - b, c), got[half : self.deep])
        self.scatter_start(unit, (3, 4))

    def scatter_deep(self, unit):
        self.scatter_wait(unit, (3, 4))
        got = self.landing(unit, 2)
        self.add(unit, (self.h, slice(None), self.b, self.c), got[0], got[1])
        self.scatter_start(unit, range(5, 4 + self.deep))

    def scatter_done(self, unit):
        self.scatter_wait(unit, range(5, 4 + self.deep))
        got = self.landing(unit, 3)
        total = self.buffer(unit)[self.h, self.a, self.b, self.c].astype(F32)
        for step in range(self.deep - 1):
            total = total + got[step].astype(F32)
        if unit in PAIR_UNITS:
            self.pair_sum[PAIR_UNITS.index(unit)] = total
        else:
            self.chunk_sum[CHUNK_UNITS.index(unit)] = total
        self.squares[...] += jnp.full(self.squares.shape, jnp.sum(total * total), F32)
        for slot in range(4 + self.deep):
            self.scatter_copy(unit, slot).wait_send()

    def everyone(self, act):
        wides = lax.axis_size("wide")
        count = wides * lax.axis_size("heads")
        me = self.h * wides + lax.axis_index("wide")

        def one(step, carry):
            flat = lax.rem(me + step, count)
            act(flat, (flat // wides, lax.rem(flat, wides)))
            return carry

        lax.fori_loop(1, count, one, 0)

    def small_copy(self, place, source, target, device):
        send, recv = self.small_sems
        return pltpu.make_async_remote_copy(
            src_ref=source, dst_ref=target, send_sem=send.at[place], recv_sem=recv.at[place],
            device_id=device, device_id_type=MESH,
        )

    def small_send(self, place, source_of, target):
        me = self.h * lax.axis_size("wide") + lax.axis_index("wide")
        self.everyone(
            lambda flat, device: self.small_copy(place, source_of(flat), target.at[me], device).start()
        )
        pltpu.make_async_copy(source_of(me), target.at[me], self.small_local.at[place]).start()

    def small_wait(self, place, source_of, target):
        me = self.h * lax.axis_size("wide") + lax.axis_index("wide")
        others = pl.ds(0, target.shape[0] - 1)
        whole = self.small_copy(place, target.at[others], target.at[others], self.beside("c"))
        whole.wait_recv()
        whole.wait_send()
        pltpu.make_async_copy(source_of(me), target.at[me], self.small_local.at[place]).wait()


def spread_matrix(lanes, width, period):
    lane = lax.broadcasted_iota(jnp.int32, (lanes, width), 0).astype(F32)
    column = lax.broadcasted_iota(jnp.int32, (lanes, width), 1).astype(F32)
    place = column - period * jnp.floor((column + 0.5) * (1.0 / period))
    return jnp.where(place == lane, 1.0, 0.0).astype(BF)


def owner_mask(count, width, period):
    owner = lax.broadcasted_iota(jnp.int32, (count, width), 0) * period
    column = lax.broadcasted_iota(jnp.int32, (count, width), 1)
    return (column >= owner) & (column < owner + period)


def split_dot(values, exact, right_dim):
    high = values.astype(BF)
    rest = values - high.astype(F32)
    middle = rest.astype(BF)
    last = (rest - middle.astype(F32)).astype(BF)
    return dot(high, exact, 1, right_dim) + dot(middle, exact, 1, right_dim) + dot(last, exact, 1, right_dim)


def step_kernel(
    length_ref, tokens_ref, cotangent_ref, own_gains_ref, own_bias_ref,
    attend_ref, output_ref, expand_ref, reduce_ref,
    block_ref, gradient_ref, pair_sum_ref, chunk_sum_ref, extra_ref, total_ref,
    pair_ref, chunk_ref, pair_land0, pair_land1, pair_land2, pair_land3,
    chunk_land0, chunk_land1, chunk_land2, chunk_land3,
    normed_ref, upstream_ref, out_ref, back_ref, gains_ref, bias_ref, gains_back_ref, bias_back_ref,
    smalls_ref, extra_send_ref, extras_ref, norm_ref, squares_ref,
    gather_send, gather_recv, scatter_send, scatter_recv, local_sem, small_send, small_recv, small_local,
    load_sem, *work,
):
    t = Traffic(
        dict(
            pair=pair_ref, chunk=chunk_ref, shards=(attend_ref, output_ref, expand_ref, reduce_ref), stage=work[4],
            pair_landing=(pair_land0, pair_land1, pair_land2, pair_land3),
            chunk_landing=(chunk_land0, chunk_land1, chunk_land2, chunk_land3),
            pair_sum=pair_sum_ref, chunk_sum=chunk_sum_ref, squares=squares_ref,
            gather_sems=(gather_send, gather_recv), scatter_sems=(scatter_send, scatter_recv),
            local_sem=local_sem, small_sems=(small_send, small_recv), small_local=small_local,
        )
    )
    slots = normed_ref.shape[0]
    devices = smalls_ref.shape[0]
    gain_width, bias_width = D // devices, FF // devices
    load_tokens = lambda: pltpu.make_async_copy(tokens_ref, normed_ref, load_sem.at[0])
    load_cotangent = lambda: pltpu.make_async_copy(cotangent_ref, upstream_ref, load_sem.at[1])
    load_tokens().start()
    load_cotangent().start()
    for unit in range(UNITS):
        t.load(unit)
    barrier = pltpu.get_barrier_semaphore()
    t.everyone(
        lambda flat, device: pl.semaphore_signal(barrier, inc=1, device_id=device, device_id_type=MESH)
    )
    t.pack(0)
    norm_ref[...] = jnp.zeros_like(norm_ref)
    norm_ref[0:3, 0:gain_width] = own_gains_ref[...]
    norm_ref[3:4, 0:bias_width] = own_bias_ref[...].astype(BF).astype(F32)
    pl.semaphore_wait(barrier, devices - 1)

    t.gather_deep(0)
    small_of = lambda flat: norm_ref
    t.small_send(0, small_of, smalls_ref)
    squares_ref[...] = jnp.zeros_like(squares_ref)
    extra_send_ref[...] = jnp.zeros_like(extra_send_ref)
    load_cotangent().wait()
    load_tokens().wait()

    def prepare(rows):
        upstream_ref[rows, :] = jnp.where(
            below(length_ref, rows), upstream_ref[rows, :].astype(F32), 0.0
        ).astype(BF)
        inputs = normed_ref[rows, :].astype(F32)
        out_ref[rows, :] = inputs
        back_ref[rows, :], _ = row_norm(inputs)

    for unit in range(1, UNITS):
        t.pack(unit)
    over_rows(slots, prepare)
    t.gather_sides(0)
    t.gather_deep(1)
    t.small_wait(0, small_of, smalls_ref)
    gain_spread = spread_matrix(128, D, gain_width)
    gain_owner = owner_mask(devices, D, gain_width)
    for row in range(3):
        spread = split_dot(smalls_ref[:, row, :], gain_spread, 0)
        gains_ref[row : row + 1, :] = jnp.sum(jnp.where(gain_owner, spread, 0.0), axis=0, keepdims=True)
    bias_spread = spread_matrix(128, FF, bias_width)
    bias_owner = owner_mask(devices, FF, bias_width)
    spread = dot(smalls_ref[:, 3, :].astype(BF), bias_spread, 1, 0)
    bias_ref[...] = jnp.sum(jnp.where(bias_owner, spread, 0.0), axis=0, keepdims=True)
    t.gather_forward(0)

    def scale(rows):
        normed_ref[rows, :] = (back_ref[rows, :] * gains_ref[0:1, :]).astype(BF)
        back_ref[rows, :] = jnp.zeros_like(back_ref[rows, :])

    over_rows(slots, scale)
    t.gather_core(0)
    t.gather_sides(1)
    t.gather_deep(2)
    t.gather_done(0)

    events = {
        (0, -1): [(t.gather_deep, 3)],
        (0, 1): [(t.gather_forward, 1), (t.gather_sides, 2), (t.gather_deep, 4), (t.gather_deep, 5)],
        (0, 2): [(t.gather_core, 1)],
        (0, 3): [(t.gather_done, 1), (t.gather_sides, 3)],
        (1, 0): [(t.gather_forward, 2)],
        (1, 1): [(t.gather_forward, 3), (t.gather_sides, 4)],
        (1, 2): [(t.gather_core, 2)],
        (1, 3): [(t.gather_done, 2), (t.scatter_core, 1), (t.gather_core, 3)],
        (2, -1): [(t.gather_sides, 5), (t.scatter_core, 0)],
        (3, -1): [(t.scatter_far, 1), (t.gather_forward, 4), (t.scatter_far, 0)],
        (4, -1): [(t.gather_done, 3), (t.scatter_core, 2), (t.scatter_sides, 1)],
        (5, -1): [(t.gather_core, 4), (t.scatter_far, 2), (t.gather_forward, 5), (t.scatter_sides, 0)],
        (6, -1): [(t.scatter_core, 3), (t.gather_done, 4)],
        (7, -1): [(t.gather_core, 5), (t.scatter_far, 3), (t.scatter_sides, 2), (t.gather_done, 5)],
        (8, -1): [(t.scatter_core, 4), (t.scatter_deep, 1), (t.scatter_deep, 0)],
        (8, 0): [(t.scatter_far, 4), (t.scatter_sides, 3)],
        (8, 1): [(t.scatter_deep, 2), (t.scatter_sides, 4)],
        (8, 2): [(t.scatter_deep, 3)],
        (8, 3): [(t.scatter_core, 5)],
        ("end", 0): [(t.scatter_far, 5)],
        ("end", 1): [(t.scatter_deep, 4), (t.scatter_sides, 5)],
        ("end", 2): [(t.scatter_done, 1)],
        ("end", 3): [
            (t.scatter_deep, 5), (t.scatter_done, 3), (t.scatter_done, 2), (t.scatter_done, 0),
            (t.scatter_done, 4),
        ],
    }

    def finish(place):
        for act, unit in events["end", place]:
            act(unit)

    def run(index, place, sections):
        for section in sections:
            if (section, place) in events:

                @pl.when(index == section)
                def _():
                    for act, unit in events[section, place]:
                        act(unit)

    def step(index, carry):
        is_pair = (index < FIRST_CHUNK) | (index == LAST_PAIR)
        pair_sections = tuple(range(FIRST_CHUNK)) + (LAST_PAIR,)
        chunk_sections = range(FIRST_CHUNK, LAST_PAIR)

        @pl.when(is_pair)
        def _():
            run(index, -1, pair_sections)
            unit = jnp.where(index == LAST_PAIR, PAIRS - 1, index)
            starts = [pl.multiple_of(half * HALF_E + unit * PAIR, PAIR) for half in range(2)]
            gain_of = lambda row: jnp.concatenate(
                [gains_ref[row : row + 1, pl.ds(start, PAIR)] for start in starts], axis=1
            )

            def store(grads, query_back, key_back):
                for half in range(2):
                    pair_ref[unit, half] = grads[half].reshape(pair_ref.shape[2:])
                    cut = slice(half * PAIR, (half + 1) * PAIR)
                    gains_back_ref[1:2, pl.ds(starts[half], PAIR)] = query_back[:, cut]
                    gains_back_ref[2:3, pl.ds(starts[half], PAIR)] = key_back[:, cut]

            attention_section(
                lambda half: pair_ref[unit, half].reshape(D, 4 * PAIR), normed_ref[...], upstream_ref[...],
                gain_of(1), gain_of(2), jnp.where(below(length_ref, pl.ds(0, slots)), 0.0, MASKED),
                out_ref, back_ref, work, store, lambda place: run(index, place, pair_sections),
            )

        @pl.when(~is_pair)
        def _():
            run(index, -1, chunk_sections)
            unit = (index - FIRST_CHUNK) // 2
            half = lax.rem(index - FIRST_CHUNK, 2)
            start = pl.multiple_of(half * HALF_F + unit * CHUNK, CHUNK)
            grad, bias_back = mlp_section(
                chunk_ref[unit, half].reshape(D, 2 * CHUNK), normed_ref[...], upstream_ref[...],
                bias_ref[0:1, pl.ds(start, CHUNK)], out_ref, back_ref,
            )
            chunk_ref[unit, half] = grad.reshape(chunk_ref.shape[2:])
            bias_back_ref[0:1, pl.ds(start, CHUNK)] = bias_back

        return carry

    lax.fori_loop(0, SECTIONS, step, 0)
    load_tokens().start()
    store_block = pltpu.make_async_copy(out_ref, block_ref, load_sem.at[2])
    store_block.start()
    finish(0)
    load_tokens().wait()
    finish_input(normed_ref, gains_ref, upstream_ref, back_ref, gains_back_ref)
    store_gradient = pltpu.make_async_copy(back_ref, gradient_ref, load_sem.at[3])
    store_gradient.start()
    finish(1)
    for row in range(3):
        rows = jnp.where(gain_owner, gains_back_ref[row : row + 1, :], 0.0)
        extra_send_ref[:, row, :] = split_dot(rows, gain_spread, 1)
    rows = jnp.where(bias_owner, bias_back_ref[...], 0.0)
    extra_send_ref[:, 3, :] = split_dot(rows, bias_spread, 1)
    extra_of = lambda flat: extra_send_ref.at[flat]
    t.small_send(1, extra_of, extras_ref)
    finish(2)
    finish(3)
    t.small_wait(1, extra_of, extras_ref)
    extra = jnp.sum(extras_ref[...], axis=0)
    extra_ref[...] = extra
    t.scatter_done(5)
    norm_ref[...] = squares_ref[...] + jnp.full(squares_ref.shape, jnp.sum(extra * extra), F32)
    norm_of = lambda flat: norm_ref
    t.small_send(2, norm_of, smalls_ref)
    store_block.wait()
    store_gradient.wait()
    t.small_wait(2, norm_of, smalls_ref)
    total_ref[...] = jnp.sum(smalls_ref[...], axis=0)


def exchanged_block(lengths, tokens, cotangent, masters):
    attend, output, expand, reduce, bias, gains = turned(masters)
    slots = tokens.shape[0]
    wides = lax.axis_size("wide")
    devices = wides * lax.axis_size("heads")
    deep = wides // 4
    rows = attend.shape[1]
    vmem = pl.BlockSpec(memory_space=pltpu.VMEM)
    hbm = pl.BlockSpec(memory_space=pl.ANY)
    landings = lambda units, pairs, width: [
        pltpu.VMEM((2, 2, deep, 2, rows, width), BF),
        pltpu.VMEM((units, deep, rows, width), BF),
        pltpu.VMEM((pairs, 2, deep, rows, width), BF),
        pltpu.VMEM((units, deep - 1, rows, width), BF),
    ]
    tile = pltpu.VMEM((8, 128), F32)
    tiles = pltpu.VMEM((devices, 8, 128), F32)
    dma = pltpu.SemaphoreType.DMA
    gather_slots, scatter_slots = deep + 7, deep + 4
    block_output, token_gradient, pair_sum, chunk_sum, extra, total = pl.pallas_call(
        step_kernel,
        in_specs=[pl.BlockSpec(memory_space=pltpu.SMEM), hbm, hbm, vmem, vmem, hbm, hbm, hbm, hbm],
        out_specs=[hbm, hbm, vmem, vmem, vmem, vmem],
        out_shape=[
            jax.ShapeDtypeStruct((slots, D), F32),
            jax.ShapeDtypeStruct((slots, D), F32),
            jax.ShapeDtypeStruct((PAIRS, rows, 4 * PAIR), F32),
            jax.ShapeDtypeStruct((CHUNKS, rows, 2 * CHUNK), F32),
            jax.ShapeDtypeStruct((8, 128), F32),
            jax.ShapeDtypeStruct((8, 128), F32),
        ],
        scratch_shapes=[
            pltpu.VMEM((PAIRS, 2, deep, 2, 2, rows, 4 * PAIR), BF),
            pltpu.VMEM((CHUNKS, 2, deep, 2, 2, rows, 2 * CHUNK), BF),
        ]
        + landings(PAIRS, 2, 4 * PAIR)
        + landings(CHUNKS, CHUNKS, 2 * CHUNK)
        + [
            pltpu.VMEM((slots, D), BF), pltpu.VMEM((slots, D), BF),
            pltpu.VMEM((slots, D), F32), pltpu.VMEM((slots, D), F32),
            pltpu.VMEM((3, D), F32), pltpu.VMEM((1, FF), F32),
            pltpu.VMEM((3, D), F32), pltpu.VMEM((1, FF), F32),
            tiles, tiles, tiles, tile, tile,
            dma((UNITS, gather_slots)), dma((UNITS, gather_slots)),
            dma((UNITS, scatter_slots)), dma((UNITS, scatter_slots)),
            dma((UNITS,)), dma((3,)), dma((3,)), dma((3,)), dma((4,)),
        ]
        + attention_scratch(slots),
        compiler_params=pltpu.CompilerParams(
            vmem_limit_bytes=67043328, collective_id=0, has_side_effects=True
        ),
        name="step_block",
    )(lengths, tokens, cotangent, gains, bias, attend, output, expand, reduce)
    return block_output, token_gradient, (pair_sum, chunk_sum, extra, total)


def optimizer_update(
    weight, raw_grad, factor, first, second, average, rate, decay, first_fix, second_fix, keep
):
    clipped = raw_grad * factor
    first_new = BETA_FIRST * first + (1.0 - BETA_FIRST) * clipped
    second_new = BETA_SECOND * second + (1.0 - BETA_SECOND) * clipped * clipped
    direction = first_new / first_fix / (jnp.sqrt(second_new / second_fix) + ADAM_EPS)
    weight_new = weight - rate * (direction + decay * weight)
    average_new = keep * average + (1.0 - keep) * weight_new
    return (clipped, first_new, second_new, weight_new, average_new)


def update_kernel(limit, step_ref, pair_ref, chunk_ref, extra_ref, total_ref, block_in, gradient_in, *refs):
    masters, firsts, seconds, averages = (refs[6 * group : 6 * group + 6] for group in range(4))
    block_out, gradient_out, norm_ref = refs[24:27]
    results = [refs[27 + 5 * index : 32 + 5 * index] for index in range(6)]
    block_out[...] = block_in[...]
    gradient_out[...] = gradient_in[...]

    step = pl.program_id(0)
    norm = jnp.sqrt(total_ref[0:1, :])
    factor = jnp.minimum(1.0, limit / norm)
    step_float = jnp.full((1, PAIR), step_ref[0].astype(F32), F32)
    first_fix = 1.0 - jnp.exp(step_float * math.log(BETA_FIRST))
    second_fix = 1.0 - jnp.exp(step_float * math.log(BETA_SECOND))
    keep = jnp.minimum(AVERAGE_CAP, (1.0 + step_float) / (10.0 + step_float))

    def apply(index, where, raw_grad):
        lanes = raw_grad.shape[1]
        new = optimizer_update(
            masters[index][where], raw_grad, factor[:, :lanes], firsts[index][where],
            seconds[index][where], averages[index][where], RATES[index], DECAYS[index],
            first_fix[:, :lanes], second_fix[:, :lanes], keep[:, :lanes],
        )
        for ref, value in zip(results[index], new):
            ref[where] = value

    everything = slice(None)
    cut = lambda place: slice(place * PAIR, (place + 1) * PAIR)

    @pl.when(step < PAIRS)
    def _():
        for part in range(3):
            apply(0, (part,), pair_ref[0, :, cut(part)])
        apply(1, (everything,), pair_ref[0, :, cut(3)])
        for place in range(CHUNK // PAIR):
            apply(2, (everything, cut(place)), chunk_ref[0, :, cut(place)])
            apply(3, (everything, cut(place)), chunk_ref[0, :, cut(CHUNK // PAIR + place)])

    @pl.when(step == PAIRS)
    def _():
        norm_ref[0] = norm[0, 0]
        apply(4, (everything,), extra_ref[3:4, : masters[4].shape[1]])
        apply(5, (everything,), extra_ref[0:3, : masters[5].shape[1]])


def turned(arrays):
    attend, output, expand, reduce, bias, gains = arrays
    return [attend, output.T, expand, reduce.T, bias[None, :], gains]


def turned_back(arrays):
    attend, output, expand, reduce, bias, gains = arrays
    return [attend, output.T, expand, reduce.T, bias[0], gains]


def updated_weights(step_count, limit, sums, block_output, token_gradient, groups):
    slots = block_output.shape[0]
    arrays = [entry for group in groups for entry in turned(group)]
    shapes = [jax.ShapeDtypeStruct(entry.shape, F32) for entry in arrays[:6] for _ in range(5)]
    steps = PAIRS + 1
    whole = lambda entry: pl.BlockSpec(entry.shape, lambda index: (0,) * len(entry.shape))
    unit = lambda index: jnp.minimum(index, PAIRS - 1)

    def part(entry):
        if entry.shape[0] < 8 and len(entry.shape) == 2:
            return whole(entry)
        block = entry.shape[:-1] + (entry.shape[-1] // PAIRS,)
        return pl.BlockSpec(block, lambda index: (0,) * (len(block) - 1) + (unit(index),))

    unit_part = lambda entry: pl.BlockSpec((1,) + entry.shape[1:], lambda index: (unit(index), 0, 0))
    rows = pl.BlockSpec((slots // steps, D), lambda index: (index, 0))
    smem = pl.BlockSpec(memory_space=pltpu.SMEM)
    image = jax.ShapeDtypeStruct((slots, D), F32)
    out = pl.pallas_call(
        partial(update_kernel, limit),
        grid=(steps,),
        in_specs=[smem]
        + [unit_part(entry) for entry in sums[:2]]
        + [whole(entry) for entry in sums[2:]]
        + [rows, rows]
        + [part(entry) for entry in arrays],
        out_specs=[rows, rows, smem] + [part(entry) for entry in shapes],
        out_shape=[image, image, jax.ShapeDtypeStruct((1,), F32)] + shapes,
        name="update_weights",
    )(step_count, *sums, block_output, token_gradient, *arrays)
    fields = [turned_back(out[3 + field :: 5]) for field in range(5)]
    return out[:3], [fields[field][index] for index in range(6) for field in range(5)]


def pack_shards(attend_weights, output_weights, expand_weights, reduce_weights):
    rows = attend_weights.shape[1]
    attend = attend_weights.astype(BF).reshape(3, rows, PAIRS, PAIR)
    attend = jnp.transpose(attend, (2, 1, 0, 3)).reshape(PAIRS, rows, 3 * PAIR)
    output = jnp.transpose(
        output_weights.astype(BF).T.reshape(rows, PAIRS, PAIR), (1, 0, 2)
    )
    expand = jnp.transpose(expand_weights.astype(BF).reshape(rows, CHUNKS, CHUNK), (1, 0, 2))
    reduce = jnp.transpose(reduce_weights.astype(BF).T.reshape(rows, CHUNKS, CHUNK), (1, 0, 2))
    return jnp.concatenate([attend, output], axis=2), jnp.concatenate([expand, reduce], axis=2)


def unpack_shards(pair_grads, chunk_grads):
    rows = pair_grads.shape[1]
    attend = jnp.transpose(
        pair_grads[:, :, : 3 * PAIR].reshape(PAIRS, rows, 3, PAIR), (2, 1, 0, 3)
    ).reshape(3, rows, HALF_E)
    join = lambda part: jnp.transpose(part, (1, 0, 2)).reshape(rows, -1)
    return (
        attend,
        join(pair_grads[:, :, 3 * PAIR :]).T,
        join(chunk_grads[:, :, :CHUNK]),
        join(chunk_grads[:, :, CHUNK:]).T,
    )


def gathered_block(lengths, tokens, cotangent, norm_gains, expand_bias, pair_own, chunk_own):
    both = ("heads", "wide")
    gains = lax.all_gather(norm_gains, both, axis=1, tiled=True)
    bias = lax.all_gather(expand_bias.astype(BF), both, axis=0, tiled=True).astype(F32)
    whole = lambda own: lax.all_gather(
        lax.all_gather(own, "wide", axis=1, tiled=True), "heads", axis=1
    )
    block_output, token_gradient, pair_grads, chunk_grads, bias_back, gains_back = local_block(
        lengths, tokens, cotangent, gains, bias[None, :], whole(pair_own), whole(chunk_own)
    )
    scatter = lambda part: lax.psum_scatter(
        lax.psum_scatter(part, "heads", scatter_dimension=1),
        "wide", scatter_dimension=1, tiled=True,
    ).astype(F32)
    grads = unpack_shards(scatter(pair_grads), scatter(chunk_grads)) + (
        lax.psum_scatter(bias_back[0], both, scatter_dimension=0, tiled=True),
        lax.psum_scatter(gains_back, both, scatter_dimension=1, tiled=True),
    )
    squares = jnp.sum(jnp.stack([jnp.sum(entry * entry) for entry in grads]))
    return block_output, token_gradient, grads, lax.psum(squares, both)


def body(
    tokens, cotangent, lengths, step_count,
    attend_weights, output_weights, expand_weights, reduce_weights, expand_bias, norm_gains,
    *moments,
):
    masters = (
        attend_weights, output_weights, expand_weights, reduce_weights, expand_bias, norm_gains,
    )
    firsts, seconds, averages = moments[:6], moments[6:12], moments[12:]
    wides = lax.axis_size("wide")
    tokens_all = tokens.shape[1] * lax.axis_size("heads") * wides
    limit = 0.02 * math.sqrt(tokens_all * D * FF)
    if wides % 8 == 0 and attend_weights.shape[1] % 16 == 0 and lax.axis_size("heads") == 2:
        block_output, token_gradient, sums = exchanged_block(lengths, tokens[0], cotangent[0], masters)
        (block_output, token_gradient, grad_norm), updated = updated_weights(
            step_count, limit, sums, block_output, token_gradient, (masters, firsts, seconds, averages)
        )
        return (block_output[None], token_gradient[None], grad_norm, *updated)
    pair_own, chunk_own = pack_shards(*masters[:4])
    block_output, token_gradient, grads, total_squares = gathered_block(
        lengths, tokens[0], cotangent[0], norm_gains, expand_bias, pair_own, chunk_own
    )
    grad_norm = jnp.sqrt(total_squares)
    factor = jnp.minimum(1.0, limit / grad_norm)
    step_float = step_count[0].astype(F32)
    first_fix = 1.0 - jnp.power(BETA_FIRST, step_float)
    second_fix = 1.0 - jnp.power(BETA_SECOND, step_float)
    keep = jnp.minimum(AVERAGE_CAP, (1.0 + step_float) / (10.0 + step_float))
    results = [block_output[None], token_gradient[None], grad_norm.reshape(1)]
    for index in range(6):
        results.extend(
            optimizer_update(
                masters[index], grads[index], factor, firsts[index], seconds[index],
                averages[index], RATES[index], DECAYS[index], first_fix, second_fix, keep,
            )
        )
    return tuple(results)


def solution(mesh):
    both = ("heads", "wide")
    weight_specs = (
        P(None, "wide", "heads"), P("heads", "wide"), P("wide", "heads"), P("heads", "wide"),
        P(both), P(None, both),
    )
    image = P(both, None, None)
    return jax.shard_map(
        body,
        mesh=mesh,
        in_specs=(image, image, P(both), P()) + weight_specs * 4,
        out_specs=(image, image, P()) + tuple(spec for spec in weight_specs for _ in range(5)),
        check_vma=False,
    )
```

```python
from functools import partial
import math

import jax
import jax.numpy as jnp
from jax import lax
from jax.experimental import pallas as pl
from jax.experimental.pallas import tpu as pltpu
from jax.sharding import PartitionSpec as P

D = 768
HEADS = 12
HEAD_DIM = 64
FF = 3072
HALF_E = D // 2
HALF_F = FF // 2
PAIR = 128
PAIRS = HALF_E // PAIR
CHUNK = 512
CHUNKS = HALF_F // CHUNK
QUERY_ROWS = 512
ROWS = 256
BF = jnp.bfloat16
F32 = jnp.float32

NORM_EPS = 1e-06
MASKED = -1e30
BETA_FIRST = 0.9
BETA_SECOND = 0.95
AVERAGE_CAP = 0.9999
ADAM_EPS = 1e-08
RATES = (0.03, 0.2, 0.03, 0.015, 0.3, 0.3)
DECAYS = (0.05, 0.05, 0.05, 0.05, 0.0, 0.0)


def dot(left, right, left_dim, right_dim):
    return lax.dot_general(
        left, right, (((left_dim,), (right_dim,)), ((), ())), preferred_element_type=F32
    )


def row_norm(values):
    center = values - jnp.mean(values, axis=-1, keepdims=True)
    inverse = lax.rsqrt(jnp.mean(center * center, axis=-1, keepdims=True) + NORM_EPS)
    return center * inverse, inverse


def head_mean(values, exact=False):
    width = values.shape[1]
    row = lax.broadcasted_iota(jnp.int32, (width, width), 0) // HEAD_DIM
    column = lax.broadcasted_iota(jnp.int32, (width, width), 1) // HEAD_DIM
    block = jnp.where(row == column, 1.0 / HEAD_DIM, 0.0).astype(BF)
    high = values.astype(BF)
    mean = dot(high, block, 1, 0)
    if not exact:
        return mean
    return mean + dot((values - high.astype(F32)).astype(BF), block, 1, 0)


def head_norm(values):
    center = values - head_mean(values, True)
    inverse = lax.rsqrt(head_mean(center * center) + NORM_EPS)
    return center * inverse, inverse


def head_norm_back(upstream, normal, inverse):
    return inverse * (upstream - head_mean(upstream) - normal * head_mean(upstream * normal))


def pair_attention(query, keyed, value, back_mixed, key_bias):
    rows = query.shape[0]
    lane = lax.broadcasted_iota(jnp.int32, (rows, PAIR), 1)
    low = lane < HEAD_DIM
    first = lane == 0
    zero = jnp.zeros((rows, PAIR), BF)
    one_lane = jnp.where(first, 1.0, 0.0).astype(BF)
    bias_lane = jnp.where(first, key_bias, 0.0).astype(BF)
    query_wide = jnp.concatenate([query, one_lane], axis=1)
    value_wide = jnp.concatenate([value, jnp.ones((rows, PAIR), BF)], axis=1)
    blocks = rows // QUERY_ROWS
    mixed = [[None] * blocks for _ in range(2)]
    back_query = [[None] * blocks for _ in range(2)]
    back_keyed = None
    back_value = None
    lane_q = lane[:QUERY_ROWS]
    low_q = low[:QUERY_ROWS]
    for head in range(2):
        mine = low if head == 0 else ~low
        mine_q = mine[:QUERY_ROWS]
        key_wide = jnp.concatenate([jnp.where(mine, keyed, zero), bias_lane], axis=1)
        query_mine = jnp.where(mine, query, zero)
        for block in range(blocks):
            cut = slice(block * QUERY_ROWS, (block + 1) * QUERY_ROWS)
            expo = jnp.exp(dot(query_wide[cut], key_wide, 1, 1))
            expo_low = expo.astype(BF)
            sums = dot(expo_low, value_wide, 1, 0)
            inverse = 1.0 / sums[:, PAIR:]
            rows_mixed = sums[:, :PAIR] * inverse
            scaled = jnp.where(mine_q, back_mixed[cut].astype(F32) * inverse, 0.0).astype(BF)
            inner = jnp.sum(rows_mixed * scaled.astype(F32), axis=1, keepdims=True)
            inner_high = inner.astype(BF).astype(F32)
            inner_lanes = jnp.where(
                lane_q == 0, -inner_high, jnp.where(lane_q == 1, inner_high - inner, 0.0)
            ).astype(BF)
            centered = dot(jnp.concatenate([scaled, inner_lanes], axis=1), value_wide, 1, 1)
            back_scores = (expo * centered).astype(BF)
            mixed[head][block] = rows_mixed
            back_query[head][block] = dot(back_scores, keyed, 1, 0)
            add_keyed = dot(query_mine[cut], back_scores, 0, 0)
            add_value = dot(scaled, expo_low, 0, 0)
            back_keyed = add_keyed if back_keyed is None else back_keyed + add_keyed
            back_value = add_value if back_value is None else back_value + add_value
    join = lambda parts: jnp.concatenate(
        [jnp.where(low_q, parts[0][block], parts[1][block]) for block in range(blocks)], axis=0
    )
    return join(mixed).astype(BF), join(back_query), back_keyed, back_value


def attention_scratch(slots):
    rows = [pltpu.VMEM((2, slots, PAIR), BF)] * 4 + [pltpu.VMEM((2, slots, PAIR), F32)] * 5
    return rows + [pltpu.VMEM((2, PAIR, slots), F32)]


def attention_section(
    weights, normed, upstream, query_gain, key_gain, key_bias, out_ref, back_ref, work, store,
    pause=lambda place: None,
):
    (
        query_ref, key_ref, value_ref, back_mixed_ref,
        query_hat_ref, query_inv_ref, key_hat_ref, key_inv_ref, back_query_ref, back_keyed_ref,
    ) = work
    three = 3 * PAIR
    halves = (slice(0, PAIR), slice(PAIR, 2 * PAIR))
    both = [weights(half) for half in range(2)]
    into = jnp.concatenate([part[:, :three] for part in both], axis=1)
    out = jnp.concatenate([part[:, three:] for part in both], axis=1)
    projected = dot(normed, into, 1, 0)
    back_mixed = dot(upstream, out, 1, 0).astype(BF)
    pick = lambda place: jnp.concatenate(
        [
            projected[:, place * PAIR : (place + 1) * PAIR],
            projected[:, three + place * PAIR : three + (place + 1) * PAIR],
        ],
        axis=1,
    )
    query_hat, query_inv = head_norm(pick(0))
    key_hat, key_inv = head_norm(pick(1))
    query = (query_hat * query_gain).astype(BF)
    query = (query.astype(F32) * HEAD_DIM ** (-0.5)).astype(BF)
    keyed = (key_hat * key_gain).astype(BF)
    value = pick(2).astype(BF)
    for half, cut in enumerate(halves):
        for ref, rows in (
            (query_ref, query), (key_ref, keyed), (value_ref, value), (back_mixed_ref, back_mixed),
            (query_hat_ref, query_hat), (query_inv_ref, query_inv),
            (key_hat_ref, key_hat), (key_inv_ref, key_inv),
        ):
            ref[half] = rows[:, cut]

    def one_pair(half, carry):
        for place in range(2):
            pl.when(half == place)(partial(pause, place))
        mixed, back_query_ref[half], back_keyed_ref[half], back_value = pair_attention(
            query_ref[half], key_ref[half], value_ref[half], back_mixed_ref[half], key_bias
        )
        query_ref[half] = mixed
        value_ref[half] = back_value.T.astype(BF)
        return carry

    lax.fori_loop(0, 2, one_pair, 0)
    pause(2)
    whole = lambda ref: jnp.concatenate([ref[0], ref[1]], axis=1)
    both = [weights(half) for half in range(2)]
    into = jnp.concatenate([part[:, :three] for part in both], axis=1)
    out = jnp.concatenate([part[:, three:] for part in both], axis=1)
    mixed = whole(query_ref)
    query_hat, key_hat = whole(query_hat_ref), whole(key_hat_ref)
    back_qn = whole(back_query_ref) * HEAD_DIM ** (-0.5)
    back_kn = jnp.concatenate([back_keyed_ref[0].T, back_keyed_ref[1].T], axis=1)
    query_gain_back = jnp.sum(back_qn * query_hat, axis=0, keepdims=True)
    key_gain_back = jnp.sum(back_kn * key_hat, axis=0, keepdims=True)
    back_query = head_norm_back(back_qn * query_gain, query_hat, whole(query_inv_ref)).astype(BF)
    back_keyed = head_norm_back(back_kn * key_gain, key_hat, whole(key_inv_ref)).astype(BF)
    back_into = jnp.concatenate(
        [
            part
            for half, cut in enumerate(halves)
            for part in (back_query[:, cut], back_keyed[:, cut], value_ref[half])
        ],
        axis=1,
    )
    grad_into = dot(normed, back_into, 0, 0).astype(BF)
    grad_out = dot(upstream, mixed, 0, 0).astype(BF)
    grads = [
        jnp.concatenate([grad_into[:, half * three : (half + 1) * three], grad_out[:, cut]], axis=1)
        for half, cut in enumerate(halves)
    ]
    store(grads, query_gain_back, key_gain_back)
    pause(3)
    out_ref[...] += dot(mixed, out, 1, 1)
    back_ref[...] += dot(back_into, into, 1, 1)


def mlp_section(weights, normed, upstream, bias, out_ref, back_ref):
    expand = weights[:, :CHUNK]
    reduce = weights[:, CHUNK:]
    pre = dot(normed, expand, 1, 0) + bias
    back_hidden = dot(upstream, reduce, 1, 0)
    phi = 0.5 * (1.0 + lax.erf(pre * math.sqrt(0.5)))
    density = jnp.exp(-0.5 * pre * pre) * (1.0 / math.sqrt(2.0 * math.pi))
    hidden = (pre * phi).astype(BF)
    back_pre = (back_hidden * (phi + pre * density)).astype(BF)
    out_ref[...] += dot(hidden, reduce, 1, 1)
    back_ref[...] += dot(back_pre, expand, 1, 1)
    grads = [dot(normed, back_pre, 0, 0).astype(BF), dot(upstream, hidden, 0, 0).astype(BF)]
    return jnp.concatenate(grads, axis=1), jnp.sum(back_pre.astype(F32), axis=0, keepdims=True)


def over_rows(slots, act):
    def one(block, carry):
        act(pl.ds(pl.multiple_of(block * ROWS, ROWS), ROWS))
        return carry

    lax.fori_loop(0, slots // ROWS, one, 0)


def below(length_ref, rows):
    place = lax.broadcasted_iota(jnp.int32, (rows.size, 1), 0) + rows.start
    return place < length_ref[0]


def start_input(
    length_ref, tokens_ref, cotangent_ref, gains_ref, normed_ref, upstream_ref, out_ref, back_ref
):
    def one(rows):
        inputs = tokens_ref[rows, :].astype(F32)
        input_hat, _ = row_norm(inputs)
        normed_ref[rows, :] = (input_hat * gains_ref[0:1, :]).astype(BF)
        upstream_ref[rows, :] = jnp.where(
            below(length_ref, rows), cotangent_ref[rows, :].astype(F32), 0.0
        ).astype(BF)
        out_ref[rows, :] = inputs
        back_ref[rows, :] = jnp.zeros_like(inputs)

    over_rows(tokens_ref.shape[0], one)


def finish_input(tokens_ref, gains_ref, upstream_ref, back_ref, gains_back_ref):
    gains_back_ref[0:1, :] = jnp.zeros_like(gains_back_ref[0:1, :])

    def one(rows):
        input_hat, input_inv = row_norm(tokens_ref[rows, :].astype(F32))
        back_normed = back_ref[rows, :]
        gains_back_ref[0:1, :] += jnp.sum(back_normed * input_hat, axis=0, keepdims=True)
        scaled = back_normed * gains_ref[0:1, :]
        back_ref[rows, :] = upstream_ref[rows, :].astype(F32) + input_inv * (
            scaled
            - jnp.mean(scaled, axis=-1, keepdims=True)
            - input_hat * jnp.mean(scaled * input_hat, axis=-1, keepdims=True)
        )

    over_rows(tokens_ref.shape[0], one)


def local_kernel(
    length_ref, tokens_ref, cotangent_ref, gains_ref, bias_ref, pair_ref, chunk_ref,
    out_ref, back_ref, grad_pair_ref, grad_chunk_ref, bias_back_ref, gains_back_ref,
    normed_ref, upstream_ref, *work,
):
    index = pl.program_id(0)

    @pl.when(index == 0)
    def _():
        start_input(
            length_ref, tokens_ref, cotangent_ref, gains_ref, normed_ref, upstream_ref, out_ref, back_ref
        )

    is_pair = (index == 0) | (index > 2 * CHUNKS)

    @pl.when(is_pair)
    def _():
        unit = jnp.where(index == 0, 0, index - 2 * CHUNKS)
        starts = [pl.multiple_of(half * HALF_E + unit * PAIR, PAIR) for half in range(2)]
        gain_of = lambda row: jnp.concatenate(
            [gains_ref[row : row + 1, pl.ds(start, PAIR)] for start in starts], axis=1
        )
        place = lax.broadcasted_iota(jnp.int32, (tokens_ref.shape[0], 1), 0)

        def store(grads, query_back, key_back):
            for half in range(2):
                grad_pair_ref[0, half] = grads[half]
                cut = slice(half * PAIR, (half + 1) * PAIR)
                gains_back_ref[1:2, pl.ds(starts[half], PAIR)] = query_back[:, cut]
                gains_back_ref[2:3, pl.ds(starts[half], PAIR)] = key_back[:, cut]

        attention_section(
            lambda half: pair_ref[0, half], normed_ref[...], upstream_ref[...],
            gain_of(1), gain_of(2), jnp.where(place < length_ref[0], 0.0, MASKED), out_ref, back_ref, work,
            store,
        )

    @pl.when(~is_pair)
    def _():
        unit = (index - 1) // 2
        half = lax.rem(index - 1, 2)
        start = pl.multiple_of(half * HALF_F + unit * CHUNK, CHUNK)
        grad, bias_back = mlp_section(
            chunk_ref[0, 0], normed_ref[...], upstream_ref[...],
            bias_ref[0:1, pl.ds(start, CHUNK)], out_ref, back_ref,
        )
        grad_chunk_ref[0, 0] = grad
        bias_back_ref[0:1, pl.ds(start, CHUNK)] = bias_back

    @pl.when(index == PAIRS + 2 * CHUNKS - 1)
    def _():
        finish_input(tokens_ref, gains_ref, upstream_ref, back_ref, gains_back_ref)


def local_block(length, tokens, cotangent, gains, bias, pair_weights, chunk_weights):
    slots = tokens.shape[0]
    steps = PAIRS + 2 * CHUNKS
    whole = lambda shape: pl.BlockSpec(shape, lambda index: (0,) * len(shape))
    pair_at = lambda index: (jnp.maximum(index - 2 * CHUNKS, 0), 0, 0, 0)

    def chunk_at(index):
        flat = jnp.clip(index - 1, 0, 2 * CHUNKS - 1)
        return (flat // 2, lax.rem(flat, 2), 0, 0)

    pair_spec = pl.BlockSpec((1, 2, D, 4 * PAIR), pair_at)
    chunk_spec = pl.BlockSpec((1, 1, D, 2 * CHUNK), chunk_at)
    return pl.pallas_call(
        local_kernel,
        grid=(steps,),
        in_specs=[
            pl.BlockSpec(memory_space=pltpu.SMEM),
            whole((slots, D)), whole((slots, D)), whole((3, D)), whole((1, FF)), pair_spec, chunk_spec,
        ],
        out_specs=[
            whole((slots, D)), whole((slots, D)), pair_spec, chunk_spec, whole((1, FF)), whole((3, D)),
        ],
        out_shape=[
            jax.ShapeDtypeStruct((slots, D), F32),
            jax.ShapeDtypeStruct((slots, D), F32),
            jax.ShapeDtypeStruct((PAIRS, 2, D, 4 * PAIR), BF),
            jax.ShapeDtypeStruct((CHUNKS, 2, D, 2 * CHUNK), BF),
            jax.ShapeDtypeStruct((1, FF), F32),
            jax.ShapeDtypeStruct((3, D), F32),
        ],
        scratch_shapes=[pltpu.VMEM((slots, D), BF), pltpu.VMEM((slots, D), BF)]
        + attention_scratch(slots),
        compiler_params=pltpu.CompilerParams(vmem_limit_bytes=60 << 20),
        name="local_block",
    )(length, tokens, cotangent, gains, bias, pair_weights, chunk_weights)


PAIR_UNITS = (0, 1, 5)
CHUNK_UNITS = (2, 3, 4)
UNITS = 6
SECTIONS = PAIRS + 2 * CHUNKS
FIRST_CHUNK = 2
LAST_PAIR = SECTIONS - 1
GATHER_COPIES = 11
SCATTER_COPIES = 8
MESH = pl.DeviceIdType.MESH


class Traffic:
    def __init__(self, refs):
        self.__dict__.update(refs)
        self.deep = self.pair.shape[2]
        self.h = lax.axis_index("heads")
        wide = lax.axis_index("wide")
        self.c = lax.rem(wide, 2)
        self.b = lax.rem(wide // 2, 2)
        self.a = wide // 4

    def buffer(self, unit):
        if unit in PAIR_UNITS:
            return self.pair.at[PAIR_UNITS.index(unit)]
        return self.chunk.at[CHUNK_UNITS.index(unit)]

    def landing(self, unit, stage):
        pair = unit in PAIR_UNITS
        landing = (self.pair_landing if pair else self.chunk_landing)[stage]
        return landing.at[(PAIR_UNITS if pair else CHUNK_UNITS).index(unit) % landing.shape[0]]

    def device(self, h=None, a=None, b=None, c=None):
        h = self.h if h is None else h
        a = self.a if a is None else a
        b = self.b if b is None else b
        c = self.c if c is None else c
        return (h, (a * 2 + b) * 2 + c)

    def beside(self, axis):
        if axis == "h":
            return self.device(h=1 - self.h)
        if axis == "b":
            return self.device(b=1 - self.b)
        return self.device(c=1 - self.c)

    def along(self, step):
        return self.device(a=lax.rem(self.a + step, self.deep))

    def copy(self, source, target, sems, unit, slot, device):
        send, recv = sems
        return pltpu.make_async_remote_copy(
            src_ref=source, dst_ref=target, send_sem=send.at[unit, slot], recv_sem=recv.at[unit, slot],
            device_id=device, device_id_type=MESH,
        )

    def gather_copy(self, unit, slot):
        buf, half = self.buffer(unit), self.deep // 2
        h, a, b, c = self.h, self.a, self.b, self.c
        if slot < self.deep - 1:
            return self.copy(buf.at[h, a, b, c], buf.at[h, a, b, c], self.gather_sems, unit, slot, self.along(slot + 1))
        slot -= self.deep - 1
        region, device = (
            (lambda r: r.at[h, :, b, c], self.beside("h")),
            (lambda r: r.at[h, :, b, c], self.beside("b")),
            (lambda r: r.at[1 - h, pl.ds(0, half), b, c], self.beside("b")),
            (lambda r: r.at[h, pl.ds(half, self.deep - half), 1 - b, c], self.beside("h")),
            (lambda r: r.at[h, :, b, c], self.beside("c")),
            (lambda r: r.at[1 - h, :, b, c], self.beside("c")),
            (lambda r: r.at[h, :, 1 - b, c], self.beside("c")),
            (lambda r: r.at[1 - h, :, 1 - b, c], self.beside("c")),
        )[slot]
        return self.copy(
            region(buf), region(buf), self.gather_sems, unit, slot + self.deep - 1, device
        )

    def gather_start(self, unit, slots):
        for slot in slots:
            self.gather_copy(unit, slot).start()

    def gather_wait(self, unit, slots):
        for slot in slots:
            self.gather_copy(unit, slot).wait_recv()

    def pieces(self, unit):
        cut = lambda place: pl.ds(place * PAIR, PAIR)
        attend, output, expand, reduce = self.shards
        if unit in PAIR_UNITS:
            place = PAIR_UNITS.index(unit)
            return [attend.at[part, :, cut(place)] for part in range(3)] + [output.at[:, cut(place)]]
        first = CHUNK_UNITS.index(unit) * (CHUNK // PAIR)
        return [ref.at[:, cut(first + place)] for ref in (expand, reduce) for place in range(CHUNK // PAIR)]

    def staged(self, unit):
        rows, count = self.pair.shape[5], len(self.pieces(unit))
        half, first = ((0, 0), (0, 4), (0, 8), (1, 0), (1, 8), (0, 16))[unit]
        return self.stage.at[half, pl.ds(first * rows, count * rows), :]

    def load(self, unit):
        rows = self.pair.shape[5]
        for place, piece in enumerate(self.pieces(unit)):
            pltpu.make_async_copy(
                piece, self.staged(unit).at[pl.ds(place * rows, rows), :], self.local_sem.at[unit]
            ).start()

    def pack(self, unit):
        rows, staged, buf = self.pair.shape[5], self.staged(unit), self.buffer(unit)
        pltpu.make_async_copy(staged, staged, self.local_sem.at[unit]).wait()
        for place in range(len(self.pieces(unit))):
            buf[self.h, self.a, self.b, self.c, :, place * PAIR : (place + 1) * PAIR] = staged[
                place * rows : (place + 1) * rows, :
            ].astype(BF)

    def gather_deep(self, unit):
        self.gather_start(unit, range(self.deep - 1))

    def gather_sides(self, unit):
        n = self.deep - 1
        self.gather_wait(unit, range(n))
        self.gather_start(unit, (n, n + 1, n + 4))

    def gather_forward(self, unit):
        n = self.deep - 1
        self.gather_wait(unit, (n, n + 1))
        self.gather_start(unit, (n + 2, n + 3, n + 5, n + 6))

    def gather_core(self, unit):
        n = self.deep - 1
        self.gather_wait(unit, (n + 2, n + 3))
        self.gather_start(unit, (n + 7,))

    def gather_done(self, unit):
        n = self.deep - 1
        self.gather_wait(unit, range(n + 4, n + 8))
        for slot in range(n + 8):
            self.gather_copy(unit, slot).wait_send()

    def scatter_copy(self, unit, slot):
        buf, half = self.buffer(unit), self.deep // 2
        h, a, b, c = self.h, self.a, self.b, self.c
        land = lambda stage: self.landing(unit, stage)
        rest = self.deep - half
        if slot >= 5:
            step = slot - 4
            source = buf.at[h, lax.rem(a + step, self.deep), b, c]
            target, device = land(3).at[step - 1], self.along(step)
        else:
            source, target, device = (
                lambda: (buf.at[:, :, :, 1 - c], land(0), self.beside("c")),
                lambda: (buf.at[1 - h, pl.ds(0, half), 1 - b, c], land(1).at[pl.ds(0, half)], self.beside("b")),
                lambda: (buf.at[1 - h, pl.ds(half, rest), 1 - b, c], land(1).at[pl.ds(half, rest)], self.beside("h")),
                lambda: (buf.at[1 - h, :, b, c], land(2).at[0], self.beside("h")),
                lambda: (buf.at[h, :, 1 - b, c], land(2).at[1], self.beside("b")),
            )[slot]()
        return self.copy(source, target, self.scatter_sems, unit, slot, device)

    def scatter_start(self, unit, slots):
        for slot in slots:
            self.scatter_copy(unit, slot).start()

    def scatter_wait(self, unit, slots):
        for slot in slots:
            self.scatter_copy(unit, slot).wait_recv()

    def add(self, unit, where, *parts):
        buf = self.buffer(unit)
        if len(parts) == 1:
            buf[where] = buf[where] + parts[0]
            return
        total = buf[where].astype(F32)
        for part in parts:
            total = total + part.astype(F32)
        buf[where] = total.astype(BF)

    def scatter_core(self, unit):
        self.scatter_start(unit, (0,))

    def scatter_far(self, unit):
        h, b, c = self.h, self.b, self.c
        self.scatter_wait(unit, (0,))
        got = self.landing(unit, 0)
        far = (1 - h, slice(None), 1 - b)
        self.add(unit, far + (c,), got[far])
        self.scatter_start(unit, (1, 2))
        for near in ((1 - h, slice(None), b), (h, slice(None), 1 - b), (h, slice(None), b)):
            self.add(unit, near + (c,), got[near])

    def scatter_sides(self, unit):
        h, b, c, half = self.h, self.b, self.c, self.deep // 2
        self.scatter_wait(unit, (1, 2))
        got = self.landing(unit, 1)
        self.add(unit, (1 - h, slice(0, half), b, c), got[0:half])
        self.add(unit, (h, slice(half, self.deep), 1 - b, c), got[half : self.deep])
        self.scatter_start(unit, (3, 4))

    def scatter_deep(self, unit):
        self.scatter_wait(unit, (3, 4))
        got = self.landing(unit, 2)
        self.add(unit, (self.h, slice(None), self.b, self.c), got[0], got[1])
        self.scatter_start(unit, range(5, 4 + self.deep))

    def scatter_done(self, unit):
        self.scatter_wait(unit, range(5, 4 + self.deep))
        got = self.landing(unit, 3)
        total = self.buffer(unit)[self.h, self.a, self.b, self.c].astype(F32)
        for step in range(self.deep - 1):
            total = total + got[step].astype(F32)
        if unit in PAIR_UNITS:
            self.pair_sum[PAIR_UNITS.index(unit)] = total
        else:
            self.chunk_sum[CHUNK_UNITS.index(unit)] = total
        self.squares[...] += jnp.full(self.squares.shape, jnp.sum(total * total), F32)
        for slot in range(4 + self.deep):
            self.scatter_copy(unit, slot).wait_send()

    def everyone(self, act):
        wides = lax.axis_size("wide")
        count = wides * lax.axis_size("heads")
        me = self.h * wides + lax.axis_index("wide")

        def one(step, carry):
            flat = lax.rem(me + step, count)
            act(flat, (flat // wides, lax.rem(flat, wides)))
            return carry

        lax.fori_loop(1, count, one, 0)

    def small_copy(self, place, source, target, device):
        send, recv = self.small_sems
        return pltpu.make_async_remote_copy(
            src_ref=source, dst_ref=target, send_sem=send.at[place], recv_sem=recv.at[place],
            device_id=device, device_id_type=MESH,
        )

    def small_send(self, place, source_of, target):
        me = self.h * lax.axis_size("wide") + lax.axis_index("wide")
        self.everyone(
            lambda flat, device: self.small_copy(place, source_of(flat), target.at[me], device).start()
        )
        pltpu.make_async_copy(source_of(me), target.at[me], self.small_local.at[place]).start()

    def small_wait(self, place, source_of, target):
        me = self.h * lax.axis_size("wide") + lax.axis_index("wide")
        others = pl.ds(0, target.shape[0] - 1)
        whole = self.small_copy(place, target.at[others], target.at[others], self.beside("c"))
        whole.wait_recv()
        whole.wait_send()
        pltpu.make_async_copy(source_of(me), target.at[me], self.small_local.at[place]).wait()


def spread_matrix(lanes, width, period):
    lane = lax.broadcasted_iota(jnp.int32, (lanes, width), 0).astype(F32)
    column = lax.broadcasted_iota(jnp.int32, (lanes, width), 1).astype(F32)
    place = column - period * jnp.floor((column + 0.5) * (1.0 / period))
    return jnp.where(place == lane, 1.0, 0.0).astype(BF)


def owner_mask(count, width, period):
    owner = lax.broadcasted_iota(jnp.int32, (count, width), 0) * period
    column = lax.broadcasted_iota(jnp.int32, (count, width), 1)
    return (column >= owner) & (column < owner + period)


def split_dot(values, exact, right_dim):
    high = values.astype(BF)
    rest = values - high.astype(F32)
    middle = rest.astype(BF)
    last = (rest - middle.astype(F32)).astype(BF)
    return dot(high, exact, 1, right_dim) + dot(middle, exact, 1, right_dim) + dot(last, exact, 1, right_dim)


def step_kernel(
    length_ref, tokens_ref, cotangent_ref, own_gains_ref, own_bias_ref,
    attend_ref, output_ref, expand_ref, reduce_ref,
    block_ref, gradient_ref, pair_sum_ref, chunk_sum_ref, extra_ref, total_ref,
    pair_ref, chunk_ref, pair_land0, pair_land1, pair_land2, pair_land3,
    chunk_land0, chunk_land1, chunk_land2, chunk_land3,
    normed_ref, upstream_ref, out_ref, back_ref, gains_ref, bias_ref, gains_back_ref, bias_back_ref,
    smalls_ref, extra_send_ref, extras_ref, norm_ref, squares_ref,
    gather_send, gather_recv, scatter_send, scatter_recv, local_sem, small_send, small_recv, small_local,
    load_sem, *work,
):
    t = Traffic(
        dict(
            pair=pair_ref, chunk=chunk_ref, shards=(attend_ref, output_ref, expand_ref, reduce_ref), stage=work[4],
            pair_landing=(pair_land0, pair_land1, pair_land2, pair_land3),
            chunk_landing=(chunk_land0, chunk_land1, chunk_land2, chunk_land3),
            pair_sum=pair_sum_ref, chunk_sum=chunk_sum_ref, squares=squares_ref,
            gather_sems=(gather_send, gather_recv), scatter_sems=(scatter_send, scatter_recv),
            local_sem=local_sem, small_sems=(small_send, small_recv), small_local=small_local,
        )
    )
    slots = normed_ref.shape[0]
    devices = smalls_ref.shape[0]
    gain_width, bias_width = D // devices, FF // devices
    load_tokens = lambda: pltpu.make_async_copy(tokens_ref, normed_ref, load_sem.at[0])
    load_cotangent = lambda: pltpu.make_async_copy(cotangent_ref, upstream_ref, load_sem.at[1])
    load_tokens().start()
    load_cotangent().start()
    for unit in range(UNITS):
        t.load(unit)
    barrier = pltpu.get_barrier_semaphore()
    t.everyone(
        lambda flat, device: pl.semaphore_signal(barrier, inc=1, device_id=device, device_id_type=MESH)
    )
    t.pack(0)
    norm_ref[...] = jnp.zeros_like(norm_ref)
    norm_ref[0:3, 0:gain_width] = own_gains_ref[...]
    norm_ref[3:4, 0:bias_width] = own_bias_ref[...].astype(BF).astype(F32)
    pl.semaphore_wait(barrier, devices - 1)

    t.gather_deep(0)
    small_of = lambda flat: norm_ref
    t.small_send(0, small_of, smalls_ref)
    squares_ref[...] = jnp.zeros_like(squares_ref)
    extra_send_ref[...] = jnp.zeros_like(extra_send_ref)
    load_cotangent().wait()
    load_tokens().wait()

    def prepare(rows):
        upstream_ref[rows, :] = jnp.where(
            below(length_ref, rows), upstream_ref[rows, :].astype(F32), 0.0
        ).astype(BF)
        inputs = normed_ref[rows, :].astype(F32)
        out_ref[rows, :] = inputs
        back_ref[rows, :], _ = row_norm(inputs)

    for unit in range(1, UNITS):
        t.pack(unit)
    over_rows(slots, prepare)
    t.gather_sides(0)
    t.gather_deep(1)
    t.small_wait(0, small_of, smalls_ref)
    gain_spread = spread_matrix(128, D, gain_width)
    gain_owner = owner_mask(devices, D, gain_width)
    for row in range(3):
        spread = split_dot(smalls_ref[:, row, :], gain_spread, 0)
        gains_ref[row : row + 1, :] = jnp.sum(jnp.where(gain_owner, spread, 0.0), axis=0, keepdims=True)
    bias_spread = spread_matrix(128, FF, bias_width)
    bias_owner = owner_mask(devices, FF, bias_width)
    spread = dot(smalls_ref[:, 3, :].astype(BF), bias_spread, 1, 0)
    bias_ref[...] = jnp.sum(jnp.where(bias_owner, spread, 0.0), axis=0, keepdims=True)
    t.gather_forward(0)

    def scale(rows):
        normed_ref[rows, :] = (back_ref[rows, :] * gains_ref[0:1, :]).astype(BF)
        back_ref[rows, :] = jnp.zeros_like(back_ref[rows, :])

    over_rows(slots, scale)
    t.gather_core(0)
    t.gather_sides(1)
    t.gather_deep(2)
    t.gather_done(0)

    events = {
        (0, -1): [(t.gather_deep, 3)],
        (0, 1): [(t.gather_forward, 1), (t.gather_sides, 2), (t.gather_deep, 4), (t.gather_deep, 5)],
        (0, 2): [(t.gather_core, 1)],
        (0, 3): [(t.gather_done, 1), (t.gather_sides, 3)],
        (1, 0): [(t.gather_forward, 2)],
        (1, 1): [(t.gather_forward, 3), (t.gather_sides, 4)],
        (1, 2): [(t.gather_core, 2)],
        (1, 3): [(t.gather_done, 2), (t.scatter_core, 1), (t.gather_core, 3)],
        (2, -1): [(t.gather_sides, 5), (t.scatter_core, 0)],
        (3, -1): [(t.scatter_far, 1), (t.gather_forward, 4), (t.scatter_far, 0)],
        (4, -1): [(t.gather_done, 3), (t.scatter_core, 2), (t.scatter_sides, 1)],
        (5, -1): [(t.gather_core, 4), (t.scatter_far, 2), (t.gather_forward, 5), (t.scatter_sides, 0)],
        (6, -1): [(t.scatter_core, 3), (t.gather_done, 4)],
        (7, -1): [(t.gather_core, 5), (t.scatter_far, 3), (t.scatter_sides, 2), (t.gather_done, 5)],
        (8, -1): [(t.scatter_core, 4), (t.scatter_deep, 1), (t.scatter_deep, 0)],
        (8, 0): [(t.scatter_far, 4), (t.scatter_sides, 3)],
        (8, 1): [(t.scatter_deep, 2), (t.scatter_sides, 4)],
        (8, 2): [(t.scatter_deep, 3)],
        (8, 3): [(t.scatter_core, 5)],
        ("end", 0): [(t.scatter_far, 5)],
        ("end", 1): [(t.scatter_deep, 4), (t.scatter_sides, 5)],
        ("end", 2): [(t.scatter_done, 1)],
        ("end", 3): [
            (t.scatter_deep, 5), (t.scatter_done, 3), (t.scatter_done, 2), (t.scatter_done, 0),
            (t.scatter_done, 4),
        ],
    }

    def finish(place):
        for act, unit in events["end", place]:
            act(unit)

    def run(index, place, sections):
        for section in sections:
            if (section, place) in events:

                @pl.when(index == section)
                def _():
                    for act, unit in events[section, place]:
                        act(unit)

    def step(index, carry):
        is_pair = (index < FIRST_CHUNK) | (index == LAST_PAIR)
        pair_sections = tuple(range(FIRST_CHUNK)) + (LAST_PAIR,)
        chunk_sections = range(FIRST_CHUNK, LAST_PAIR)

        @pl.when(is_pair)
        def _():
            run(index, -1, pair_sections)
            unit = jnp.where(index == LAST_PAIR, PAIRS - 1, index)
            starts = [pl.multiple_of(half * HALF_E + unit * PAIR, PAIR) for half in range(2)]
            gain_of = lambda row: jnp.concatenate(
                [gains_ref[row : row + 1, pl.ds(start, PAIR)] for start in starts], axis=1
            )

            def store(grads, query_back, key_back):
                for half in range(2):
                    pair_ref[unit, half] = grads[half].reshape(pair_ref.shape[2:])
                    cut = slice(half * PAIR, (half + 1) * PAIR)
                    gains_back_ref[1:2, pl.ds(starts[half], PAIR)] = query_back[:, cut]
                    gains_back_ref[2:3, pl.ds(starts[half], PAIR)] = key_back[:, cut]

            attention_section(
                lambda half: pair_ref[unit, half].reshape(D, 4 * PAIR), normed_ref[...], upstream_ref[...],
                gain_of(1), gain_of(2), jnp.where(below(length_ref, pl.ds(0, slots)), 0.0, MASKED),
                out_ref, back_ref, work, store, lambda place: run(index, place, pair_sections),
            )

        @pl.when(~is_pair)
        def _():
            run(index, -1, chunk_sections)
            unit = (index - FIRST_CHUNK) // 2
            half = lax.rem(index - FIRST_CHUNK, 2)
            start = pl.multiple_of(half * HALF_F + unit * CHUNK, CHUNK)
            grad, bias_back = mlp_section(
                chunk_ref[unit, half].reshape(D, 2 * CHUNK), normed_ref[...], upstream_ref[...],
                bias_ref[0:1, pl.ds(start, CHUNK)], out_ref, back_ref,
            )
            chunk_ref[unit, half] = grad.reshape(chunk_ref.shape[2:])
            bias_back_ref[0:1, pl.ds(start, CHUNK)] = bias_back

        return carry

    lax.fori_loop(0, SECTIONS, step, 0)
    load_tokens().start()
    store_block = pltpu.make_async_copy(out_ref, block_ref, load_sem.at[2])
    store_block.start()
    finish(0)
    load_tokens().wait()
    finish_input(normed_ref, gains_ref, upstream_ref, back_ref, gains_back_ref)
    store_gradient = pltpu.make_async_copy(back_ref, gradient_ref, load_sem.at[3])
    store_gradient.start()
    finish(1)
    for row in range(3):
        rows = jnp.where(gain_owner, gains_back_ref[row : row + 1, :], 0.0)
        extra_send_ref[:, row, :] = split_dot(rows, gain_spread, 1)
    rows = jnp.where(bias_owner, bias_back_ref[...], 0.0)
    extra_send_ref[:, 3, :] = split_dot(rows, bias_spread, 1)
    extra_of = lambda flat: extra_send_ref.at[flat]
    t.small_send(1, extra_of, extras_ref)
    finish(2)
    finish(3)
    t.small_wait(1, extra_of, extras_ref)
    extra = jnp.sum(extras_ref[...], axis=0)
    extra_ref[...] = extra
    t.scatter_done(5)
    norm_ref[...] = squares_ref[...] + jnp.full(squares_ref.shape, jnp.sum(extra * extra), F32)
    norm_of = lambda flat: norm_ref
    t.small_send(2, norm_of, smalls_ref)
    store_block.wait()
    store_gradient.wait()
    t.small_wait(2, norm_of, smalls_ref)
    total_ref[...] = jnp.sum(smalls_ref[...], axis=0)


def exchanged_block(lengths, tokens, cotangent, masters):
    attend, output, expand, reduce, bias, gains = turned(masters)
    slots = tokens.shape[0]
    wides = lax.axis_size("wide")
    devices = wides * lax.axis_size("heads")
    deep = wides // 4
    rows = attend.shape[1]
    vmem = pl.BlockSpec(memory_space=pltpu.VMEM)
    hbm = pl.BlockSpec(memory_space=pl.ANY)
    landings = lambda units, pairs, width: [
        pltpu.VMEM((2, 2, deep, 2, rows, width), BF),
        pltpu.VMEM((units, deep, rows, width), BF),
        pltpu.VMEM((pairs, 2, deep, rows, width), BF),
        pltpu.VMEM((units, deep - 1, rows, width), BF),
    ]
    tile = pltpu.VMEM((8, 128), F32)
    tiles = pltpu.VMEM((devices, 8, 128), F32)
    dma = pltpu.SemaphoreType.DMA
    gather_slots, scatter_slots = deep + 7, deep + 4
    block_output, token_gradient, pair_sum, chunk_sum, extra, total = pl.pallas_call(
        step_kernel,
        in_specs=[pl.BlockSpec(memory_space=pltpu.SMEM), hbm, hbm, vmem, vmem, hbm, hbm, hbm, hbm],
        out_specs=[hbm, hbm, vmem, vmem, vmem, vmem],
        out_shape=[
            jax.ShapeDtypeStruct((slots, D), F32),
            jax.ShapeDtypeStruct((slots, D), F32),
            jax.ShapeDtypeStruct((PAIRS, rows, 4 * PAIR), F32),
            jax.ShapeDtypeStruct((CHUNKS, rows, 2 * CHUNK), F32),
            jax.ShapeDtypeStruct((8, 128), F32),
            jax.ShapeDtypeStruct((8, 128), F32),
        ],
        scratch_shapes=[
            pltpu.VMEM((PAIRS, 2, deep, 2, 2, rows, 4 * PAIR), BF),
            pltpu.VMEM((CHUNKS, 2, deep, 2, 2, rows, 2 * CHUNK), BF),
        ]
        + landings(PAIRS, 2, 4 * PAIR)
        + landings(CHUNKS, CHUNKS, 2 * CHUNK)
        + [
            pltpu.VMEM((slots, D), BF), pltpu.VMEM((slots, D), BF),
            pltpu.VMEM((slots, D), F32), pltpu.VMEM((slots, D), F32),
            pltpu.VMEM((3, D), F32), pltpu.VMEM((1, FF), F32),
            pltpu.VMEM((3, D), F32), pltpu.VMEM((1, FF), F32),
            tiles, tiles, tiles, tile, tile,
            dma((UNITS, gather_slots)), dma((UNITS, gather_slots)),
            dma((UNITS, scatter_slots)), dma((UNITS, scatter_slots)),
            dma((UNITS,)), dma((3,)), dma((3,)), dma((3,)), dma((4,)),
        ]
        + attention_scratch(slots),
        compiler_params=pltpu.CompilerParams(
            vmem_limit_bytes=67043328, collective_id=0, has_side_effects=True
        ),
        name="step_block",
    )(lengths, tokens, cotangent, gains, bias, attend, output, expand, reduce)
    return block_output, token_gradient, (pair_sum, chunk_sum, extra, total)


def optimizer_update(
    weight, raw_grad, factor, first, second, average, rate, decay, first_fix, second_fix, keep
):
    clipped = raw_grad * factor
    first_new = BETA_FIRST * first + (1.0 - BETA_FIRST) * clipped
    second_new = BETA_SECOND * second + (1.0 - BETA_SECOND) * clipped * clipped
    direction = first_new / first_fix / (jnp.sqrt(second_new / second_fix) + ADAM_EPS)
    weight_new = weight - rate * (direction + decay * weight)
    average_new = keep * average + (1.0 - keep) * weight_new
    return (clipped, first_new, second_new, weight_new, average_new)


def update_kernel(limit, step_ref, pair_ref, chunk_ref, extra_ref, total_ref, block_in, gradient_in, *refs):
    masters, firsts, seconds, averages = (refs[6 * group : 6 * group + 6] for group in range(4))
    block_out, gradient_out, norm_ref = refs[24:27]
    results = [refs[27 + 5 * index : 32 + 5 * index] for index in range(6)]
    block_out[...] = block_in[...]
    gradient_out[...] = gradient_in[...]

    step = pl.program_id(0)
    norm = jnp.sqrt(total_ref[0:1, :])
    factor = jnp.minimum(1.0, limit / norm)
    step_float = jnp.full((1, PAIR), step_ref[0].astype(F32), F32)
    first_fix = 1.0 - jnp.exp(step_float * math.log(BETA_FIRST))
    second_fix = 1.0 - jnp.exp(step_float * math.log(BETA_SECOND))
    keep = jnp.minimum(AVERAGE_CAP, (1.0 + step_float) / (10.0 + step_float))

    def apply(index, where, raw_grad):
        lanes = raw_grad.shape[1]
        new = optimizer_update(
            masters[index][where], raw_grad, factor[:, :lanes], firsts[index][where],
            seconds[index][where], averages[index][where], RATES[index], DECAYS[index],
            first_fix[:, :lanes], second_fix[:, :lanes], keep[:, :lanes],
        )
        for ref, value in zip(results[index], new):
            ref[where] = value

    everything = slice(None)
    cut = lambda place: slice(place * PAIR, (place + 1) * PAIR)

    @pl.when(step < PAIRS)
    def _():
        for part in range(3):
            apply(0, (part,), pair_ref[0, :, cut(part)])
        apply(1, (everything,), pair_ref[0, :, cut(3)])
        for place in range(CHUNK // PAIR):
            apply(2, (everything, cut(place)), chunk_ref[0, :, cut(place)])
            apply(3, (everything, cut(place)), chunk_ref[0, :, cut(CHUNK // PAIR + place)])

    @pl.when(step == PAIRS)
    def _():
        norm_ref[0] = norm[0, 0]
        apply(4, (everything,), extra_ref[3:4, : masters[4].shape[1]])
        apply(5, (everything,), extra_ref[0:3, : masters[5].shape[1]])


def turned(arrays):
    attend, output, expand, reduce, bias, gains = arrays
    return [attend, output.T, expand, reduce.T, bias[None, :], gains]


def turned_back(arrays):
    attend, output, expand, reduce, bias, gains = arrays
    return [attend, output.T, expand, reduce.T, bias[0], gains]


def updated_weights(step_count, limit, sums, block_output, token_gradient, groups):
    slots = block_output.shape[0]
    arrays = [entry for group in groups for entry in turned(group)]
    shapes = [jax.ShapeDtypeStruct(entry.shape, F32) for entry in arrays[:6] for _ in range(5)]
    steps = PAIRS + 1
    whole = lambda entry: pl.BlockSpec(entry.shape, lambda index: (0,) * len(entry.shape))
    unit = lambda index: jnp.minimum(index, PAIRS - 1)

    def part(entry):
        if entry.shape[0] < 8 and len(entry.shape) == 2:
            return whole(entry)
        block = entry.shape[:-1] + (entry.shape[-1] // PAIRS,)
        return pl.BlockSpec(block, lambda index: (0,) * (len(block) - 1) + (unit(index),))

    unit_part = lambda entry: pl.BlockSpec((1,) + entry.shape[1:], lambda index: (unit(index), 0, 0))
    rows = pl.BlockSpec((slots // steps, D), lambda index: (index, 0))
    smem = pl.BlockSpec(memory_space=pltpu.SMEM)
    image = jax.ShapeDtypeStruct((slots, D), F32)
    out = pl.pallas_call(
        partial(update_kernel, limit),
        grid=(steps,),
        in_specs=[smem]
        + [unit_part(entry) for entry in sums[:2]]
        + [whole(entry) for entry in sums[2:]]
        + [rows, rows]
        + [part(entry) for entry in arrays],
        out_specs=[rows, rows, smem] + [part(entry) for entry in shapes],
        out_shape=[image, image, jax.ShapeDtypeStruct((1,), F32)] + shapes,
        name="update_weights",
    )(step_count, *sums, block_output, token_gradient, *arrays)
    fields = [turned_back(out[3 + field :: 5]) for field in range(5)]
    return out[:3], [fields[field][index] for index in range(6) for field in range(5)]


def pack_shards(attend_weights, output_weights, expand_weights, reduce_weights):
    rows = attend_weights.shape[1]
    attend = attend_weights.astype(BF).reshape(3, rows, PAIRS, PAIR)
    attend = jnp.transpose(attend, (2, 1, 0, 3)).reshape(PAIRS, rows, 3 * PAIR)
    output = jnp.transpose(
        output_weights.astype(BF).T.reshape(rows, PAIRS, PAIR), (1, 0, 2)
    )
    expand = jnp.transpose(expand_weights.astype(BF).reshape(rows, CHUNKS, CHUNK), (1, 0, 2))
    reduce = jnp.transpose(reduce_weights.astype(BF).T.reshape(rows, CHUNKS, CHUNK), (1, 0, 2))
    return jnp.concatenate([attend, output], axis=2), jnp.concatenate([expand, reduce], axis=2)


def unpack_shards(pair_grads, chunk_grads):
    rows = pair_grads.shape[1]
    attend = jnp.transpose(
        pair_grads[:, :, : 3 * PAIR].reshape(PAIRS, rows, 3, PAIR), (2, 1, 0, 3)
    ).reshape(3, rows, HALF_E)
    join = lambda part: jnp.transpose(part, (1, 0, 2)).reshape(rows, -1)
    return (
        attend,
        join(pair_grads[:, :, 3 * PAIR :]).T,
        join(chunk_grads[:, :, :CHUNK]),
        join(chunk_grads[:, :, CHUNK:]).T,
    )


def gathered_block(lengths, tokens, cotangent, norm_gains, expand_bias, pair_own, chunk_own):
    both = ("heads", "wide")
    gains = lax.all_gather(norm_gains, both, axis=1, tiled=True)
    bias = lax.all_gather(expand_bias.astype(BF), both, axis=0, tiled=True).astype(F32)
    whole = lambda own: lax.all_gather(
        lax.all_gather(own, "wide", axis=1, tiled=True), "heads", axis=1
    )
    block_output, token_gradient, pair_grads, chunk_grads, bias_back, gains_back = local_block(
        lengths, tokens, cotangent, gains, bias[None, :], whole(pair_own), whole(chunk_own)
    )
    scatter = lambda part: lax.psum_scatter(
        lax.psum_scatter(part, "heads", scatter_dimension=1),
        "wide", scatter_dimension=1, tiled=True,
    ).astype(F32)
    grads = unpack_shards(scatter(pair_grads), scatter(chunk_grads)) + (
        lax.psum_scatter(bias_back[0], both, scatter_dimension=0, tiled=True),
        lax.psum_scatter(gains_back, both, scatter_dimension=1, tiled=True),
    )
    squares = jnp.sum(jnp.stack([jnp.sum(entry * entry) for entry in grads]))
    return block_output, token_gradient, grads, lax.psum(squares, both)


def body(
    tokens, cotangent, lengths, step_count,
    attend_weights, output_weights, expand_weights, reduce_weights, expand_bias, norm_gains,
    *moments,
):
    masters = (
        attend_weights, output_weights, expand_weights, reduce_weights, expand_bias, norm_gains,
    )
    firsts, seconds, averages = moments[:6], moments[6:12], moments[12:]
    wides = lax.axis_size("wide")
    tokens_all = tokens.shape[1] * lax.axis_size("heads") * wides
    limit = 0.02 * math.sqrt(tokens_all * D * FF)
    if wides % 8 == 0 and attend_weights.shape[1] % 16 == 0 and lax.axis_size("heads") == 2:
        block_output, token_gradient, sums = exchanged_block(lengths, tokens[0], cotangent[0], masters)
        (block_output, token_gradient, grad_norm), updated = updated_weights(
            step_count, limit, sums, block_output, token_gradient, (masters, firsts, seconds, averages)
        )
        return (block_output[None], token_gradient[None], grad_norm, *updated)
    pair_own, chunk_own = pack_shards(*masters[:4])
    block_output, token_gradient, grads, total_squares = gathered_block(
        lengths, tokens[0], cotangent[0], norm_gains, expand_bias, pair_own, chunk_own
    )
    grad_norm = jnp.sqrt(total_squares)
    factor = jnp.minimum(1.0, limit / grad_norm)
    step_float = step_count[0].astype(F32)
    first_fix = 1.0 - jnp.power(BETA_FIRST, step_float)
    second_fix = 1.0 - jnp.power(BETA_SECOND, step_float)
    keep = jnp.minimum(AVERAGE_CAP, (1.0 + step_float) / (10.0 + step_float))
    results = [block_output[None], token_gradient[None], grad_norm.reshape(1)]
    for index in range(6):
        results.extend(
            optimizer_update(
                masters[index], grads[index], factor, firsts[index], seconds[index],
                averages[index], RATES[index], DECAYS[index], first_fix, second_fix, keep,
            )
        )
    return tuple(results)


def solution(mesh):
    both = ("heads", "wide")
    weight_specs = (
        P(None, "wide", "heads"), P("heads", "wide"), P("wide", "heads"), P("heads", "wide"),
        P(both), P(None, both),
    )
    image = P(both, None, None)
    return jax.shard_map(
        body,
        mesh=mesh,
        in_specs=(image, image, P(both), P()) + weight_specs * 4,
        out_specs=(image, image, P()) + tuple(spec for spec in weight_specs for _ in range(5)),
        check_vma=False,
    )
```
